256 devices in a mesh: gx: 16 (over x, y), gy: 16 (over z, core).
Axes of the slice: x: 4, y: 4, z: 8, core: 2. Of those that a mesh axis runs over, the one named last changes fastest.
Arguments:
- fine_nodes: bfloat16 [524288, 256], P(('gx', 'gy')), may hold values from -6 to 6
- fine_weights: bfloat16 [6, 256, 256], replicated, may hold values from -0.375 to 0.375
- coarse_weights: bfloat16 [6, 256, 256], replicated, may hold values from -0.375 to 0.375
- top_weights: bfloat16 [6, 256, 256], replicated, may hold values from -0.375 to 0.375
- gains: float32 [3, 256], replicated, may hold values from 0.1 to 1.9
- send_list: int32 [16, 16, 4, 512], P('gx', 'gy'), may hold values from 0 to 2047
- fine_sender: int32 [16, 16, 8192], P('gx', 'gy'), may hold values from 0 to 4095, as said below
- fine_receiver: int32 [16, 16, 8192], P('gx', 'gy'), may hold values from 0 to 2048, as said below
- pool_owner: int32 [524288, 1], P(('gx', 'gy')), may hold values from 0 to 15; in each aligned block of 2048 rows (0 to 2047, 2048 to 4095, ...) at most 256 rows name the same one
- pool_local: int32 [524288], P(('gx', 'gy')), may hold values from 0 to 255
- coarse_sender: int32 [16, 16384], P('gy', 'gx'), may hold values from 0 to 4095
- coarse_receiver: int32 [16, 16384], P('gy', 'gx'), may hold values from 0 to 255
- top_parent: int32 [16, 4096], P('gy', 'gx'), may hold values from 0 to 511
- top_sender: int32 [16, 2048], P('gy'), may hold values from 0 to 511
- top_receiver: int32 [16, 2048], P('gy'), may hold values from 0 to 511
Outputs:
- fine_state: bfloat16 [524288, 256], P(('gx', 'gy'))
- coarse_state: bfloat16 [16, 4096, 256], P('gy', 'gx')
The draws below stay inside these ranges and needn't reach their ends.
Inputs may be any that keep to these rules, and one draw needn't show every extreme that they name: `fine_sender`: values below 2048 name the device's own nodes; larger values name a halo row of a neighbour that exists. `fine_receiver`: 2048 marks an empty slot; a device's live slots come first, and some device has no empty slot. `pool_owner`: among the rows of one device no member is named more than 256 times.
All inputs are finite; a program needn't handle non-finite values.
Results may differ from the reference program's by a relative error of at most 0.015.
Values may be sent and summed in bfloat16 or wider, within the bound.
A program may use at most 64 MiB of HBM per device.

```python
import math
import jax
import jax.numpy as jnp
import numpy as np
from jax import lax

H = 256
NF_DEV = 2048
HALO = 512
NF_ALL = 524288
EF_DEV = 8192
NC_DEV = 256
EC_DEV = 1024
NC_SUB = 4096
NT = 512
ET = 2048
CAP = 256
N_GX = 16
N_GY = 16


def draw_fine_sender(key, part):
    extent = (N_GX, N_GY, EF_DEV)
    key_own, key_side, key_halo, key_pick = jax.random.split(jax.random.fold_in(key, 11), 4)
    own_rows = jax.random.randint(key_own, extent, 0, NF_DEV)
    direction = jax.random.randint(key_side, extent, 0, 4)
    halo_row = jax.random.randint(key_halo, extent, 0, HALO)
    remote = jax.random.randint(key_pick, extent, 0, 4) == 0
    dev_row = lax.broadcasted_iota(jnp.int32, extent, 0)
    dev_col = lax.broadcasted_iota(jnp.int32, extent, 1)
    exists = jnp.where(direction == 0, dev_row > 0, jnp.where(direction == 1, dev_row < N_GX - 1, jnp.where(direction == 2, dev_col > 0, dev_col < N_GY - 1)))
    return jnp.where(remote & exists, NF_DEV + direction * HALO + halo_row, own_rows).astype(jnp.int32)


def draw_fine_receiver(key, part):
    extent = (N_GX, N_GY, EF_DEV)
    key_live, key_full, key_node = jax.random.split(jax.random.fold_in(key, 23), 3)
    live = jax.random.randint(key_live, (N_GX, N_GY), EF_DEV // 2, EF_DEV + 1)
    full_device = jax.random.randint(key_full, (), 0, N_GX * N_GY)
    device = lax.broadcasted_iota(jnp.int32, (N_GX, N_GY), 0) * N_GY + lax.broadcasted_iota(jnp.int32, (N_GX, N_GY), 1)
    live = jnp.where(device == full_device, EF_DEV, live)
    targets = jax.random.randint(key_node, extent, 0, NF_DEV)
    slot = lax.broadcasted_iota(jnp.int32, extent, 2)
    return jnp.where(slot < live[:, :, None], targets, NF_DEV).astype(jnp.int32)


def draw_coarse_sender(key, part):
    extent = (N_GY, N_GX * EC_DEV)
    key_near, key_far, key_pick = jax.random.split(jax.random.fold_in(key, 37), 3)
    owner = lax.broadcasted_iota(jnp.int32, extent, 1) // EC_DEV
    nearby = owner * NC_DEV + jax.random.randint(key_near, extent, 0, NC_DEV)
    anywhere = jax.random.randint(key_far, extent, 0, NC_SUB)
    choose_near = jax.random.randint(key_pick, extent, 0, 2) == 0
    return jnp.where(choose_near, nearby, anywhere).astype(jnp.int32)


def place_ends(drawn, key, least, largest):
    index_at = [jax.random.randint(jax.random.fold_in(key, axis), (), 0, length) for axis, length in enumerate(drawn.shape)]
    widest = drawn.shape.index(max(drawn.shape))
    beside = index_at[:widest] + [(index_at[widest] + 1) % drawn.shape[widest]] + index_at[widest + 1:]
    return drawn.at[tuple(index_at)].set(least).at[tuple(beside)].set(largest)


def level_of(own_key, shape, shards, smallest, high):
    level = 1.0
    for dim, parts in shards:
        heights = jax.random.uniform(jax.random.fold_in(jax.random.fold_in(own_key, 6), dim), (parts,), jnp.float32, smallest / len(shards), high / len(shards))
        level = level * jnp.repeat(jnp.exp(heights), shape[dim] // parts).reshape((-1,) + (1,) * (len(shape) - 1 - dim))
    return level


def rank_table(amount, lean):
    portions = [(1 << 20) // math.isqrt(rank ** lean) + 1 for rank in range(1, amount + 1)]
    deviation = 1 + sum(portions) // (1 << 30)
    return np.cumsum(np.array([max(1, weight // deviation) for weight in portions]))


def ranked(stream_key, shape, number_of, slope):
    table = rank_table(number_of, slope)
    ticket = jax.random.randint(jax.random.fold_in(stream_key, 1), shape, 0, int(table[number_of - 1]))
    grade = jnp.searchsorted(jnp.asarray(table, jnp.int32), ticket, side="right")
    return jax.random.permutation(jax.random.fold_in(stream_key, 2), number_of)[grade].astype(jnp.int32)


def assign_block(stream_key, own, number, rows, count, top, limit, skew):
    sequence = jax.random.permutation(stream_key, count)
    heavy_load, usual = shares(count, rows * top, limit, skew, True), shares(count, rows * top, limit, skew, False)
    places = jnp.arange(count)

    def named(tallies, turn):
        used = int((tallies > 0).sum())
        fixed = max(1, used // 4)
        moved = fixed + (places - fixed + turn * (used - fixed)) % max(1, count - fixed)
        return jnp.zeros((count,), jnp.int32).at[sequence[jnp.where(places < fixed, places, moved)]].set(jnp.asarray(tallies, jnp.int32))

    tallies = jnp.where(number % 4 == 0, named(heavy_load, number // 4), named(usual, number - number // 4 - 1))
    mixed = jax.random.permutation(jax.random.fold_in(own, 3), count)
    donor, receiver = mixed[0:count // 2 * 2:2], mixed[1:count // 2 * 2:2]
    room = jnp.minimum(tallies[donor] - 1, limit - tallies[receiver]) // 2
    room = jnp.where((donor == sequence[0]) | (receiver == sequence[0]) | (tallies[receiver] == 0), 0, jnp.maximum(room, 0))
    moved = jax.random.randint(jax.random.fold_in(own, 4), (count // 2,), 0, 1 << 20) % (room + 1)
    tallies = tallies.at[donor].add(-moved).at[receiver].add(moved)
    members = jnp.searchsorted(jnp.cumsum(tallies), jnp.arange(rows * top), side="right").astype(jnp.int32)
    listing = members.reshape(top, rows).T
    listing = listing[jax.random.permutation(jax.random.fold_in(own, 1), rows)]
    turn = jax.random.randint(jax.random.fold_in(own, 2), (rows, 1), 0, top)
    return jnp.take_along_axis(listing, (jnp.arange(top)[None, :] + turn) % top, axis=1)


def shares(amount, total, most, lean, full):
    weights = [(1 << 20) // math.isqrt(grade ** lean) + 1 for grade in range(1, amount + 1)]
    largest = most if full else min(most, max(-(-total // amount), total * weights[0] // sum(weights)))
    least = 1 if total - largest >= amount - 1 else 0
    counts, surplus = [largest] + [least] * (amount - 1), total - largest - least * (amount - 1)
    while surplus > 0:
        candidates = [i for i in range(1, amount) if counts[i] < largest] or [i for i in range(1, amount) if counts[i] < most]
        mass, remaining = sum([weights[i] for i in candidates]), surplus
        for i in candidates:
            addition = min(most - counts[i], max(1, remaining * weights[i] // mass), surplus)
            counts[i] = counts[i] + addition
            surplus = surplus - addition
    return np.array(counts)


def noise(key, shape, scale, most, pieces=(), held_as=jnp.bfloat16):
    values = scale * jax.random.normal(key, shape, jnp.float32)
    if pieces:
        values = values * level_of(key, shape, pieces, -0.22, 0.18)
    return jnp.clip(values, -most, most).astype(held_as)


def setup_inputs(seed: int = 0) -> dict:
    arg_keys = jax.random.split(jax.random.key(seed), 16)
    fine_nodes = noise(arg_keys[0], (NF_ALL, H), 1.0, 6.0, ((0, 256),))
    fine_weights = noise(arg_keys[1], (6, H, H), H ** -0.5, 0.375)
    coarse_weights = noise(arg_keys[2], (6, H, H), H ** -0.5, 0.375)
    top_weights = noise(arg_keys[3], (6, H, H), H ** -0.5, 0.375)
    gains = jnp.clip(1.0 + 0.18 * jax.random.normal(arg_keys[4], (3, H), jnp.float32), 0.1, 1.9)
    send_list = place_ends(jax.random.randint(arg_keys[5], (N_GX, N_GY, 4, HALO), 0, NF_DEV), jax.random.fold_in(arg_keys[5], 1), 0, NF_DEV - 1).astype(jnp.int32)
    fine_sender = draw_fine_sender(jax.random.fold_in(arg_keys[15], 71), 0)
    fine_receiver = draw_fine_receiver(jax.random.fold_in(arg_keys[15], 71), 0)
    pool_owner_keys = jax.random.split(jax.random.fold_in(arg_keys[8], 1), NF_ALL // NF_DEV)
    pool_owner_turns = jax.random.permutation(jax.random.fold_in(arg_keys[8], 3), NF_ALL // NF_DEV)
    pool_owner = jax.vmap(lambda own, number: assign_block(jax.random.fold_in(arg_keys[8], 2), own, number, NF_DEV, N_GX, 1, CAP, 2))(pool_owner_keys, pool_owner_turns).reshape((NF_ALL, 1))
    pool_local = place_ends(jax.random.randint(arg_keys[9], (NF_ALL,), 0, NC_DEV), jax.random.fold_in(arg_keys[9], 1), 0, NC_DEV - 1).astype(jnp.int32)
    coarse_sender = draw_coarse_sender(jax.random.fold_in(arg_keys[15], 71), 0)
    coarse_receiver = place_ends(jax.random.randint(arg_keys[11], (N_GY, N_GX * EC_DEV), 0, NC_DEV), jax.random.fold_in(arg_keys[11], 1), 0, NC_DEV - 1).astype(jnp.int32)
    top_parent = place_ends(ranked(arg_keys[12], (N_GY, NC_SUB), NT, 1), jax.random.fold_in(arg_keys[12], 3), 0, NT - 1).astype(jnp.int32)
    top_sender = place_ends(jax.random.randint(arg_keys[13], (N_GY, ET), 0, NT), jax.random.fold_in(arg_keys[13], 1), 0, NT - 1).astype(jnp.int32)
    top_receiver = place_ends(jax.random.randint(arg_keys[14], (N_GY, ET), 0, NT), jax.random.fold_in(arg_keys[14], 1), 0, NT - 1).astype(jnp.int32)
    return {"fine_nodes": fine_nodes, "fine_weights": fine_weights, "coarse_weights": coarse_weights, "top_weights": top_weights, "gains": gains, "send_list": send_list, "fine_sender": fine_sender, "fine_receiver": fine_receiver, "pool_owner": pool_owner, "pool_local": pool_local, "coarse_sender": coarse_sender, "coarse_receiver": coarse_receiver, "top_parent": top_parent, "top_sender": top_sender, "top_receiver": top_receiver}


def project(states, weights):
    sender_term = jnp.dot(states, weights[0], preferred_element_type=jnp.float32).astype(jnp.bfloat16)
    receiver_term = jnp.dot(states, weights[1], preferred_element_type=jnp.float32).astype(jnp.bfloat16)
    return (sender_term, receiver_term)

def gather_messages(fetch, receiver_term, receivers, weight_out, count, most):
    edges = receivers.shape[0]
    block = math.gcd(edges, most)
    width = receiver_term.shape[1]

    def advance(summed, turn):
        begin = (turn * block).astype(jnp.int32)
        targets = lax.dynamic_slice_in_dim(receivers, begin, block)
        before = fetch(begin, block) + jnp.take(receiver_term, jnp.minimum(targets, count - 1), axis=0).astype(jnp.float32)
        hidden = jax.nn.silu(before).astype(jnp.bfloat16)
        message = jnp.dot(hidden, weight_out, preferred_element_type=jnp.float32)
        return (summed.at[targets].add(message, mode='drop'), None)
    turns = jnp.arange(edges // block, dtype=jnp.int32)
    summed, unused = lax.scan(advance, jnp.zeros((count, width), jnp.float32), turns)
    return summed

def update_nodes(states, aggregate, weights, gain):
    merged = jnp.dot(states, weights[3], preferred_element_type=jnp.float32)
    merged = merged + jnp.dot(aggregate.astype(jnp.bfloat16), weights[4], preferred_element_type=jnp.float32)
    inner = jax.nn.silu(merged).astype(jnp.bfloat16)
    output = jnp.dot(inner, weights[5], preferred_element_type=jnp.float32)
    centred = output - lax.optimization_barrier(jnp.mean(output, axis=1, keepdims=True))
    spread = lax.optimization_barrier(jnp.mean(centred * centred, axis=1, keepdims=True))
    return (states.astype(jnp.float32) + gain * centred * lax.rsqrt(spread + 1e-05)).astype(jnp.bfloat16)

def run_layer(states, senders, receivers, weights, gain, most):
    sender_term, receiver_term = project(states, weights)
    count = states.shape[0]

    def fetch(begin, rows):
        picked = lax.dynamic_slice_in_dim(senders, begin, rows)
        return jnp.take(sender_term, picked, axis=0).astype(jnp.float32)
    aggregate = gather_messages(fetch, receiver_term, receivers, weights[2], count, most)
    return update_nodes(states, aggregate, weights, gain)

def reference(fine_nodes, fine_weights, coarse_weights, top_weights, gains, send_list, fine_sender, fine_receiver, pool_owner, pool_local, coarse_sender, coarse_receiver, top_parent, top_sender, top_receiver):
    extent = (N_GX, N_GY, EF_DEV)
    dev_row = lax.broadcasted_iota(jnp.int32, extent, 0)
    dev_col = lax.broadcasted_iota(jnp.int32, extent, 1)
    device = dev_row * N_GY + dev_col
    offset = fine_sender - NF_DEV
    direction = jnp.clip(offset // HALO, 0, 3).astype(jnp.int32)
    halo_row = jnp.clip(offset % HALO, 0, HALO - 1).astype(jnp.int32)
    row_step = jnp.array([-1, 1, 0, 0], jnp.int32)[direction]
    col_step = jnp.array([0, 0, -1, 1], jnp.int32)[direction]
    from_row = jnp.clip(dev_row + row_step, 0, N_GX - 1)
    from_col = jnp.clip(dev_col + col_step, 0, N_GY - 1)
    listed = send_list[from_row, from_col, direction, halo_row]
    fine_senders = jnp.where(fine_sender < NF_DEV, device * NF_DEV + fine_sender, (from_row * N_GY + from_col) * NF_DEV + listed).astype(jnp.int32)
    fine_receivers = jnp.where(fine_receiver < NF_DEV, device * NF_DEV + fine_receiver, NF_ALL).astype(jnp.int32)
    fine_one = run_layer(fine_nodes, fine_senders.reshape(-1), fine_receivers.reshape(-1), fine_weights, gains[0], 65536)
    fine_ids = jnp.arange(NF_ALL, dtype=jnp.int32)
    subgroup = fine_ids // NF_DEV % N_GY
    coarse_index = (subgroup * NC_SUB + pool_owner[:, 0] * NC_DEV + pool_local).astype(jnp.int32)
    coarse_count = N_GY * NC_SUB
    coarse_sum = jnp.zeros((coarse_count, H), jnp.float32).at[coarse_index].add(fine_one.astype(jnp.float32))
    child_count = jnp.zeros((coarse_count,), jnp.float32).at[coarse_index].add(1.0)
    coarse_zero = (coarse_sum / jnp.maximum(child_count, 1.0)[:, None]).astype(jnp.bfloat16)
    coarse_extent = (N_GY, N_GX * EC_DEV)
    coarse_group = lax.broadcasted_iota(jnp.int32, coarse_extent, 0)
    coarse_column = lax.broadcasted_iota(jnp.int32, coarse_extent, 1)
    coarse_senders = (coarse_group * NC_SUB + coarse_sender).astype(jnp.int32)
    coarse_receivers = (coarse_group * NC_SUB + coarse_column // EC_DEV * NC_DEV + coarse_receiver).astype(jnp.int32)
    coarse_one = run_layer(coarse_zero, coarse_senders.reshape(-1), coarse_receivers.reshape(-1), coarse_weights, gains[1], 65536)
    parent_group = lax.broadcasted_iota(jnp.int32, (N_GY, NC_SUB), 0)
    top_index = (parent_group * NT + top_parent).reshape(-1).astype(jnp.int32)
    top_sum = jnp.zeros((N_GY * NT, H), jnp.float32).at[top_index].add(coarse_one.astype(jnp.float32))
    top_count = jnp.zeros((N_GY * NT,), jnp.float32).at[top_index].add(1.0)
    top_zero = (top_sum / jnp.maximum(top_count, 1.0)[:, None]).astype(jnp.bfloat16)
    top_group = lax.broadcasted_iota(jnp.int32, (N_GY, ET), 0)
    top_senders = (top_group * NT + top_sender).reshape(-1).astype(jnp.int32)
    top_receivers = (top_group * NT + top_receiver).reshape(-1).astype(jnp.int32)
    top_one = run_layer(top_zero, top_senders, top_receivers, top_weights, gains[2], 65536)
    coarse_two = (coarse_one.astype(jnp.float32) + jnp.take(top_one, top_index, axis=0).astype(jnp.float32)).astype(jnp.bfloat16)
    fine_state = (fine_one.astype(jnp.float32) + jnp.take(coarse_two, coarse_index, axis=0).astype(jnp.float32)).astype(jnp.bfloat16)
    return (fine_state, coarse_two.reshape(N_GY, NC_SUB, H))
```

```python
import functools

import jax
import jax.numpy as jnp
from jax import lax
from jax.experimental import pallas as pl
from jax.experimental.pallas import tpu as pltpu
from jax.sharding import PartitionSpec as P

F32 = jnp.float32
BF16 = jnp.bfloat16
LANES = 128
VMEM = pltpu.VMEM
SMEM = pltpu.SMEM


def silu(v):
    half = 0.5 * v
    return half + half * jnp.tanh(half)


def dot(a, b):
    return jnp.dot(a, b, preferred_element_type=F32)


def put_rows(pairs, begin, rows, value):
    pairs[pl.ds(2 * begin, rows, stride=2), :] = value[:, :LANES]
    pairs[pl.ds(2 * begin + 1, rows, stride=2), :] = value[:, LANES:]


def get_rows(pairs, begin, rows):
    left = pairs[pl.ds(2 * begin, rows, stride=2), :]
    right = pairs[pl.ds(2 * begin + 1, rows, stride=2), :]
    return left, right


def project_rows(states, weight, pairs, at, rows, block):
    @pl.loop(0, rows // block)
    def _(t):
        begin = pl.multiple_of(t * block, block)
        term = dot(states[pl.ds(begin, block), :], weight).astype(BF16).astype(F32)
        put_rows(pairs, at + begin, block, term)


def spread_rows(table, pairs, at, rows, block):
    @pl.loop(0, rows // block)
    def _(t):
        begin = pl.multiple_of(t * block, block)
        put_rows(pairs, at + begin, block, table[pl.ds(begin, block), :].astype(F32))


def pick_pairs(edges, unroll, out, pick):
    @pl.loop(0, edges // unroll)
    def _(t):
        begin = t * unroll
        found = [pick(begin + u) for u in range(unroll)]
        for u in range(unroll):
            out[pl.ds(2 * (begin + u), 2), :] = found[u]


def one_hot(targets, begin, rows):
    shape = (rows, targets.shape[1])
    return jnp.where(
        lax.broadcasted_iota(jnp.int32, shape, 0) + begin == targets, 1.0, 0.0
    ).astype(BF16)


def pass_edges(senders, receivers, target_row, table, terms, sums, hidden, total, count, chunk, tile):
    edges = receivers.shape[0]

    @pl.loop(0, count // tile)
    def _(t):
        total[pl.ds(pl.multiple_of(t * tile, tile), tile), :] = jnp.zeros((tile, 2 * LANES), F32)

    @pl.loop(0, edges // chunk)
    def _(c):
        first = c * chunk

        def pick(e):
            s = senders[first + e]
            r = receivers[first + e]
            return table[pl.ds(2 * s, 2), :] + terms[pl.ds(2 * r, 2), :]

        pick_pairs(chunk, 16, sums, pick)

        @pl.loop(0, chunk // 64)
        def _(t):
            begin = pl.multiple_of(t * 64, 64)
            left, right = get_rows(sums, begin, 64)
            hidden[pl.ds(begin, 64), :LANES] = silu(left).astype(BF16)
            hidden[pl.ds(begin, 64), LANES:] = silu(right).astype(BF16)

        targets = target_row[:, pl.ds(pl.multiple_of(first, chunk), chunk)]

        @pl.loop(0, count // tile)
        def _(t):
            begin = pl.multiple_of(t * tile, tile)
            total[pl.ds(begin, tile), :] += dot(one_hot(targets, begin, tile), hidden[...])


def update(states, total, weights, gain, begin, rows):
    h = states[pl.ds(begin, rows), :]
    aggregate = dot(total[pl.ds(begin, rows), :].astype(BF16), weights[2]).astype(BF16)
    inner = silu(dot(h, weights[3]) + dot(aggregate, weights[4])).astype(BF16)
    output = dot(inner, weights[5])
    centred = output - jnp.mean(output, axis=1, keepdims=True)
    spread = jnp.mean(centred * centred, axis=1, keepdims=True)
    return (h.astype(F32) + gain * centred * lax.rsqrt(spread + 1e-05)).astype(BF16)


def send_kernel(list_ref, nodes, weights, out, pairs, picked):
    rows = nodes.shape[0]
    project_rows(nodes, weights[0], pairs, 0, rows, 256)
    pick_pairs(list_ref.shape[0], 16, picked, lambda e: pairs[pl.ds(2 * list_ref[e], 2), :])

    @pl.loop(0, out.shape[0] // 64)
    def _(t):
        begin = pl.multiple_of(t * 64, 64)
        left, right = get_rows(picked, begin, 64)
        out[pl.ds(begin, 64), :LANES] = left.astype(BF16)
        out[pl.ds(begin, 64), LANES:] = right.astype(BF16)


def fine_kernel(
    senders, receivers, nodes, halo0, halo1, halo2, halo3, weights, gains, target_row, parent_row,
    fine_one, pooled, table, terms, sums, hidden, total,
):
    rows = nodes.shape[0]
    halo = halo0.shape[0]
    project_rows(nodes, weights[0], table, 0, rows, 256)
    project_rows(nodes, weights[1], terms, 0, rows, 256)
    terms[pl.ds(2 * rows, 8), :] = jnp.zeros((8, LANES), F32)
    for slot, part in enumerate((halo0, halo1, halo2, halo3)):
        spread_rows(part, table, rows + slot * halo, halo, 64)
    pass_edges(senders, receivers, target_row, table, terms, sums, hidden, total, rows, 1024, 256)

    @pl.loop(0, rows // 256)
    def _(t):
        begin = pl.multiple_of(t * 256, 256)
        fine_one[pl.ds(begin, 256), :] = update(nodes, total, weights, gains[0:1, :], begin, 256)

    parents = parent_row[...]

    @pl.loop(0, pooled.shape[0] // 256)
    def _(t):
        begin = pl.multiple_of(t * 256, 256)
        pooled[pl.ds(begin, 256), :] = dot(one_hot(parents, begin, 256), fine_one[...]).astype(BF16)


def coarse_kernel(
    senders, receivers, states, gathered, weights, gains, target_row,
    out, table, terms, sums, hidden, total,
):
    rows = states.shape[0]
    spread_rows(gathered, table, 0, gathered.shape[0], 64)
    project_rows(states, weights[1], terms, 0, rows, 256)
    pass_edges(senders, receivers, target_row, table, terms, sums, hidden, total, rows, 1024, 256)
    out[...] = update(states, total, weights, gains[1:2, :], 0, rows)


def top_kernel(
    senders, receivers, parents, fine_parents, place, coarse, fine_one, weights, gains, target_row,
    parent_row, top_count,
    fine_state, coarse_state, coarse_pairs, table, terms, sums, hidden, total, top_zero,
):
    count = top_zero.shape[0]
    own = coarse_state.shape[0]
    spread_rows(coarse, coarse_pairs, 0, coarse.shape[0], 64)
    above = parent_row[...]

    @pl.loop(0, count // 256)
    def _(t):
        begin = pl.multiple_of(t * 256, 256)
        summed = dot(one_hot(above, begin, 256), coarse[...])
        children = top_count[pl.ds(begin, 256), :]
        top_zero[pl.ds(begin, 256), :] = (summed / jnp.maximum(children, 1.0)).astype(BF16)

    project_rows(top_zero, weights[0], table, 0, count, 256)
    project_rows(top_zero, weights[1], terms, 0, count, 256)
    pass_edges(senders, receivers, target_row, table, terms, sums, hidden, total, count, 1024, 256)

    @pl.loop(0, count // 256)
    def _(t):
        begin = pl.multiple_of(t * 256, 256)
        result = update(top_zero, total, weights, gains[2:3, :], begin, 256).astype(F32)
        put_rows(table, begin, 256, result)

    def lift(parent):
        return coarse_pairs[pl.ds(2 * parent, 2), :] + table[pl.ds(2 * parents[parent], 2), :]

    first = place[0] * own
    pick_pairs(own, 16, sums, lambda e: lift(first + e))

    @pl.loop(0, own // 64)
    def _(t):
        begin = pl.multiple_of(t * 64, 64)
        left, right = get_rows(sums, begin, 64)
        coarse_state[pl.ds(begin, 64), :LANES] = left.astype(BF16)
        coarse_state[pl.ds(begin, 64), LANES:] = right.astype(BF16)

    chunk = sums.shape[0] // 2

    @pl.loop(0, fine_one.shape[0] // chunk)
    def _(c):
        pick_pairs(chunk, 16, sums, lambda e: lift(fine_parents[c * chunk + e]))

        @pl.loop(0, chunk // 64)
        def _(t):
            begin = pl.multiple_of(t * 64, 64)
            to = pl.multiple_of(c * chunk + begin, 64)
            left, right = get_rows(sums, begin, 64)
            for value, at in ((left, 0), (right, LANES)):
                own_part = fine_one[pl.ds(to, 64), at : at + LANES].astype(F32)
                fine_state[pl.ds(to, 64), at : at + LANES] = (
                    own_part + value.astype(BF16).astype(F32)
                ).astype(BF16)


def call(kernel, outs, scalars, arrays, scratch, name, flops=10**9):
    in_specs = [pl.BlockSpec(memory_space=SMEM)] * len(scalars)
    in_specs += [pl.BlockSpec(memory_space=VMEM)] * len(arrays)
    return pl.pallas_call(
        kernel,
        out_shape=outs,
        in_specs=in_specs,
        out_specs=jax.tree.map(lambda _: pl.BlockSpec(memory_space=VMEM), outs),
        scratch_shapes=scratch,
        compiler_params=pltpu.CompilerParams(vmem_limit_bytes=56 << 20),
        cost_estimate=pl.CostEstimate(flops=flops, bytes_accessed=1 << 20, transcendentals=0),
        name=name,
    )(*scalars, *arrays)


def passed_along(block, axis, distance):
    devices = range(lax.axis_size(axis))
    route = [(i - distance, i) for i in devices if i - distance in devices]
    return lax.ppermute(block, axis, route)


def spread_counts(high, low, highs, lows):
    by_high = (high[None, :] == jnp.arange(highs, dtype=jnp.int32)[:, None]).astype(BF16)
    by_low = (low[:, None] == jnp.arange(lows, dtype=jnp.int32)[None, :]).astype(BF16)
    return dot(by_high, by_low)


def shape(rows, width=256, dtype=BF16):
    return jax.ShapeDtypeStruct((rows, width), dtype)


def body(
    fine_nodes, fine_weights, coarse_weights, top_weights, gains, send_list, fine_sender,
    fine_receiver, pool_owner, pool_local, coarse_sender, coarse_receiver, top_parent, top_sender,
    top_receiver,
):
    nodes = fine_nodes.shape[0]
    width = fine_nodes.shape[1]
    members = lax.axis_size("gx")
    coarse_rows = nodes // 8
    coarse_all = coarse_rows * members
    top_rows = coarse_all // 8
    lists = send_list.reshape(-1)
    halo = lists.shape[0] // 4
    owner = pool_owner.reshape(-1)
    parent = owner * coarse_rows + pool_local
    parents = top_parent.reshape(-1)

    counts = spread_counts(owner, pool_local, members, coarse_rows)
    child_count = lax.psum_scatter(counts, "gx", scatter_dimension=0, tiled=True).reshape(-1)
    all_parents = lax.all_gather(parents, "gx", axis=0, tiled=True)
    top_count = spread_counts(all_parents // 32, all_parents % 32, top_rows // 32, 32)
    top_count = top_count.reshape(-1, 1)

    sent = call(
        send_kernel, shape(4 * halo), (lists,), (fine_nodes, fine_weights),
        [VMEM((2 * nodes, LANES), F32), VMEM((8 * halo, LANES), F32)], "send_rows",
    )
    halos = [
        passed_along(sent[slot * halo : (slot + 1) * halo], axis, offset)
        for slot, (axis, offset) in enumerate((("gx", 1), ("gx", -1), ("gy", 1), ("gy", -1)))
    ]
    edges = fine_sender.reshape(-1), fine_receiver.reshape(-1)
    fine_one, pooled = call(
        fine_kernel, (shape(nodes), shape(coarse_all)), edges,
        (fine_nodes, *halos, fine_weights, gains, edges[1][None, :], parent[None, :]),
        [
            VMEM((2 * (nodes + 4 * halo), LANES), F32), VMEM((2 * nodes + 8, LANES), F32),
            VMEM((2048, LANES), F32), VMEM((1024, width), BF16), VMEM((nodes, width), F32),
        ],
        "fine_layer",
    )
    arrived = lax.all_to_all(
        pooled.reshape(members, coarse_rows, width), "gx", split_axis=0, concat_axis=0, tiled=True
    )
    coarse_sum = arrived.astype(F32).sum(axis=0)
    coarse_zero = (coarse_sum / jnp.maximum(child_count, 1.0)[:, None]).astype(BF16)
    coarse_send = dot(coarse_zero, coarse_weights[0]).astype(BF16)
    gathered = lax.all_gather(coarse_send, "gx", axis=0, tiled=True)
    edges = coarse_sender.reshape(-1), coarse_receiver.reshape(-1)
    coarse_one = call(
        coarse_kernel, shape(coarse_rows), edges,
        (coarse_zero, gathered, coarse_weights, gains, edges[1][None, :]),
        [
            VMEM((2 * coarse_all, LANES), F32), VMEM((2 * coarse_rows, LANES), F32),
            VMEM((2048, LANES), F32), VMEM((1024, width), BF16), VMEM((coarse_rows, width), F32),
        ],
        "coarse_layer",
    )
    coarse_whole = lax.all_gather(coarse_one, "gx", axis=0, tiled=True)
    edges = top_sender.reshape(-1), top_receiver.reshape(-1)
    place = lax.axis_index("gx").astype(jnp.int32).reshape(1)
    fine_state, coarse_state = call(
        top_kernel, (shape(nodes), shape(coarse_rows)), (*edges, all_parents, parent, place),
        (
            coarse_whole, fine_one, top_weights, gains, edges[1][None, :], all_parents[None, :],
            top_count,
        ),
        [
            VMEM((2 * coarse_all, LANES), F32), VMEM((2 * top_rows, LANES), F32),
            VMEM((2 * top_rows, LANES), F32), VMEM((2048, LANES), F32), VMEM((1024, width), BF16),
            VMEM((top_rows, width), F32), VMEM((top_rows, width), BF16),
        ],
        "top_layer",
    )
    return (fine_state, coarse_state[None])


def solution(mesh):
    placed = (
        P(("gx", "gy"), None), P(), P(), P(), P(),
        P("gx", "gy", None, None), P("gx", "gy", None), P("gx", "gy", None),
        P(("gx", "gy"), None), P(("gx", "gy")),
        P("gy", "gx"), P("gy", "gx"), P("gy", "gx"), P("gy", None), P("gy", None),
    )
    return jax.shard_map(
        body,
        mesh=mesh,
        in_specs=placed,
        out_specs=(P(("gx", "gy"), None), P("gy", "gx", None)),
        check_vma=False,
    )
```

```python
import math

import jax
import jax.numpy as jnp
from jax import lax
from jax.experimental import pallas as pl
from jax.experimental.pallas import tpu as pltpu
from jax.sharding import PartitionSpec as P

F32 = jnp.float32
BF16 = jnp.bfloat16
LANES = 128
VMEM = pltpu.VMEM
SMEM = pltpu.SMEM


def silu(v):
    half = 0.5 * v
    return half + half * jnp.tanh(half)


def dot(a, b):
    return jnp.dot(a, b, preferred_element_type=F32)


def put_rows(pairs, begin, rows, value):
    pairs[pl.ds(2 * begin, rows, stride=2), :] = value[:, :LANES]
    pairs[pl.ds(2 * begin + 1, rows, stride=2), :] = value[:, LANES:]


def get_rows(pairs, begin, rows):
    left = pairs[pl.ds(2 * begin, rows, stride=2), :]
    right = pairs[pl.ds(2 * begin + 1, rows, stride=2), :]
    return left, right


def project_rows(states, weight, pairs, at, rows, block):
    @pl.loop(0, rows // block)
    def _(t):
        begin = pl.multiple_of(t * block, block)
        term = dot(states[pl.ds(begin, block), :], weight).astype(BF16).astype(F32)
        put_rows(pairs, at + begin, block, term)


def spread_rows(table, pairs, at, rows, block):
    @pl.loop(0, rows // block)
    def _(t):
        begin = pl.multiple_of(t * block, block)
        put_rows(pairs, at + begin, block, table[pl.ds(begin, block), :].astype(F32))


def pick_pairs(edges, unroll, out, pick):
    @pl.loop(0, edges // unroll)
    def _(t):
        begin = t * unroll
        found = [pick(begin + u) for u in range(unroll)]
        for u in range(unroll):
            out[pl.ds(2 * (begin + u), 2), :] = found[u]


def one_hot(targets, begin, rows):
    shape = (rows, targets.shape[1])
    return jnp.where(
        lax.broadcasted_iota(jnp.int32, shape, 0) + begin == targets, 1.0, 0.0
    ).astype(BF16)


def pass_edges(senders, receivers, target_row, table, terms, sums, hidden, total, count, chunk, tile):
    edges = receivers.shape[0]

    @pl.loop(0, count // tile)
    def _(t):
        total[pl.ds(pl.multiple_of(t * tile, tile), tile), :] = jnp.zeros((tile, 2 * LANES), F32)

    @pl.loop(0, edges // chunk)
    def _(c):
        first = c * chunk

        def pick(e):
            s = senders[first + e]
            r = receivers[first + e]
            return table[pl.ds(2 * s, 2), :] + terms[pl.ds(2 * r, 2), :]

        pick_pairs(chunk, 16, sums, pick)

        @pl.loop(0, chunk // 64)
        def _(t):
            begin = pl.multiple_of(t * 64, 64)
            left, right = get_rows(sums, begin, 64)
            hidden[pl.ds(begin, 64), :LANES] = silu(left).astype(BF16)
            hidden[pl.ds(begin, 64), LANES:] = silu(right).astype(BF16)

        targets = target_row[:, pl.ds(pl.multiple_of(first, chunk), chunk)]

        @pl.loop(0, count // tile)
        def _(t):
            begin = pl.multiple_of(t * tile, tile)
            total[pl.ds(begin, tile), :] += dot(one_hot(targets, begin, tile), hidden[...])


def update(states, total, weights, gain, begin, rows):
    h = states[pl.ds(begin, rows), :]
    aggregate = dot(total[pl.ds(begin, rows), :].astype(BF16), weights[2]).astype(BF16)
    inner = silu(dot(h, weights[3]) + dot(aggregate, weights[4])).astype(BF16)
    output = dot(inner, weights[5])
    centred = output - jnp.mean(output, axis=1, keepdims=True)
    spread = jnp.mean(centred * centred, axis=1, keepdims=True)
    return (h.astype(F32) + gain * centred * lax.rsqrt(spread + 1e-05)).astype(BF16)


def send_kernel(list_ref, nodes, weights, out, pairs, picked):
    rows = nodes.shape[0]
    project_rows(nodes, weights[0], pairs, 0, rows, 256)
    pick_pairs(list_ref.shape[0], 16, picked, lambda e: pairs[pl.ds(2 * list_ref[e], 2), :])

    @pl.loop(0, out.shape[0] // 64)
    def _(t):
        begin = pl.multiple_of(t * 64, 64)
        left, right = get_rows(picked, begin, 64)
        out[pl.ds(begin, 64), :LANES] = left.astype(BF16)
        out[pl.ds(begin, 64), LANES:] = right.astype(BF16)


def fine_kernel(
    senders, receivers, nodes, halo, weights, gains, target_row, parent_row,
    fine_one, pooled, table, terms, sums, hidden, total,
):
    rows = nodes.shape[0]
    project_rows(nodes, weights[0], table, 0, rows, 256)
    project_rows(nodes, weights[1], terms, 0, rows, 256)
    terms[pl.ds(2 * rows, 8), :] = jnp.zeros((8, LANES), F32)
    for slot in range(4):
        spread_rows(halo.at[slot], table, rows + slot * halo.shape[1], halo.shape[1], 64)
    pass_edges(senders, receivers, target_row, table, terms, sums, hidden, total, rows, 1024, 256)

    @pl.loop(0, rows // 256)
    def _(t):
        begin = pl.multiple_of(t * 256, 256)
        fine_one[pl.ds(begin, 256), :] = update(nodes, total, weights, gains[0:1, :], begin, 256)

    parents = parent_row[...]

    across, block = pooled.shape[1], pooled.shape[2]

    @pl.loop(0, pooled.shape[0] * across)
    def _(t):
        summed = dot(one_hot(parents, t * block, block), fine_one[...])
        pooled[t // across, lax.rem(t, across)] = summed.astype(BF16)


def coarse_kernel(
    senders, receivers, states, gathered, weights, gains, target_row,
    out, table, terms, sums, hidden, total,
):
    rows = states.shape[0]
    spread_rows(gathered, table, 0, gathered.shape[0], 64)
    project_rows(states, weights[1], terms, 0, rows, 256)
    pass_edges(senders, receivers, target_row, table, terms, sums, hidden, total, rows, 1024, 256)
    out[...] = update(states, total, weights, gains[1:2, :], 0, rows)


def top_kernel(
    senders, receivers, parents, fine_parents, place, coarse, fine_one, weights, gains, target_row,
    parent_row,
    fine_state, coarse_state, coarse_pairs, table, terms, sums, hidden, total, top_zero,
):
    count = top_zero.shape[0]
    own = coarse_state.shape[0]
    spread_rows(coarse, coarse_pairs, 0, coarse.shape[0], 64)
    above = parent_row[...]

    @pl.loop(0, count // 256)
    def _(t):
        begin = pl.multiple_of(t * 256, 256)
        chosen = one_hot(above, begin, 256)
        summed = dot(chosen, coarse[...])
        children = jnp.maximum(dot(chosen, jnp.ones((coarse.shape[0], LANES), BF16))[:, :1], 1.0)
        top_zero[pl.ds(begin, 256), :] = (summed / children).astype(BF16)

    project_rows(top_zero, weights[0], table, 0, count, 256)
    project_rows(top_zero, weights[1], terms, 0, count, 256)
    pass_edges(senders, receivers, target_row, table, terms, sums, hidden, total, count, 1024, 256)

    @pl.loop(0, count // 256)
    def _(t):
        begin = pl.multiple_of(t * 256, 256)
        result = update(top_zero, total, weights, gains[2:3, :], begin, 256).astype(F32)
        put_rows(table, begin, 256, result)

    def lift(parent):
        return coarse_pairs[pl.ds(2 * parent, 2), :] + table[pl.ds(2 * parents[parent], 2), :]

    first = place[0] * own
    pick_pairs(own, 16, sums, lambda e: lift(first + e))

    @pl.loop(0, own // 64)
    def _(t):
        begin = pl.multiple_of(t * 64, 64)
        left, right = get_rows(sums, begin, 64)
        coarse_state[pl.ds(begin, 64), :LANES] = left.astype(BF16)
        coarse_state[pl.ds(begin, 64), LANES:] = right.astype(BF16)

    chunk = sums.shape[0] // 2

    @pl.loop(0, fine_one.shape[0] // chunk)
    def _(c):
        pick_pairs(chunk, 16, sums, lambda e: lift(fine_parents[c * chunk + e]))

        @pl.loop(0, chunk // 64)
        def _(t):
            begin = pl.multiple_of(t * 64, 64)
            to = pl.multiple_of(c * chunk + begin, 64)
            left, right = get_rows(sums, begin, 64)
            for value, at in ((left, 0), (right, LANES)):
                own_part = fine_one[pl.ds(to, 64), at : at + LANES].astype(F32)
                fine_state[pl.ds(to, 64), at : at + LANES] = (
                    own_part + value.astype(BF16).astype(F32)
                ).astype(BF16)


MESH = pl.DeviceIdType.MESH


def step(place, by, span):
    return lax.rem(place + by + span, span)


def remote(source, target, sems, which, device):
    return pltpu.make_async_remote_copy(
        src_ref=source, dst_ref=target, send_sem=sems[0].at[which], recv_sem=sems[1].at[which],
        device_id=device, device_id_type=MESH,
    )


def greet(devices):
    barrier = pltpu.get_barrier_semaphore()
    for device in devices:
        pl.semaphore_signal(barrier, inc=1, device_id=device, device_id_type=MESH)
    pl.semaphore_wait(barrier, len(devices))


class Torus:
    def __init__(self, side):
        self.side = side
        me = lax.axis_index("gx")
        self.at = me // side, lax.rem(me, side)

    def near(self, axis, by):
        x, y = self.at
        if axis == 0:
            return {"gx": step(x, by, self.side) * self.side + y}
        return {"gx": x * self.side + step(y, by, self.side)}

    def neighbours(self):
        return [self.near(axis, by) for axis in (0, 1) for by in (1, -1)]

    def there(self, axis, by):
        return step(self.at[axis], by, self.side)


def exchange_kernel(
    sent, counts, parents, halo, all_counts, all_parents, send_halo, recv_halo, send_count,
    recv_count, send_parent, recv_parent,
):
    members, across = lax.axis_size("gx"), lax.axis_size("gy")
    me, beside = lax.axis_index("gx"), lax.axis_index("gy")
    ahead = {"gx": step(me, 1, members)}, {"gx": step(me, -1, members)}
    aside = {"gy": step(beside, 1, across)}, {"gy": step(beside, -1, across)}
    peers = [{"gx": step(me, by, members)} for by in range(1, members)]
    greet(peers + list(aside))
    copies = [
        remote(sent.at[slot], halo.at[slot], (send_halo, recv_halo), slot, device)
        for slot, device in enumerate(ahead + aside)
    ]
    for by, device in enumerate(peers):
        goal = step(me, by + 1, members)
        sems = send_count, recv_count
        copies.append(remote(counts.at[goal], all_counts.at[me], sems, by, device))
        sems = send_parent, recv_parent
        copies.append(remote(parents.at[0], all_parents.at[me], sems, by, device))
    for copy in copies:
        copy.start()
    all_counts[me] = counts[me]
    all_parents[me] = parents[0]
    for copy in copies:
        copy.wait()


def gather_around(torus, whole, sems):
    rows = whole.shape[2]
    half, quarter = rows // 2, rows // 4
    opened = []

    def begin(source, which, device):
        copy = remote(source, source, sems, which, device)
        copy.start()
        opened.append(copy)
        return copy

    def block(first, one, two, low, length):
        place = (one, two) if first == 0 else (two, one)
        return whole.at[place[0], place[1], pl.ds(low, length)]

    order = (0, -1, 1, 2)
    def number(first, phase, way, forwarded, column):
        return (((first * 2 + phase) * 2 + way) * 2 + forwarded) * 4 + column

    ways = (1, -1)
    outer, inner, onward = {}, {}, {}
    for first in (0, 1):
        low = first * half
        for way in (0, 1):
            mine = block(first, torus.at[first], torus.at[1 - first], low, half)
            outer[first, way] = begin(
                mine, number(first, 0, way, 0, 0), torus.near(first, ways[way])
            )

    def second(first, column):
        low = first * half
        for way in (0, 1):
            held = block(
                first, torus.there(first, order[column]), torus.at[1 - first], low, half
            )
            inner[first, way, column] = begin(
                held, number(first, 1, way, 0, column), torus.near(1 - first, ways[way])
            )

    for first in (0, 1):
        second(first, 0)
    for way in (0, 1):
        for first in (0, 1):
            outer[first, way].wait_recv()
            low = first * half + way * quarter
            came = block(
                first, torus.there(first, -ways[way]), torus.at[1 - first], low, quarter
            )
            onward[first, way] = begin(
                came, number(first, 0, way, 1, 0), torus.near(first, ways[way])
            )
            second(first, way + 1)
    for first in (0, 1):
        for way in (0, 1):
            onward[first, way].wait_recv()
        second(first, 3)
    last = []
    for column in range(4):
        for way in (0, 1):
            for first in (0, 1):
                inner[first, way, column].wait_recv()
                low = first * half + way * quarter
                came = block(
                    first, torus.there(first, order[column]),
                    torus.there(1 - first, -ways[way]), low, quarter,
                )
                last.append(
                    begin(
                        came, number(first, 1, way, 1, column),
                        torus.near(1 - first, ways[way]),
                    )
                )
    for copy in last:
        copy.wait_recv()
    for copy in opened:
        copy.wait_send()


def collect_kernel(
    pooled, all_counts, weights, coarse_zero, gathered,
    passing, joined, arrived, partial, passing2, joined2, arrived2,
    send_sum, recv_sum, send_all, recv_all,
):
    torus = Torus(pooled.shape[0])
    greet(torus.neighbours())
    rows = pooled.shape[2]
    half, quarter = rows // 2, rows // 4
    ways = (1, -1)
    opened = []

    def begin(source, target, which, device):
        copy = remote(source, target, (send_sum, recv_sum), which, device)
        copy.start()
        opened.append(copy)
        return copy

    def share(first, goal, low):
        if first == 0:
            return pooled.at[goal, :, pl.ds(low, quarter)]
        return pooled.at[:, goal, pl.ds(low, quarter)]

    firsts = (1, 0)
    far, plain, summed = {}, {}, {}
    for way in (0, 1):
        for part in (0, 1):
            first = firsts[part]
            far[part, way] = begin(
                share(first, torus.there(first, 2), part * half + way * quarter),
                passing.at[part, way], part * 2 + way, torus.near(first, ways[way]),
            )
    for way in (0, 1):
        for part in (0, 1):
            first = firsts[part]
            plain[part, way] = begin(
                share(first, torus.there(first, ways[way]), part * half + (1 - way) * quarter),
                arrived.at[part, way, :, pl.ds((1 - way) * quarter, quarter)],
                4 + part * 2 + way, torus.near(first, ways[way]),
            )
    for way in (0, 1):
        for part in (0, 1):
            first = firsts[part]
            far[part, way].wait_recv()
            mine = share(first, torus.there(first, ways[way]), part * half + way * quarter)
            joined[part, way] = (
                mine[...].astype(F32) + passing[part, way].astype(F32)
            ).astype(BF16)
            summed[part, way] = begin(
                joined.at[part, way],
                arrived.at[part, way, :, pl.ds(way * quarter, quarter)],
                8 + part * 2 + way, torus.near(first, ways[way]),
            )
    for part in (0, 1):
        for way in (0, 1):
            plain[part, way].wait_recv()
        for way in (0, 1):
            summed[part, way].wait_recv()
        for way in (0, 1):
            first = firsts[part]
            own = share(first, torus.at[first], part * half + way * quarter)
            cut = pl.ds(way * quarter, quarter)
            partial[part, :, cut] = (
                own[...].astype(F32)
                + arrived[part, 0, :, cut].astype(F32)
                + arrived[part, 1, :, cut].astype(F32)
            ).astype(BF16)
        second = 1 - firsts[part]
        for way in (0, 1):
            cut = pl.ds(way * quarter, quarter)
            far[part, way] = begin(
                partial.at[part, torus.there(second, 2), cut], passing2.at[part, way],
                12 + part * 2 + way, torus.near(second, ways[way]),
            )
        for way in (0, 1):
            cut = pl.ds((1 - way) * quarter, quarter)
            plain[part, way] = begin(
                partial.at[part, torus.there(second, ways[way]), cut],
                arrived2.at[part, way, cut], 16 + part * 2 + way,
                torus.near(second, ways[way]),
            )
    for part in (0, 1):
        second = 1 - firsts[part]
        for way in (0, 1):
            cut = pl.ds(way * quarter, quarter)
            far[part, way].wait_recv()
            joined2[part, way] = (
                partial[part, torus.there(second, ways[way]), cut].astype(F32)
                + passing2[part, way].astype(F32)
            ).astype(BF16)
            summed[part, way] = begin(
                joined2.at[part, way], arrived2.at[part, way, cut], 20 + part * 2 + way,
                torus.near(second, ways[way]),
            )
    total_count = jnp.sum(all_counts[...], axis=(0, 1)).reshape(1, rows)
    square = (rows, rows)
    diagonal = lax.broadcasted_iota(jnp.int32, square, 0) == lax.broadcasted_iota(
        jnp.int32, square, 1
    )
    children = jnp.maximum(
        jnp.sum(jnp.where(diagonal, total_count, 0.0), axis=1, keepdims=True), 1.0
    )
    x, y = torus.at
    for part in (0, 1):
        second = 1 - firsts[part]
        for way in (0, 1):
            plain[part, way].wait_recv()
            summed[part, way].wait_recv()
        whole = (
            partial[part, torus.at[second]].astype(F32)
            + arrived2[part, 0].astype(F32)
            + arrived2[part, 1].astype(F32)
        )
        mean = (whole / children[part * half : (part + 1) * half]).astype(BF16)
        coarse_zero[pl.ds(part * half, half), :] = mean
        gathered[x, y, pl.ds(part * half, half)] = dot(mean, weights[0]).astype(BF16)
    for copy in opened:
        copy.wait_send()
    gather_around(torus, gathered, (send_all, recv_all))


def share_kernel(block, whole, send_all, recv_all):
    torus = Torus(whole.shape[0])
    x, y = torus.at
    whole[x, y] = block[...]
    greet(torus.neighbours())
    gather_around(torus, whole, (send_all, recv_all))


def call(kernel, outs, scalars, arrays, scratch, name, collective=None):
    in_specs = [pl.BlockSpec(memory_space=SMEM)] * len(scalars)
    in_specs += [pl.BlockSpec(memory_space=VMEM)] * len(arrays)
    return pl.pallas_call(
        kernel,
        out_shape=outs,
        in_specs=in_specs,
        out_specs=jax.tree.map(lambda _: pl.BlockSpec(memory_space=VMEM), outs),
        scratch_shapes=scratch,
        compiler_params=pltpu.CompilerParams(
            vmem_limit_bytes=56 << 20, collective_id=collective,
            has_side_effects=collective is not None,
        ),
        cost_estimate=pl.CostEstimate(flops=10**9, bytes_accessed=1 << 20, transcendentals=0),
        name=name,
    )(*scalars, *arrays)


def spread_counts(high, low, highs, lows):
    by_high = (high[None, :] == jnp.arange(highs, dtype=jnp.int32)[:, None]).astype(BF16)
    by_low = (low[:, None] == jnp.arange(lows, dtype=jnp.int32)[None, :]).astype(BF16)
    return dot(by_high, by_low)


def shape(rows, width=256, dtype=BF16):
    return jax.ShapeDtypeStruct((rows, width), dtype)


def body(
    fine_nodes, fine_weights, coarse_weights, top_weights, gains, send_list, fine_sender,
    fine_receiver, pool_owner, pool_local, coarse_sender, coarse_receiver, top_parent, top_sender,
    top_receiver,
):
    nodes = fine_nodes.shape[0]
    width = fine_nodes.shape[1]
    members = lax.axis_size("gx")
    coarse_rows = nodes // 8
    coarse_all = coarse_rows * members
    top_rows = coarse_all // 8
    lists = send_list.reshape(-1)
    halo = lists.shape[0] // 4
    owner = pool_owner.reshape(-1)
    parent = owner * coarse_rows + pool_local
    parents = top_parent.reshape(-1)

    side = math.isqrt(members)
    counts = spread_counts(owner, pool_local, members, coarse_rows)
    dma = pltpu.SemaphoreType.DMA

    sent = call(
        send_kernel, shape(4 * halo), (lists,), (fine_nodes, fine_weights),
        [VMEM((2 * nodes, LANES), F32), VMEM((8 * halo, LANES), F32)], "send_rows",
    )
    halos, all_counts, all_parents = call(
        exchange_kernel,
        (
            jax.ShapeDtypeStruct((4, halo, width), BF16),
            jax.ShapeDtypeStruct((members, 1, coarse_rows), F32),
            jax.ShapeDtypeStruct((members, 1, coarse_rows), jnp.int32),
        ),
        (),
        (
            sent.reshape(4, halo, width), counts.reshape(members, 1, coarse_rows),
            parents.reshape(1, 1, coarse_rows),
        ),
        [dma((4,))] * 2 + [dma((members - 1,))] * 4, "exchange", 0,
    )
    all_parents = all_parents.reshape(-1)
    edges = fine_sender.reshape(-1), fine_receiver.reshape(-1)
    fine_one, pooled = call(
        fine_kernel,
        (shape(nodes), jax.ShapeDtypeStruct((side, side, coarse_rows, width), BF16)), edges,
        (fine_nodes, halos, fine_weights, gains, edges[1][None, :], parent[None, :]),
        [
            VMEM((2 * (nodes + 4 * halo), LANES), F32), VMEM((2 * nodes + 8, LANES), F32),
            VMEM((2048, LANES), F32), VMEM((1024, width), BF16), VMEM((nodes, width), F32),
        ],
        "fine_layer",
    )
    half, quarter = coarse_rows // 2, coarse_rows // 4
    coarse_zero, gathered = call(
        collect_kernel,
        (shape(coarse_rows), jax.ShapeDtypeStruct((side, side, coarse_rows, width), BF16)), (),
        (pooled, all_counts, coarse_weights),
        [
            VMEM((2, 2, side, quarter, width), BF16), VMEM((2, 2, side, quarter, width), BF16),
            VMEM((2, 2, side, half, width), BF16), VMEM((2, side, half, width), BF16),
            VMEM((2, 2, quarter, width), BF16), VMEM((2, 2, quarter, width), BF16),
            VMEM((2, 2, half, width), BF16),
            dma((24,)), dma((24,)), dma((64,)), dma((64,)),
        ],
        "collect", 1,
    )
    edges = coarse_sender.reshape(-1), coarse_receiver.reshape(-1)
    coarse_one = call(
        coarse_kernel, shape(coarse_rows), edges,
        (
            coarse_zero, gathered.reshape(coarse_all, width), coarse_weights, gains,
            edges[1][None, :],
        ),
        [
            VMEM((2 * coarse_all, LANES), F32), VMEM((2 * coarse_rows, LANES), F32),
            VMEM((2048, LANES), F32), VMEM((1024, width), BF16), VMEM((coarse_rows, width), F32),
        ],
        "coarse_layer",
    )
    coarse_whole = call(
        share_kernel, jax.ShapeDtypeStruct((side, side, coarse_rows, width), BF16), (),
        (coarse_one,), [dma((64,)), dma((64,))], "share", 2,
    ).reshape(coarse_all, width)
    edges = top_sender.reshape(-1), top_receiver.reshape(-1)
    place = lax.axis_index("gx").astype(jnp.int32).reshape(1)
    fine_state, coarse_state = call(
        top_kernel, (shape(nodes), shape(coarse_rows)), (*edges, all_parents, parent, place),
        (coarse_whole, fine_one, top_weights, gains, edges[1][None, :], all_parents[None, :]),
        [
            VMEM((2 * coarse_all, LANES), F32), VMEM((2 * top_rows, LANES), F32),
            VMEM((2 * top_rows, LANES), F32), VMEM((2048, LANES), F32), VMEM((1024, width), BF16),
            VMEM((top_rows, width), F32), VMEM((top_rows, width), BF16),
        ],
        "top_layer",
    )
    return (fine_state, coarse_state[None])


def solution(mesh):
    placed = (
        P(("gx", "gy"), None), P(), P(), P(), P(),
        P("gx", "gy", None, None), P("gx", "gy", None), P("gx", "gy", None),
        P(("gx", "gy"), None), P(("gx", "gy")),
        P("gy", "gx"), P("gy", "gx"), P("gy", "gx"), P("gy", None), P("gy", None),
    )
    return jax.shard_map(
        body,
        mesh=mesh,
        in_specs=placed,
        out_specs=(P(("gx", "gy"), None), P("gy", "gx", None)),
        check_vma=False,
    )
```

```python
import math

import jax
import jax.numpy as jnp
from jax import lax
from jax.experimental import pallas as pl
from jax.experimental.pallas import tpu as pltpu
from jax.sharding import PartitionSpec as P

F32 = jnp.float32
BF16 = jnp.bfloat16
LANES = 128
VMEM = pltpu.VMEM
SMEM = pltpu.SMEM


def silu(v):
    half = 0.5 * v
    return half + half * jnp.tanh(half)


def dot(a, b):
    return jnp.dot(a, b, preferred_element_type=F32)


def put_rows(pairs, begin, rows, value):
    pairs[pl.ds(2 * begin, rows, stride=2), :] = value[:, :LANES]
    pairs[pl.ds(2 * begin + 1, rows, stride=2), :] = value[:, LANES:]


def get_rows(pairs, begin, rows):
    left = pairs[pl.ds(2 * begin, rows, stride=2), :]
    right = pairs[pl.ds(2 * begin + 1, rows, stride=2), :]
    return left, right


def project_rows(states, weight, pairs, at, rows, block):
    @pl.loop(0, rows // block)
    def _(t):
        begin = pl.multiple_of(t * block, block)
        term = dot(states[pl.ds(begin, block), :], weight).astype(BF16).astype(F32)
        put_rows(pairs, at + begin, block, term)


def spread_rows(table, pairs, at, rows, block):
    @pl.loop(0, rows // block)
    def _(t):
        begin = pl.multiple_of(t * block, block)
        put_rows(pairs, at + begin, block, table[pl.ds(begin, block), :].astype(F32))


def pick_some(at, edges, group, out, pick):
    for begin in range(0, edges, group):
        found = [pick(begin + u) for u in range(group)]
        for u in range(0, group, 4):
            to = pl.multiple_of(2 * (at + begin + u), 8)
            out[pl.ds(to, 8), :] = jnp.concatenate(found[u : u + 4], axis=0)


def pick_pairs(edges, unroll, out, pick):
    @pl.loop(0, edges // unroll)
    def _(t):
        begin = t * unroll
        pick_some(begin, unroll, 16, out, lambda u: pick(begin + u))


def pair(table, twice):
    return table[pl.ds(pl.multiple_of(twice, 2), 2), :]


def one_hot(targets, begin, rows):
    shape = (rows, targets.shape[1])
    return jnp.where(
        lax.broadcasted_iota(jnp.int32, shape, 0) + begin == targets, 1.0, 0.0
    ).astype(BF16)


def activate(sums, hidden, begin, rows):
    left, right = get_rows(sums, begin, rows)
    hidden[pl.ds(begin, rows), :LANES] = silu(left).astype(BF16)
    hidden[pl.ds(begin, rows), LANES:] = silu(right).astype(BF16)


def pass_edges(pick, target_row, sums, hidden, total, edges, chunk):
    count = total.shape[0]
    chunks = edges // chunk

    def ready(c, slot):
        pick_some(0, chunk, 16, sums, lambda u: pick(c * chunk + u))
        activate(sums, hidden.at[slot], 0, chunk)

    def summed(c, slot):
        targets = target_row[:, pl.ds(pl.multiple_of(c * chunk, chunk), chunk)]
        return dot(one_hot(targets, 0, count), hidden[slot])

    ready(0, 0)
    total[...] = jnp.zeros_like(total)

    if chunks > 1:
        @pl.loop(1, chunks)
        def _(c):
            slot = lax.rem(c, 2)
            total[...] += summed(c - 1, 1 - slot)
            ready(c, slot)

    total[...] += summed(chunks - 1, (chunks - 1) % 2)


def update(states, total, weights, gain, begin, rows):
    h = states[pl.ds(begin, rows), :]
    aggregate = dot(total[pl.ds(begin, rows), :].astype(BF16), weights[2]).astype(BF16)
    inner = silu(dot(h, weights[3]) + dot(aggregate, weights[4])).astype(BF16)
    output = dot(inner, weights[5])
    centred = output - jnp.mean(output, axis=1, keepdims=True)
    spread = jnp.mean(centred * centred, axis=1, keepdims=True)
    return (h.astype(F32) + gain * centred * lax.rsqrt(spread + 1e-05)).astype(BF16)


def fine_kernel(
    senders, receivers, nodes, halo, weights, gains, target_row,
    fine_one, table, terms, sums, hidden, total,
):
    rows = nodes.shape[0]
    project_rows(nodes, weights[0], table, 0, rows, rows)
    project_rows(nodes, weights[1], terms, 0, rows, rows)
    terms[pl.ds(2 * rows, 8), :] = jnp.zeros((8, LANES), F32)
    for slot in range(4):
        spread_rows(halo.at[slot], table, rows + slot * halo.shape[1], halo.shape[1], 64)
    pass_edges(
        lambda e: pair(table, senders[0, e]) + pair(terms, receivers[0, e]),
        target_row, sums, hidden, total, target_row.shape[1], 1024,
    )
    fine_one[...] = update(nodes, total, weights, gains[0:1, :], 0, rows)


def coarse_kernel(
    senders, receivers, states, gathered, weights, gains, target_row,
    out, table, terms, sums, hidden, total,
):
    rows = states.shape[0]
    spread_rows(gathered, table, 0, gathered.shape[0], 64)
    project_rows(states, weights[1], terms, 0, rows, 256)
    pass_edges(
        lambda e: pair(table, 2 * senders[e]) + pair(terms, 2 * receivers[e]),
        target_row, sums, hidden, total, target_row.shape[1], 1024,
    )
    out[...] = update(states, total, weights, gains[1:2, :], 0, rows)


def top_kernel(
    senders, receivers, parents, fine_parents, place, coarse, fine_one, weights, gains, target_row,
    parent_row,
    fine_state, coarse_state, coarse_pairs, table, terms, sums, hidden, total, top_zero,
):
    count = top_zero.shape[0]
    own = coarse_state.shape[0]
    spread_rows(coarse, coarse_pairs, 0, coarse.shape[0], 64)
    above = parent_row[...]

    @pl.loop(0, count // 256)
    def _(t):
        begin = pl.multiple_of(t * 256, 256)
        chosen = one_hot(above, begin, 256)
        summed = dot(chosen, coarse[...])
        children = jnp.maximum(dot(chosen, jnp.ones((coarse.shape[0], LANES), BF16))[:, :1], 1.0)
        top_zero[pl.ds(begin, 256), :] = (summed / children).astype(BF16)

    project_rows(top_zero, weights[0], table, 0, count, 512)
    project_rows(top_zero, weights[1], terms, 0, count, 512)
    pass_edges(
        lambda e: pair(table, 2 * senders[e]) + pair(terms, 2 * receivers[e]),
        target_row, sums, hidden, total, target_row.shape[1], 1024,
    )
    put_rows(table, 0, count, update(top_zero, total, weights, gains[2:3, :], 0, count).astype(F32))

    def lift(parent):
        return pair(coarse_pairs, 2 * parent) + pair(table, 2 * parents[parent])

    first = place[0] * own
    pick_pairs(own, 32, sums, lambda e: lift(first + e))
    left, right = get_rows(sums, 0, own)
    coarse_state[:, :LANES] = left.astype(BF16)
    coarse_state[:, LANES:] = right.astype(BF16)
    chunk = sums.shape[0] // 2

    @pl.loop(0, fine_one.shape[0] // chunk)
    def _(c):
        pick_pairs(chunk, 64, sums, lambda e: lift(fine_parents[c * chunk + e]))

        @pl.loop(0, chunk // 256)
        def _(t):
            begin = pl.multiple_of(t * 256, 256)
            to = pl.multiple_of(c * chunk + begin, 256)
            left, right = get_rows(sums, begin, 256)
            for value, at in ((left, 0), (right, LANES)):
                own_part = fine_one[pl.ds(to, 256), at : at + LANES].astype(F32)
                fine_state[pl.ds(to, 256), at : at + LANES] = (
                    own_part + value.astype(BF16).astype(F32)
                ).astype(BF16)


MESH = pl.DeviceIdType.MESH


def step(place, by, span):
    return lax.rem(place + by + span, span)


def remote(source, target, sems, which, device):
    return pltpu.make_async_remote_copy(
        src_ref=source, dst_ref=target, send_sem=sems[0].at[which], recv_sem=sems[1].at[which],
        device_id=device, device_id_type=MESH,
    )


WAYS = (1, -1, 2)


def greet_first(devices):
    barrier = pltpu.get_barrier_semaphore()
    for device in devices:
        pl.semaphore_signal(barrier, inc=1, device_id=device, device_id_type=MESH)


def greet_last(devices):
    pl.semaphore_wait(pltpu.get_barrier_semaphore(), len(devices))


class Torus:
    def __init__(self, side):
        self.side = side
        me = lax.axis_index("gx")
        self.at = me // side, lax.rem(me, side)

    def near(self, axis, by):
        x, y = self.at
        if axis == 0:
            return {"gx": step(x, by, self.side) * self.side + y}
        return {"gx": x * self.side + step(y, by, self.side)}

    def ring(self):
        return [self.near(axis, by) for axis in (0, 1) for by in WAYS]

    def there(self, axis, by):
        return step(self.at[axis], by, self.side)


def send_kernel(
    lists, nodes, weights, owners, locals_, senders, receivers,
    sent, counts, twice_senders, twice_receivers, pairs, picked,
):
    by_owner = one_hot(owners[...], 0, counts.shape[0])
    by_local = one_hot(locals_[...], 0, counts.shape[2])
    found = lax.dot_general(
        by_owner, by_local, (((1,), (1,)), ((), ())), preferred_element_type=F32
    )
    for member in range(counts.shape[0]):
        counts[member] = found[member : member + 1]
    rows = nodes.shape[0]
    project_rows(nodes, weights[0], pairs, 0, rows, rows)
    twice_senders[...] = 2 * senders[...]
    twice_receivers[...] = 2 * receivers[...]
    length = lists.shape[1]
    for slot in range(lists.shape[0]):
        pick_pairs(length, 64, picked.at[slot], lambda e: pair(pairs, 2 * lists[slot, e]))
        left, right = get_rows(picked.at[slot], 0, length)
        sent[slot, :, :LANES] = left.astype(BF16)
        sent[slot, :, LANES:] = right.astype(BF16)


def exchange_kernel(
    sent, counts, parents,
    halo, all_counts, all_parents,
    send_halo, recv_halo, send_count, recv_count, send_parent, recv_parent,
):
    members, across = lax.axis_size("gx"), lax.axis_size("gy")
    me, beside = lax.axis_index("gx"), lax.axis_index("gy")
    ahead = {"gx": step(me, 1, members)}, {"gx": step(me, -1, members)}
    aside = {"gy": step(beside, 1, across)}, {"gy": step(beside, -1, across)}
    peers = [{"gx": step(me, by, members)} for by in range(1, members)]
    greet_first(peers + list(aside))
    greet_last(peers + list(aside))
    copies = [
        remote(sent.at[slot], halo.at[slot], (send_halo, recv_halo), slot, device)
        for slot, device in enumerate(ahead + aside)
    ]
    for by, device in enumerate(peers):
        goal = step(me, by + 1, members)
        sems = send_count, recv_count
        copies.append(remote(counts.at[goal], all_counts.at[me], sems, by, device))
        sems = send_parent, recv_parent
        copies.append(remote(parents.at[0], all_parents.at[me], sems, by, device))
    for copy in copies:
        copy.start()
    all_counts[me] = counts[me]
    all_parents[me] = parents[0]
    for copy in copies:
        copy.wait()


class Gathering:
    def __init__(self, torus, whole, sems):
        self.torus, self.whole, self.sems = torus, whole, sems
        self.half = whole.shape[2] // 2
        self.opened, self.outer, self.inner = [], {}, {}

    def block(self, first, one, two):
        x, y = (one, two) if first == 0 else (two, one)
        return self.whole.at[x, y, pl.ds(first * self.half, self.half)]

    def send(self, first, axis, held, which, way):
        copy = remote(
            held, held, self.sems, (first * 5 + which) * 3 + way,
            self.torus.near(axis, WAYS[way]),
        )
        copy.start()
        self.opened.append(copy)
        return copy

    def begin(self, first):
        torus = self.torus
        held = self.block(first, torus.at[first], torus.at[1 - first])
        for way in range(3):
            self.outer[first, way] = self.send(first, first, held, 0, way)
        self.pass_on(first, 0)

    def pass_on(self, first, column):
        torus = self.torus
        one = torus.at[first] if column == 0 else torus.there(first, -WAYS[column - 1])
        held = self.block(first, one, torus.at[1 - first])
        for way in range(3):
            self.inner[first, column, way] = self.send(first, 1 - first, held, 1 + column, way)

    def finish(self):
        for way in range(3):
            for first in (0, 1):
                self.outer[first, way].wait_recv()
                self.pass_on(first, 1 + way)
        for column in range(4):
            for way in range(3):
                for first in (0, 1):
                    self.inner[first, column, way].wait_recv()
        for copy in self.opened:
            copy.wait_send()


def collect_kernel(
    fine_one, parent_row, all_counts, weights, coarse_zero, gathered,
    pooled, kept, arrived, partial, arrived2, send_sum, recv_sum, send_all, recv_all,
):
    torus = Torus(gathered.shape[0])
    side, rows = torus.side, gathered.shape[2]
    half = rows // 2
    greet_first(torus.ring())
    parents = parent_row[...]
    opened, first_hop, second_hop = [], {}, {}

    def share(part, goal):
        begins = [
            (k * side + goal if part == 0 else goal * side + k) * rows + part * half
            for k in range(side)
        ]
        chosen = jnp.concatenate([one_hot(parents, begin, half) for begin in begins], axis=0)
        return dot(chosen, fine_one[...]).reshape(side, half, 2 * LANES)

    for way in (2, 0, 1):
        for part in (0, 1):
            axis = 1 - part
            pooled[part, way] = share(part, torus.there(axis, WAYS[way])).astype(BF16)
            if (way, part) == (2, 0):
                greet_last(torus.ring())
            copy = remote(
                pooled.at[part, way], arrived.at[part, way], (send_sum, recv_sum),
                part * 3 + way, torus.near(axis, WAYS[way]),
            )
            copy.start()
            opened.append(copy)
            first_hop[part, way] = copy
    for part in (0, 1):
        kept[part] = share(part, torus.at[1 - part])
    for part in (0, 1):
        for way in range(3):
            first_hop[part, way].wait_recv()
        partial[part] = (
            kept[part]
            + arrived[part, 0].astype(F32)
            + arrived[part, 1].astype(F32)
            + arrived[part, 2].astype(F32)
        ).astype(BF16)
        for way in range(3):
            copy = remote(
                partial.at[part, torus.there(part, WAYS[way])], arrived2.at[part, way],
                (send_sum, recv_sum), 6 + part * 3 + way, torus.near(part, WAYS[way]),
            )
            copy.start()
            opened.append(copy)
            second_hop[part, way] = copy
    total_count = jnp.sum(all_counts[...], axis=(0, 1)).reshape(1, rows)
    square = (rows, rows)
    diagonal = lax.broadcasted_iota(jnp.int32, square, 0) == lax.broadcasted_iota(
        jnp.int32, square, 1
    )
    children = jnp.maximum(
        jnp.sum(jnp.where(diagonal, total_count, 0.0), axis=1, keepdims=True), 1.0
    )
    x, y = torus.at
    gathering = Gathering(torus, gathered, (send_all, recv_all))
    for part in (0, 1):
        for way in range(3):
            second_hop[part, way].wait_recv()
        whole = (
            partial[part, torus.at[part]].astype(F32)
            + arrived2[part, 0].astype(F32)
            + arrived2[part, 1].astype(F32)
            + arrived2[part, 2].astype(F32)
        )
        mean = (whole / children[part * half : (part + 1) * half]).astype(BF16)
        coarse_zero[pl.ds(part * half, half), :] = mean
        gathered[x, y, pl.ds(part * half, half)] = dot(mean, weights[0]).astype(BF16)
        gathering.begin(part)
    gathering.finish()
    for copy in opened:
        copy.wait_send()


def share_kernel(block, whole, send_all, recv_all):
    torus = Torus(whole.shape[0])
    x, y = torus.at
    greet_first(torus.ring())
    whole[x, y] = block[...]
    greet_last(torus.ring())
    gathering = Gathering(torus, whole, (send_all, recv_all))
    gathering.begin(0)
    gathering.begin(1)
    gathering.finish()


def call(kernel, outs, scalars, arrays, scratch, name, collective=None):
    in_specs = [pl.BlockSpec(memory_space=SMEM)] * len(scalars)
    in_specs += [pl.BlockSpec(memory_space=VMEM)] * len(arrays)
    return pl.pallas_call(
        kernel,
        out_shape=outs,
        in_specs=in_specs,
        out_specs=jax.tree.map(lambda _: pl.BlockSpec(memory_space=VMEM), outs),
        scratch_shapes=scratch,
        compiler_params=pltpu.CompilerParams(
            vmem_limit_bytes=56 << 20, collective_id=collective,
            has_side_effects=collective is not None,
        ),
        cost_estimate=pl.CostEstimate(flops=10**9, bytes_accessed=1 << 20, transcendentals=0),
        name=name,
    )(*scalars, *arrays)


def shape(rows, width=256, dtype=BF16):
    return jax.ShapeDtypeStruct((rows, width), dtype)


def body(
    fine_nodes, fine_weights, coarse_weights, top_weights, gains, send_list, fine_sender,
    fine_receiver, pool_owner, pool_local, coarse_sender, coarse_receiver, top_parent, top_sender,
    top_receiver,
):
    nodes = fine_nodes.shape[0]
    width = fine_nodes.shape[1]
    members = lax.axis_size("gx")
    coarse_rows = nodes // 8
    coarse_all = coarse_rows * members
    top_rows = coarse_all // 8
    lists = send_list.reshape(4, -1)
    halo = lists.shape[1]
    owner = pool_owner.reshape(1, -1)
    local = pool_local.reshape(1, -1)
    parent = owner * coarse_rows + local
    parents = top_parent.reshape(1, 1, -1)
    senders = fine_sender.reshape(1, -1)
    receivers = fine_receiver.reshape(1, -1)
    side = math.isqrt(members)
    dma = pltpu.SemaphoreType.DMA
    whole = jax.ShapeDtypeStruct((side, side, coarse_rows, width), BF16)
    gather_sems = [dma((30,)), dma((30,))]
    ints = jnp.int32

    rows16 = jax.ShapeDtypeStruct((members, 1, coarse_rows), F32)
    halo_shape = jax.ShapeDtypeStruct((4, halo, width), BF16)
    doubled = shape(1, senders.shape[1], ints)
    sent, counts, twice_senders, twice_receivers = call(
        send_kernel, (halo_shape, rows16, doubled, doubled), (lists,),
        (fine_nodes, fine_weights, owner, local, senders, receivers),
        [VMEM((2 * nodes, LANES), F32), VMEM((4, 2 * halo, LANES), F32)],
        "send_rows",
    )
    halos, all_counts, all_parents = call(
        exchange_kernel,
        (halo_shape, rows16, jax.ShapeDtypeStruct((members, 1, coarse_rows), ints)),
        (), (sent, counts, parents),
        [dma((4,))] * 2 + [dma((members - 1,))] * 4,
        "exchange", 0,
    )
    all_parents = all_parents.reshape(-1)
    fine_one = call(
        fine_kernel, shape(nodes), (twice_senders, twice_receivers),
        (fine_nodes, halos, fine_weights, gains, receivers),
        [
            VMEM((2 * (nodes + 4 * halo), LANES), F32), VMEM((2 * nodes + 8, LANES), F32),
            VMEM((2048, LANES), F32), VMEM((2, 1024, width), BF16), VMEM((nodes, width), F32),
        ],
        "fine_layer",
    )
    half = coarse_rows // 2
    coarse_zero, gathered = call(
        collect_kernel, (shape(coarse_rows), whole), (),
        (fine_one, parent, all_counts, coarse_weights),
        [
            VMEM((2, 3, side, half, width), BF16), VMEM((2, side, half, width), F32),
            VMEM((2, 3, side, half, width), BF16), VMEM((2, side, half, width), BF16),
            VMEM((2, 3, half, width), BF16),
            dma((12,)), dma((12,)), *gather_sems,
        ],
        "collect", 1,
    )
    edges = coarse_sender.reshape(-1), coarse_receiver.reshape(-1)
    coarse_one = call(
        coarse_kernel, shape(coarse_rows), edges,
        (
            coarse_zero, gathered.reshape(coarse_all, width), coarse_weights, gains,
            edges[1][None, :],
        ),
        [
            VMEM((2 * coarse_all, LANES), F32), VMEM((2 * coarse_rows, LANES), F32),
            VMEM((2048, LANES), F32), VMEM((2, 1024, width), BF16), VMEM((coarse_rows, width), F32),
        ],
        "coarse_layer",
    )
    coarse_whole = call(
        share_kernel, whole, (), (coarse_one,), gather_sems, "share", 2,
    ).reshape(coarse_all, width)
    edges = top_sender.reshape(-1), top_receiver.reshape(-1)
    place = lax.axis_index("gx").astype(jnp.int32).reshape(1)
    fine_state, coarse_state = call(
        top_kernel, (shape(nodes), shape(coarse_rows)), (*edges, all_parents, parent.reshape(-1), place),
        (coarse_whole, fine_one, top_weights, gains, edges[1][None, :], all_parents[None, :]),
        [
            VMEM((2 * coarse_all, LANES), F32), VMEM((2 * top_rows, LANES), F32),
            VMEM((2 * top_rows, LANES), F32), VMEM((2048, LANES), F32), VMEM((2, 1024, width), BF16),
            VMEM((top_rows, width), F32), VMEM((top_rows, width), BF16),
        ],
        "top_layer",
    )
    return (fine_state, coarse_state[None])


def solution(mesh):
    placed = (
        P(("gx", "gy"), None), P(), P(), P(), P(),
        P("gx", "gy", None, None), P("gx", "gy", None), P("gx", "gy", None),
        P(("gx", "gy"), None), P(("gx", "gy")),
        P("gy", "gx"), P("gy", "gx"), P("gy", "gx"), P("gy", None), P("gy", None),
    )
    return jax.shard_map(
        body,
        mesh=mesh,
        in_specs=placed,
        out_specs=(P(("gx", "gy"), None), P("gy", "gx", None)),
        check_vma=False,
    )
```

```python
import math

import jax
import jax.numpy as jnp
from jax import lax
from jax.experimental import pallas as pl
from jax.experimental.pallas import tpu as pltpu
from jax.sharding import PartitionSpec as P

F32 = jnp.float32
BF16 = jnp.bfloat16
LANES = 128
VMEM = pltpu.VMEM
SMEM = pltpu.SMEM


def silu(v):
    half = 0.5 * v
    return half + half * jnp.tanh(half)


def dot(a, b):
    return jnp.dot(a, b, preferred_element_type=F32)


def put_rows(pairs, begin, rows, value):
    pairs[pl.ds(2 * begin, rows, stride=2), :] = value[:, :LANES]
    pairs[pl.ds(2 * begin + 1, rows, stride=2), :] = value[:, LANES:]


def get_rows(pairs, begin, rows):
    left = pairs[pl.ds(2 * begin, rows, stride=2), :]
    right = pairs[pl.ds(2 * begin + 1, rows, stride=2), :]
    return left, right


def project_rows(states, weight, pairs, at, rows, block):
    @pl.loop(0, rows // block)
    def _(t):
        begin = pl.multiple_of(t * block, block)
        term = dot(states[pl.ds(begin, block), :], weight).astype(BF16).astype(F32)
        put_rows(pairs, at + begin, block, term)


def spread_rows(table, pairs, at, rows, block):
    @pl.loop(0, rows // block)
    def _(t):
        begin = pl.multiple_of(t * block, block)
        put_rows(pairs, at + begin, block, table[pl.ds(begin, block), :].astype(F32))


def pick_some(at, edges, group, out, pick):
    for begin in range(0, edges, group):
        found = [pick(begin + u) for u in range(group)]
        for u in range(0, group, 4):
            to = pl.multiple_of(2 * (at + begin + u), 8)
            out[pl.ds(to, 8), :] = jnp.concatenate(found[u : u + 4], axis=0)


def pick_pairs(edges, unroll, out, pick):
    @pl.loop(0, edges // unroll)
    def _(t):
        begin = t * unroll
        pick_some(begin, unroll, 16, out, lambda u: pick(begin + u))


def pair(table, twice):
    return table[pl.ds(pl.multiple_of(twice, 2), 2), :]


def one_hot(targets, begin, rows):
    shape = (rows, targets.shape[1])
    return jnp.where(
        lax.broadcasted_iota(jnp.int32, shape, 0) + begin == targets, 1.0, 0.0
    ).astype(BF16)


def activate(sums, hidden, begin, rows):
    left, right = get_rows(sums, begin, rows)
    hidden[pl.ds(begin, rows), :LANES] = silu(left).astype(BF16)
    hidden[pl.ds(begin, rows), LANES:] = silu(right).astype(BF16)


def pass_edges(pick, target_row, sums, hidden, total, edges, chunk):
    count = total.shape[0]
    chunks = edges // chunk

    def ready(c, slot):
        pick_some(0, chunk, 16, sums, lambda u: pick(c * chunk + u))
        activate(sums, hidden.at[slot], 0, chunk)

    def summed(c, slot):
        targets = target_row[:, pl.ds(pl.multiple_of(c * chunk, chunk), chunk)]
        return dot(one_hot(targets, 0, count), hidden[slot])

    ready(0, 0)
    total[...] = jnp.zeros_like(total)

    if chunks > 1:
        @pl.loop(1, chunks)
        def _(c):
            slot = lax.rem(c, 2)
            total[...] += summed(c - 1, 1 - slot)
            ready(c, slot)

    total[...] += summed(chunks - 1, (chunks - 1) % 2)


def update(states, total, weights, gain, begin, rows):
    h = states[pl.ds(begin, rows), :]
    aggregate = dot(total[pl.ds(begin, rows), :].astype(BF16), weights[2]).astype(BF16)
    inner = silu(dot(h, weights[3]) + dot(aggregate, weights[4])).astype(BF16)
    output = dot(inner, weights[5])
    centred = output - jnp.mean(output, axis=1, keepdims=True)
    spread = jnp.mean(centred * centred, axis=1, keepdims=True)
    return (h.astype(F32) + gain * centred * lax.rsqrt(spread + 1e-05)).astype(BF16)


def fine_kernel(
    senders, receivers, nodes, halo, weights, gains, target_row,
    fine_one, table, terms, sums, hidden, total,
):
    rows = nodes.shape[0]
    project_rows(nodes, weights[0], table, 0, rows, rows)
    project_rows(nodes, weights[1], terms, 0, rows, rows)
    terms[pl.ds(2 * rows, 8), :] = jnp.zeros((8, LANES), F32)
    for slot in range(4):
        spread_rows(halo.at[slot], table, rows + slot * halo.shape[1], halo.shape[1], 512)
    pass_edges(
        lambda e: pair(table, senders[0, e]) + pair(terms, receivers[0, e]),
        target_row, sums, hidden, total, target_row.shape[1], 1024,
    )
    fine_one[...] = update(nodes, total, weights, gains[0:1, :], 0, rows)


def coarse_kernel(
    senders, receivers, states, table, weights, gains, target_row,
    out, terms, sums, hidden, total,
):
    rows = states.shape[0]
    project_rows(states, weights[1], terms, 0, rows, 256)
    pass_edges(
        lambda e: pair(table, 2 * senders[e]) + pair(terms, 2 * receivers[e]),
        target_row, sums, hidden, total, target_row.shape[1], 1024,
    )
    out[...] = update(states, total, weights, gains[1:2, :], 0, rows)


def top_kernel(
    senders, receivers, twice_parents, fine_parents, place, coarse_pairs, top_zero, fine_one,
    weights, gains, target_row,
    fine_state, coarse_state, table, terms, sums, hidden, total,
):
    count = top_zero.shape[0]
    own = coarse_state.shape[0]
    project_rows(top_zero, weights[0], table, 0, count, 512)
    project_rows(top_zero, weights[1], terms, 0, count, 512)
    pass_edges(
        lambda e: pair(table, 2 * senders[e]) + pair(terms, 2 * receivers[e]),
        target_row, sums, hidden, total, target_row.shape[1], 1024,
    )
    put_rows(table, 0, count, update(top_zero, total, weights, gains[2:3, :], 0, count).astype(F32))

    def lift(parent):
        return pair(coarse_pairs, 2 * parent) + pair(table, twice_parents[parent])

    first = place[0] * own
    pick_pairs(own, 32, sums, lambda e: lift(first + e))
    left, right = get_rows(sums, 0, own)
    coarse_state[:, :LANES] = left.astype(BF16)
    coarse_state[:, LANES:] = right.astype(BF16)
    chunk = sums.shape[0] // 2

    @pl.loop(0, fine_one.shape[0] // chunk)
    def _(c):
        pick_pairs(chunk, 64, sums, lambda e: lift(fine_parents[c * chunk + e]))

        @pl.loop(0, chunk // 256)
        def _(t):
            begin = pl.multiple_of(t * 256, 256)
            to = pl.multiple_of(c * chunk + begin, 256)
            left, right = get_rows(sums, begin, 256)
            for value, at in ((left, 0), (right, LANES)):
                own_part = fine_one[pl.ds(to, 256), at : at + LANES].astype(F32)
                fine_state[pl.ds(to, 256), at : at + LANES] = (
                    own_part + value.astype(BF16).astype(F32)
                ).astype(BF16)


MESH = pl.DeviceIdType.MESH


def step(place, by, span):
    return lax.rem(place + by + span, span)


def remote(source, target, sems, which, device):
    return pltpu.make_async_remote_copy(
        src_ref=source, dst_ref=target, send_sem=sems[0].at[which], recv_sem=sems[1].at[which],
        device_id=device, device_id_type=MESH,
    )


WAYS = (1, -1, 2)


def greet_first(devices):
    barrier = pltpu.get_barrier_semaphore()
    for device in devices:
        pl.semaphore_signal(barrier, inc=1, device_id=device, device_id_type=MESH)


def greet_last(devices):
    pl.semaphore_wait(pltpu.get_barrier_semaphore(), len(devices))


class Torus:
    def __init__(self, side):
        self.side = side
        me = lax.axis_index("gx")
        self.at = me // side, lax.rem(me, side)

    def near(self, axis, by):
        x, y = self.at
        if axis == 0:
            return {"gx": step(x, by, self.side) * self.side + y}
        return {"gx": x * self.side + step(y, by, self.side)}

    def ring(self):
        return [self.near(axis, by) for axis in (0, 1) for by in WAYS]

    def there(self, axis, by):
        return step(self.at[axis], by, self.side)


def exchange_kernel(
    lists, nodes, weights, owners, locals_, parents, senders, receivers,
    halo, all_counts, all_parents, twice_parents, twice_senders, twice_receivers, fine_parents,
    rows3, picked, sent, counts,
    send_halo, recv_halo, send_count, recv_count, send_parent, recv_parent,
):
    members, across = lax.axis_size("gx"), lax.axis_size("gy")
    me, beside = lax.axis_index("gx"), lax.axis_index("gy")
    ahead = {"gx": step(me, 1, members)}, {"gx": step(me, -1, members)}
    aside = {"gy": step(beside, 1, across)}, {"gy": step(beside, -1, across)}
    peers = [{"gx": step(me, by, members)} for by in range(1, members)]
    greet_first(peers + list(aside))
    term = dot(nodes[...], weights[0]).astype(BF16).astype(F32)
    rows3[:, 0, :] = term[:, :LANES]
    rows3[:, 1, :] = term[:, LANES:]
    length = lists.shape[1]
    copies = []
    for slot, device in enumerate(ahead + aside):

        @pl.loop(0, length // 32)
        def _(t):
            begin = t * 32
            found = [rows3[lists[slot, begin + u]] for u in range(32)]
            for u in range(32):
                picked[slot, begin + u] = found[u]

        sent[slot, :, :LANES] = picked[slot, :, 0, :].astype(BF16)
        sent[slot, :, LANES:] = picked[slot, :, 1, :].astype(BF16)
        if slot == 0:
            greet_last(peers + list(aside))
        copy = remote(sent.at[slot], halo.at[slot], (send_halo, recv_halo), slot, device)
        copy.start()
        copies.append(copy)
    for by, device in enumerate(peers):
        sems = send_parent, recv_parent
        copies.append(remote(parents.at[0], all_parents.at[me], sems, by, device))
        copies[-1].start()
    by_owner = one_hot(owners[...], 0, members)
    by_local = one_hot(locals_[...], 0, counts.shape[2])
    found = lax.dot_general(
        by_owner, by_local, (((1,), (1,)), ((), ())), preferred_element_type=F32
    )
    for member in range(members):
        counts[member] = found[member : member + 1]
    for by, device in enumerate(peers):
        goal = step(me, by + 1, members)
        sems = send_count, recv_count
        copies.append(remote(counts.at[goal], all_counts.at[me], sems, by, device))
        copies[-1].start()
    all_counts[me] = counts[me]
    all_parents[me] = parents[0]
    twice_senders[...] = 2 * senders[...]
    twice_receivers[...] = 2 * receivers[...]
    fine_parents[...] = owners[...] * counts.shape[2] + locals_[...]
    for copy in copies:
        copy.wait()
    twice_parents[...] = 2 * all_parents[...]


class Gathering:
    def __init__(self, torus, whole, sems):
        self.torus, self.whole, self.sems = torus, whole, sems
        self.half = whole.shape[2] // 2
        self.opened, self.outer, self.inner = [], {}, {}

    def block(self, first, one, two):
        x, y = (one, two) if first == 0 else (two, one)
        return self.whole.at[x, y, pl.ds(first * self.half, self.half)]

    def send(self, first, axis, held, which, way):
        copy = remote(
            held, held, self.sems, (first * 5 + which) * 3 + way,
            self.torus.near(axis, WAYS[way]),
        )
        copy.start()
        self.opened.append(copy)
        return copy

    def widen(self, pairs, first, one, two):
        x, y = (one, two) if first == 0 else (two, one)
        side, rows = self.torus.side, self.whole.shape[2]
        begin = (x * side + y) * rows + first * self.half
        value = self.whole[x, y, pl.ds(first * self.half, self.half)].astype(F32)
        put_rows(pairs, begin, self.half, value)

    def begin(self, first):
        torus = self.torus
        held = self.block(first, torus.at[first], torus.at[1 - first])
        for way in range(3):
            self.outer[first, way] = self.send(first, first, held, 0, way)
        self.pass_on(first, 0)

    def place(self, first, column):
        torus = self.torus
        return torus.at[first] if column == 0 else torus.there(first, -WAYS[column - 1])

    def pass_on(self, first, column):
        held = self.block(first, self.place(first, column), self.torus.at[1 - first])
        for way in range(3):
            self.inner[first, column, way] = self.send(first, 1 - first, held, 1 + column, way)

    def finish(self, pairs, after=lambda column: None):
        torus = self.torus
        for way in range(3):
            for first in (0, 1):
                self.outer[first, way].wait_recv()
                self.pass_on(first, 1 + way)
        for column in range(4):
            for first in (0, 1):
                self.widen(pairs, first, self.place(first, column), torus.at[1 - first])
            for way in range(3):
                for first in (0, 1):
                    self.inner[first, column, way].wait_recv()
                    self.widen(
                        pairs, first, self.place(first, column),
                        torus.there(1 - first, -WAYS[way]),
                    )
            after(column)
        for copy in self.opened:
            copy.wait_send()


def collect_kernel(
    fine_one, parent_row, all_counts, all_parents, weights,
    coarse_zero, pairs, top_count,
    gathered, pooled, kept, arrived, partial, arrived2, send_sum, recv_sum, send_all, recv_all,
):
    torus = Torus(gathered.shape[0])
    side, rows = torus.side, gathered.shape[2]
    half = rows // 2
    greet_first(torus.ring())
    parents = parent_row[...]
    opened, first_hop, second_hop = [], {}, {}

    def share(part, goal):
        begins = [
            (k * side + goal if part == 0 else goal * side + k) * rows + part * half
            for k in range(side)
        ]
        chosen = jnp.concatenate([one_hot(parents, begin, half) for begin in begins], axis=0)
        return dot(chosen, fine_one[...]).reshape(side, half, 2 * LANES)

    for way in (2, 0, 1):
        for part in (0, 1):
            axis = 1 - part
            pooled[part, way] = share(part, torus.there(axis, WAYS[way])).astype(BF16)
            if (way, part) == (2, 0):
                greet_last(torus.ring())
            copy = remote(
                pooled.at[part, way], arrived.at[part, way], (send_sum, recv_sum),
                part * 3 + way, torus.near(axis, WAYS[way]),
            )
            copy.start()
            opened.append(copy)
            first_hop[part, way] = copy
    for part in (0, 1):
        kept[part] = share(part, torus.at[1 - part])
    ones = jnp.ones((side * rows, LANES), BF16)
    top_count[...] = jnp.zeros_like(top_count)

    @pl.loop(0, side)
    def _(k):
        above = jnp.concatenate([all_parents[k * side + q] for q in range(side)], axis=1)
        top_count[...] += dot(one_hot(above, 0, top_count.shape[0]), ones)

    for part in (0, 1):
        for way in range(3):
            first_hop[part, way].wait_recv()
        partial[part] = (
            kept[part]
            + arrived[part, 0].astype(F32)
            + arrived[part, 1].astype(F32)
            + arrived[part, 2].astype(F32)
        ).astype(BF16)
        for way in range(3):
            copy = remote(
                partial.at[part, torus.there(part, WAYS[way])], arrived2.at[part, way],
                (send_sum, recv_sum), 6 + part * 3 + way, torus.near(part, WAYS[way]),
            )
            copy.start()
            opened.append(copy)
            second_hop[part, way] = copy
    total_count = jnp.sum(all_counts[...], axis=(0, 1)).reshape(1, rows)
    square = (rows, rows)
    diagonal = lax.broadcasted_iota(jnp.int32, square, 0) == lax.broadcasted_iota(
        jnp.int32, square, 1
    )
    children = jnp.maximum(
        jnp.sum(jnp.where(diagonal, total_count, 0.0), axis=1, keepdims=True), 1.0
    )
    x, y = torus.at
    gathering = Gathering(torus, gathered, (send_all, recv_all))
    for part in (0, 1):
        for way in range(3):
            second_hop[part, way].wait_recv()
        whole = (
            partial[part, torus.at[part]].astype(F32)
            + arrived2[part, 0].astype(F32)
            + arrived2[part, 1].astype(F32)
            + arrived2[part, 2].astype(F32)
        )
        mean = (whole / children[part * half : (part + 1) * half]).astype(BF16)
        coarse_zero[pl.ds(part * half, half), :] = mean
        gathered[x, y, pl.ds(part * half, half)] = dot(mean, weights[0]).astype(BF16)
        gathering.begin(part)
    gathering.finish(pairs)
    for copy in opened:
        copy.wait_send()


def share_kernel(
    block, all_parents, top_count, pairs, top_zero, whole, total, send_all, recv_all
):
    torus = Torus(whole.shape[0])
    side, half = torus.side, whole.shape[2] // 2
    x, y = torus.at
    greet_first(torus.ring())
    whole[x, y] = block[...]
    greet_last(torus.ring())
    gathering = Gathering(torus, whole, (send_all, recv_all))
    gathering.begin(0)
    gathering.begin(1)
    total[...] = jnp.zeros_like(total)

    def after(column):
        at_x, at_y = gathering.place(0, column), gathering.place(1, column)
        low, high = slice(0, half), slice(half, 2 * half)
        above = [all_parents[at_x * side + k, :, low] for k in range(side)]
        above += [all_parents[k * side + at_y, :, high] for k in range(side)]
        states = [whole[at_x, k, low] for k in range(side)]
        states += [whole[k, at_y, high] for k in range(side)]
        chosen = one_hot(jnp.concatenate(above, axis=1), 0, total.shape[0])
        total[...] += dot(chosen, jnp.concatenate(states, axis=0))

    gathering.finish(pairs, after)
    children = jnp.maximum(top_count[...], 1.0)
    top_zero[:, :LANES] = (total[:, :LANES] / children).astype(BF16)
    top_zero[:, LANES:] = (total[:, LANES:] / children).astype(BF16)


def call(kernel, outs, scalars, arrays, scratch, name, collective=None):
    in_specs = [pl.BlockSpec(memory_space=SMEM)] * len(scalars)
    in_specs += [pl.BlockSpec(memory_space=VMEM)] * len(arrays)
    return pl.pallas_call(
        kernel,
        out_shape=outs,
        in_specs=in_specs,
        out_specs=jax.tree.map(lambda _: pl.BlockSpec(memory_space=VMEM), outs),
        scratch_shapes=scratch,
        compiler_params=pltpu.CompilerParams(
            vmem_limit_bytes=40 << 20, collective_id=collective,
            has_side_effects=collective is not None,
        ),
        cost_estimate=pl.CostEstimate(flops=10**9, bytes_accessed=1 << 20, transcendentals=0),
        name=name,
    )(*scalars, *arrays)


def shape(rows, width=256, dtype=BF16):
    return jax.ShapeDtypeStruct((rows, width), dtype)


def body(
    fine_nodes, fine_weights, coarse_weights, top_weights, gains, send_list, fine_sender,
    fine_receiver, pool_owner, pool_local, coarse_sender, coarse_receiver, top_parent, top_sender,
    top_receiver,
):
    nodes = fine_nodes.shape[0]
    width = fine_nodes.shape[1]
    members = lax.axis_size("gx")
    coarse_rows = nodes // 8
    coarse_all = coarse_rows * members
    top_rows = coarse_all // 8
    lists = send_list.reshape(4, -1)
    halo = lists.shape[1]
    owner = pool_owner.reshape(1, -1)
    local = pool_local.reshape(1, -1)
    parents = top_parent.reshape(1, 1, -1)
    senders = fine_sender.reshape(1, -1)
    receivers = fine_receiver.reshape(1, -1)
    side = math.isqrt(members)
    dma = pltpu.SemaphoreType.DMA
    gather_sems = [dma((30,)), dma((30,))]
    ints = jnp.int32
    rows16 = jax.ShapeDtypeStruct((members, 1, coarse_rows), F32)
    ints16 = jax.ShapeDtypeStruct((members, 1, coarse_rows), ints)
    doubled = shape(1, senders.shape[1], ints)
    pairs_shape = shape(2 * coarse_all, LANES, F32)

    halos, all_counts, all_parents, twice_parents, twice_senders, twice_receivers, parent = call(
        exchange_kernel,
        (
            jax.ShapeDtypeStruct((4, halo, width), BF16), rows16, ints16, ints16,
            doubled, doubled, shape(1, nodes, ints),
        ),
        (lists,), (fine_nodes, fine_weights, owner, local, parents, senders, receivers),
        [
            VMEM((nodes, 2, LANES), F32), VMEM((4, halo, 2, LANES), F32),
            VMEM((4, halo, width), BF16), VMEM((members, 1, coarse_rows), F32),
        ]
        + [dma((4,))] * 2 + [dma((members - 1,))] * 4,
        "exchange", 0,
    )
    fine_one = call(
        fine_kernel, shape(nodes), (twice_senders, twice_receivers),
        (fine_nodes, halos, fine_weights, gains, receivers),
        [
            VMEM((2 * (nodes + 4 * halo), LANES), F32), VMEM((2 * nodes + 8, LANES), F32),
            VMEM((2048, LANES), F32), VMEM((2, 1024, width), BF16), VMEM((nodes, width), F32),
        ],
        "fine_layer",
    )
    half = coarse_rows // 2
    gathered = VMEM((side, side, coarse_rows, width), BF16)
    coarse_zero, pairs, top_count = call(
        collect_kernel, (shape(coarse_rows), pairs_shape, shape(top_rows, LANES, F32)), (),
        (fine_one, parent, all_counts, all_parents, coarse_weights),
        [
            gathered,
            VMEM((2, 3, side, half, width), BF16), VMEM((2, side, half, width), F32),
            VMEM((2, 3, side, half, width), BF16), VMEM((2, side, half, width), BF16),
            VMEM((2, 3, half, width), BF16),
            dma((12,)), dma((12,)), *gather_sems,
        ],
        "collect", 1,
    )
    edges = coarse_sender.reshape(-1), coarse_receiver.reshape(-1)
    coarse_one = call(
        coarse_kernel, shape(coarse_rows), edges,
        (coarse_zero, pairs, coarse_weights, gains, edges[1][None, :]),
        [
            VMEM((2 * coarse_rows, LANES), F32), VMEM((2048, LANES), F32),
            VMEM((2, 1024, width), BF16), VMEM((coarse_rows, width), F32),
        ],
        "coarse_layer",
    )
    pairs, top_zero = call(
        share_kernel, (pairs_shape, shape(top_rows)), (), (coarse_one, all_parents, top_count),
        [gathered, VMEM((top_rows, width), F32), *gather_sems], "share", 2,
    )
    edges = top_sender.reshape(-1), top_receiver.reshape(-1)
    place = lax.axis_index("gx").astype(ints).reshape(1)
    fine_state, coarse_state = call(
        top_kernel, (shape(nodes), shape(coarse_rows)),
        (*edges, twice_parents.reshape(-1), parent.reshape(-1), place),
        (pairs, top_zero, fine_one, top_weights, gains, edges[1][None, :]),
        [
            VMEM((2 * top_rows, LANES), F32), VMEM((2 * top_rows, LANES), F32),
            VMEM((2048, LANES), F32), VMEM((2, 1024, width), BF16), VMEM((top_rows, width), F32),
        ],
        "top_layer",
    )
    return (fine_state, coarse_state[None])


def solution(mesh):
    placed = (
        P(("gx", "gy"), None), P(), P(), P(), P(),
        P("gx", "gy", None, None), P("gx", "gy", None), P("gx", "gy", None),
        P(("gx", "gy"), None), P(("gx", "gy")),
        P("gy", "gx"), P("gy", "gx"), P("gy", "gx"), P("gy", None), P("gy", None),
    )
    return jax.shard_map(
        body,
        mesh=mesh,
        in_specs=placed,
        out_specs=(P(("gx", "gy"), None), P("gy", "gx", None)),
        check_vma=False,
    )
```

```python
import math

import jax
import jax.numpy as jnp
from jax import lax
from jax.experimental import pallas as pl
from jax.experimental.pallas import tpu as pltpu
from jax.sharding import PartitionSpec as P

F32 = jnp.float32
BF16 = jnp.bfloat16
LANES = 128
VMEM = pltpu.VMEM
SMEM = pltpu.SMEM


def silu(v):
    half = 0.5 * v
    return half + half * jnp.tanh(half)


def dot(a, b):
    return jnp.dot(a, b, preferred_element_type=F32)


def put_rows(pairs, begin, rows, value):
    pairs[pl.ds(2 * begin, rows, stride=2), :] = value[:, :LANES]
    pairs[pl.ds(2 * begin + 1, rows, stride=2), :] = value[:, LANES:]


def get_rows(pairs, begin, rows):
    left = pairs[pl.ds(2 * begin, rows, stride=2), :]
    right = pairs[pl.ds(2 * begin + 1, rows, stride=2), :]
    return left, right


def project_rows(states, weight, pairs, at, rows, block):
    @pl.loop(0, rows // block)
    def _(t):
        begin = pl.multiple_of(t * block, block)
        term = dot(states[pl.ds(begin, block), :], weight).astype(BF16).astype(F32)
        put_rows(pairs, at + begin, block, term)


def spread_rows(table, pairs, at, rows, block):
    @pl.loop(0, rows // block)
    def _(t):
        begin = pl.multiple_of(t * block, block)
        put_rows(pairs, at + begin, block, table[pl.ds(begin, block), :].astype(F32))


def pick_some(at, edges, group, out, pick):
    for begin in range(0, edges, group):
        found = [pick(begin + u) for u in range(group)]
        for u in range(0, group, 4):
            to = pl.multiple_of(2 * (at + begin + u), 8)
            out[pl.ds(to, 8), :] = jnp.concatenate(found[u : u + 4], axis=0)


def pick_pairs(edges, unroll, out, pick):
    @pl.loop(0, edges // unroll)
    def _(t):
        begin = t * unroll
        pick_some(begin, unroll, 16, out, lambda u: pick(begin + u))


def pair(table, twice):
    return table[pl.ds(pl.multiple_of(twice, 2), 2), :]


def one_hot(targets, begin, rows):
    shape = (rows, targets.shape[1])
    return jnp.where(
        lax.broadcasted_iota(jnp.int32, shape, 0) + begin == targets, 1.0, 0.0
    ).astype(BF16)


def activate(sums, hidden, begin, rows):
    left, right = get_rows(sums, begin, rows)
    hidden[pl.ds(begin, rows), :LANES] = silu(left).astype(BF16)
    hidden[pl.ds(begin, rows), LANES:] = silu(right).astype(BF16)


def pass_edges(pick, target_row, sums, hidden, total, edges, chunk):
    count = total.shape[0]
    chunks = edges // chunk

    def ready(c, slot):
        pick_some(0, chunk, 16, sums, lambda u: pick(c * chunk + u))
        activate(sums, hidden.at[slot], 0, chunk)

    def summed(c, slot):
        targets = target_row[:, pl.ds(pl.multiple_of(c * chunk, chunk), chunk)]
        return dot(one_hot(targets, 0, count), hidden[slot])

    ready(0, 0)
    total[...] = jnp.zeros_like(total)

    if chunks > 1:
        @pl.loop(1, chunks)
        def _(c):
            slot = lax.rem(c, 2)
            total[...] += summed(c - 1, 1 - slot)
            ready(c, slot)

    total[...] += summed(chunks - 1, (chunks - 1) % 2)


def update(states, total, weights, gain, begin, rows):
    h = states[pl.ds(begin, rows), :]
    aggregate = dot(total[pl.ds(begin, rows), :].astype(BF16), weights[2]).astype(BF16)
    inner = silu(dot(h, weights[3]) + dot(aggregate, weights[4])).astype(BF16)
    output = dot(inner, weights[5])
    centred = output - jnp.mean(output, axis=1, keepdims=True)
    spread = jnp.mean(centred * centred, axis=1, keepdims=True)
    return (h.astype(F32) + gain * centred * lax.rsqrt(spread + 1e-05)).astype(BF16)


def fine_kernel(
    senders, receivers, table, terms, nodes, weights, gains, target_row,
    fine_one, sums, hidden, total,
):
    pass_edges(
        lambda e: pair(table, senders[0, e]) + pair(terms, receivers[0, e]),
        target_row, sums, hidden, total, target_row.shape[1], 1024,
    )
    fine_one[...] = update(nodes, total, weights, gains[0:1, :], 0, nodes.shape[0])


def top_kernel(
    senders, receivers, twice_parents, fine_parents, place, coarse_pairs, top_zero, fine_one,
    weights, gains, target_row,
    fine_state, coarse_state, table, terms, sums, hidden, total,
):
    count = top_zero.shape[0]
    own = coarse_state.shape[0]
    project_rows(top_zero, weights[0], table, 0, count, 512)
    project_rows(top_zero, weights[1], terms, 0, count, 512)
    pass_edges(
        lambda e: pair(table, 2 * senders[e]) + pair(terms, 2 * receivers[e]),
        target_row, sums, hidden, total, target_row.shape[1], 1024,
    )
    put_rows(table, 0, count, update(top_zero, total, weights, gains[2:3, :], 0, count).astype(F32))

    def lift(parent):
        return pair(coarse_pairs, 2 * parent) + pair(table, twice_parents[parent])

    first = place[0] * own
    pick_pairs(own, 32, sums, lambda e: lift(first + e))
    left, right = get_rows(sums, 0, own)
    coarse_state[:, :LANES] = left.astype(BF16)
    coarse_state[:, LANES:] = right.astype(BF16)
    chunk = sums.shape[0] // 2

    @pl.loop(0, fine_one.shape[0] // chunk)
    def _(c):
        pick_pairs(chunk, 64, sums, lambda e: lift(fine_parents[c * chunk + e]))

        @pl.loop(0, chunk // 256)
        def _(t):
            begin = pl.multiple_of(t * 256, 256)
            to = pl.multiple_of(c * chunk + begin, 256)
            left, right = get_rows(sums, begin, 256)
            for value, at in ((left, 0), (right, LANES)):
                own_part = fine_one[pl.ds(to, 256), at : at + LANES].astype(F32)
                fine_state[pl.ds(to, 256), at : at + LANES] = (
                    own_part + value.astype(BF16).astype(F32)
                ).astype(BF16)


MESH = pl.DeviceIdType.MESH


def step(place, by, span):
    return lax.rem(place + by + span, span)


def remote(source, target, sems, which, device):
    return pltpu.make_async_remote_copy(
        src_ref=source, dst_ref=target, send_sem=sems[0].at[which], recv_sem=sems[1].at[which],
        device_id=device, device_id_type=MESH,
    )


WAYS = (1, -1, 2)


def greet_first(devices):
    barrier = pltpu.get_barrier_semaphore()
    for device in devices:
        pl.semaphore_signal(barrier, inc=1, device_id=device, device_id_type=MESH)


def greet_last(devices):
    pl.semaphore_wait(pltpu.get_barrier_semaphore(), len(devices))


class Torus:
    def __init__(self, side):
        self.side = side
        me = lax.axis_index("gx")
        self.at = me // side, lax.rem(me, side)

    def near(self, axis, by):
        x, y = self.at
        if axis == 0:
            return {"gx": step(x, by, self.side) * self.side + y}
        return {"gx": x * self.side + step(y, by, self.side)}

    def ring(self):
        return [self.near(axis, by) for axis in (0, 1) for by in WAYS]

    def there(self, axis, by):
        return step(self.at[axis], by, self.side)


def exchange_kernel(
    lists_far, nodes_far, weights_far, coarse_weights_far, top_weights_far, gains_far, owners_far, locals_far,
    parents_far, senders_far, receivers_far, coarse_row_far, top_row_far,
    table, terms, nodes, weights, coarse_weights, top_weights, gains, receivers, coarse_row,
    top_row, all_counts, all_parents, twice_parents, twice_senders, twice_receivers, fine_parents,
    lists, owners, locals_, parents, senders, rows3, picked, sent, halo, counts, fetched,
    send_halo, recv_halo, send_count, recv_count, send_parent, recv_parent,
):
    members, across = lax.axis_size("gx"), lax.axis_size("gy")
    me, beside = lax.axis_index("gx"), lax.axis_index("gy")
    ahead = {"gx": step(me, 1, members)}, {"gx": step(me, -1, members)}
    aside = {"gy": step(beside, 1, across)}, {"gy": step(beside, -1, across)}
    peers = [{"gx": step(me, by, members)} for by in range(1, members)]
    greet_first(peers + list(aside))
    wanted = (
        (weights_far.at[0], weights.at[0]), (nodes_far, nodes), (parents_far, parents),
        (owners_far, owners), (locals_far, locals_), (senders_far, senders),
        (receivers_far, receivers), (weights_far.at[pl.ds(1, 5)], weights.at[pl.ds(1, 5)]),
        (coarse_weights_far, coarse_weights), (top_weights_far, top_weights),
        (gains_far, gains), (coarse_row_far, coarse_row), (top_row_far, top_row),
        (lists_far, lists),
    )
    fetches = [
        pltpu.make_async_copy(source, target, fetched.at[k])
        for k, (source, target) in enumerate(wanted)
    ]
    for fetch in fetches:
        fetch.start()
    for k in (0, 1, 13):
        fetches[k].wait()
    rows = nodes.shape[0]
    term = dot(nodes[...], weights[0]).astype(BF16).astype(F32)
    rows3[:, 0, :] = term[:, :LANES]
    rows3[:, 1, :] = term[:, LANES:]
    length = lists.shape[1]
    halos, copies = [], []
    for slot, device in enumerate(ahead + aside):

        @pl.loop(0, length // 32)
        def _(t):
            begin = t * 32
            found = [rows3[lists[slot, begin + u]] for u in range(32)]
            for u in range(32):
                picked[slot, begin + u] = found[u]

        sent[slot, :, :LANES] = picked[slot, :, 0, :].astype(BF16)
        sent[slot, :, LANES:] = picked[slot, :, 1, :].astype(BF16)
        if slot == 0:
            greet_last(peers + list(aside))
        copy = remote(sent.at[slot], halo.at[slot], (send_halo, recv_halo), slot, device)
        copy.start()
        halos.append(copy)
    fetches[2].wait()
    for by, device in enumerate(peers):
        sems = send_parent, recv_parent
        copies.append(remote(parents.at[0], all_parents.at[me], sems, by, device))
        copies[-1].start()
    fetches[3].wait()
    fetches[4].wait()
    by_owner = one_hot(owners[...], 0, members)
    by_local = one_hot(locals_[...], 0, counts.shape[2])
    found = lax.dot_general(
        by_owner, by_local, (((1,), (1,)), ((), ())), preferred_element_type=F32
    )
    for member in range(members):
        counts[member] = found[member : member + 1]
    for by, device in enumerate(peers):
        goal = step(me, by + 1, members)
        sems = send_count, recv_count
        copies.append(remote(counts.at[goal], all_counts.at[me], sems, by, device))
        copies[-1].start()
    all_counts[me] = counts[me]
    all_parents[me] = parents[0]
    fine_parents[...] = owners[...] * counts.shape[2] + locals_[...]
    for fetch in fetches[5:13]:
        fetch.wait()
    put_rows(table, 0, rows, dot(nodes[...], weights[0]).astype(BF16).astype(F32))
    project_rows(nodes, weights[1], terms, 0, rows, rows)
    terms[pl.ds(2 * rows, 8), :] = jnp.zeros((8, LANES), F32)
    twice_senders[...] = 2 * senders[...]
    twice_receivers[...] = 2 * receivers[...]
    for slot, copy in enumerate(halos):
        copy.wait()
        put_rows(table, rows + slot * length, length, halo[slot].astype(F32))
    for copy in copies:
        copy.wait()
    twice_parents[...] = 2 * all_parents[...]


class Gathering:
    def __init__(self, torus, whole, sems):
        self.torus, self.whole, self.sems = torus, whole, sems
        self.half = whole.shape[2] // 2
        self.opened, self.outer, self.inner = [], {}, {}

    def block(self, first, one, two):
        x, y = (one, two) if first == 0 else (two, one)
        return self.whole.at[x, y, pl.ds(first * self.half, self.half)]

    def send(self, first, axis, held, which, way):
        copy = remote(
            held, held, self.sems, (first * 5 + which) * 3 + way,
            self.torus.near(axis, WAYS[way]),
        )
        copy.start()
        self.opened.append(copy)
        return copy

    def widen(self, pairs, first, one, two):
        x, y = (one, two) if first == 0 else (two, one)
        side, rows = self.torus.side, self.whole.shape[2]
        begin = (x * side + y) * rows + first * self.half
        value = self.whole[x, y, pl.ds(first * self.half, self.half)].astype(F32)
        if len(pairs.shape) == 2:
            put_rows(pairs, begin, self.half, value)
        else:
            pairs[pl.ds(begin, self.half), 0, :] = value[:, :LANES]
            pairs[pl.ds(begin, self.half), 1, :] = value[:, LANES:]

    def begin(self, first):
        torus = self.torus
        held = self.block(first, torus.at[first], torus.at[1 - first])
        for way in range(3):
            self.outer[first, way] = self.send(first, first, held, 0, way)
        self.pass_on(first, 0)

    def place(self, first, column):
        torus = self.torus
        return torus.at[first] if column == 0 else torus.there(first, -WAYS[column - 1])

    def pass_on(self, first, column):
        held = self.block(first, self.place(first, column), self.torus.at[1 - first])
        for way in range(3):
            self.inner[first, column, way] = self.send(first, 1 - first, held, 1 + column, way)

    def finish(self, pairs, after=lambda column: None):
        torus = self.torus
        for way in range(3):
            for first in (0, 1):
                self.outer[first, way].wait_recv()
                self.pass_on(first, 1 + way)
        for column in range(4):
            for first in (0, 1):
                self.widen(pairs, first, self.place(first, column), torus.at[1 - first])
            for way in range(3):
                for first in (0, 1):
                    self.inner[first, column, way].wait_recv()
                    self.widen(
                        pairs, first, self.place(first, column),
                        torus.there(1 - first, -WAYS[way]),
                    )
            after(column)
        for copy in self.opened:
            copy.wait_send()


def coarse_kernel(
    senders, receivers, fine_one, parent_row, all_counts, all_parents, weights, gains, target_row,
    pairs, top_zero,
    coarse_zero, top_count, table3, terms3, sums, hidden, total, top_total, whole_one,
    gathered, pooled, kept, arrived, partial, arrived2, send_sum, recv_sum, send_all, recv_all,
    send_one, recv_one,
):
    torus = Torus(gathered.shape[0])
    side, rows = torus.side, gathered.shape[2]
    half = rows // 2
    greet_first(torus.ring())
    parents = parent_row[...]
    opened, first_hop, second_hop = [], {}, {}

    def share(part, goal):
        begins = [
            (k * side + goal if part == 0 else goal * side + k) * rows + part * half
            for k in range(side)
        ]
        chosen = jnp.concatenate([one_hot(parents, begin, half) for begin in begins], axis=0)
        return dot(chosen, fine_one[...]).reshape(side, half, 2 * LANES)

    for way in (2, 0, 1):
        for part in (0, 1):
            axis = 1 - part
            pooled[part, way] = share(part, torus.there(axis, WAYS[way])).astype(BF16)
            if (way, part) == (2, 0):
                greet_last(torus.ring())
            copy = remote(
                pooled.at[part, way], arrived.at[part, way], (send_sum, recv_sum),
                part * 3 + way, torus.near(axis, WAYS[way]),
            )
            copy.start()
            opened.append(copy)
            first_hop[part, way] = copy
    for part in (0, 1):
        kept[part] = share(part, torus.at[1 - part])
    ones = jnp.ones((side * rows, LANES), BF16)
    top_count[...] = jnp.zeros_like(top_count)

    @pl.loop(0, side)
    def _(k):
        above = jnp.concatenate([all_parents[k * side + q] for q in range(side)], axis=1)
        top_count[...] += dot(one_hot(above, 0, top_count.shape[0]), ones)

    for part in (0, 1):
        for way in range(3):
            first_hop[part, way].wait_recv()
        partial[part] = (
            kept[part]
            + arrived[part, 0].astype(F32)
            + arrived[part, 1].astype(F32)
            + arrived[part, 2].astype(F32)
        ).astype(BF16)
        for way in range(3):
            copy = remote(
                partial.at[part, torus.there(part, WAYS[way])], arrived2.at[part, way],
                (send_sum, recv_sum), 6 + part * 3 + way, torus.near(part, WAYS[way]),
            )
            copy.start()
            opened.append(copy)
            second_hop[part, way] = copy
    total_count = jnp.sum(all_counts[...], axis=(0, 1)).reshape(1, rows)
    square = (rows, rows)
    diagonal = lax.broadcasted_iota(jnp.int32, square, 0) == lax.broadcasted_iota(
        jnp.int32, square, 1
    )
    children = jnp.maximum(
        jnp.sum(jnp.where(diagonal, total_count, 0.0), axis=1, keepdims=True), 1.0
    )
    x, y = torus.at
    gathering = Gathering(torus, gathered, (send_all, recv_all))
    for part in (0, 1):
        for way in range(3):
            second_hop[part, way].wait_recv()
        whole = (
            partial[part, torus.at[part]].astype(F32)
            + arrived2[part, 0].astype(F32)
            + arrived2[part, 1].astype(F32)
            + arrived2[part, 2].astype(F32)
        )
        mean = (whole / children[part * half : (part + 1) * half]).astype(BF16)
        coarse_zero[pl.ds(part * half, half), :] = mean
        gathered[x, y, pl.ds(part * half, half)] = dot(mean, weights[0]).astype(BF16)
        gathering.begin(part)
    term = dot(coarse_zero[...], weights[1]).astype(BF16).astype(F32)
    terms3[:, 0, :] = term[:, :LANES]
    terms3[:, 1, :] = term[:, LANES:]
    gathering.finish(table3)
    for copy in opened:
        copy.wait_send()

    edges = target_row.shape[1]
    pick_pairs(edges, 32, sums, lambda e: table3[senders[e]] + terms3[receivers[e]])
    activate(sums, hidden, 0, edges)
    total[...] = dot(one_hot(target_row[...], 0, rows), hidden[...])
    whole_one[x, y] = update(coarse_zero, total, weights, gains[1:2, :], 0, rows)

    sharing = Gathering(torus, whole_one, (send_one, recv_one))
    sharing.begin(0)
    sharing.begin(1)
    top_total[...] = jnp.zeros_like(top_total)

    def after(column):
        at_x, at_y = sharing.place(0, column), sharing.place(1, column)
        low, high = slice(0, half), slice(half, 2 * half)
        above = [all_parents[at_x * side + k, :, low] for k in range(side)]
        above += [all_parents[k * side + at_y, :, high] for k in range(side)]
        states = [whole_one[at_x, k, low] for k in range(side)]
        states += [whole_one[k, at_y, high] for k in range(side)]
        chosen = one_hot(jnp.concatenate(above, axis=1), 0, top_total.shape[0])
        top_total[...] += dot(chosen, jnp.concatenate(states, axis=0))

    sharing.finish(pairs, after)
    above = jnp.maximum(top_count[...], 1.0)
    top_zero[:, :LANES] = (top_total[:, :LANES] / above).astype(BF16)
    top_zero[:, LANES:] = (top_total[:, LANES:] / above).astype(BF16)


def call(kernel, outs, scalars, arrays, scratch, name, collective=None, space=VMEM):
    if space is not VMEM:
        arrays = [pltpu.with_memory_space_constraint(a, space) for a in arrays]
    in_specs = [pl.BlockSpec(memory_space=SMEM)] * len(scalars)
    in_specs += [pl.BlockSpec(memory_space=space)] * len(arrays)
    return pl.pallas_call(
        kernel,
        out_shape=outs,
        in_specs=in_specs,
        out_specs=jax.tree.map(lambda _: pl.BlockSpec(memory_space=VMEM), outs),
        scratch_shapes=scratch,
        compiler_params=pltpu.CompilerParams(
            vmem_limit_bytes=40 << 20, collective_id=collective,
            has_side_effects=collective is not None,
        ),
        cost_estimate=pl.CostEstimate(flops=10**9, bytes_accessed=1 << 20, transcendentals=0),
        name=name,
    )(*scalars, *arrays)


def shape(rows, width=256, dtype=BF16):
    return jax.ShapeDtypeStruct((rows, width), dtype)


def body(
    fine_nodes, fine_weights, coarse_weights, top_weights, gains, send_list, fine_sender,
    fine_receiver, pool_owner, pool_local, coarse_sender, coarse_receiver, top_parent, top_sender,
    top_receiver,
):
    nodes = fine_nodes.shape[0]
    width = fine_nodes.shape[1]
    members = lax.axis_size("gx")
    coarse_rows = nodes // 8
    coarse_all = coarse_rows * members
    top_rows = coarse_all // 8
    lists = send_list.reshape(4, -1)
    halo = lists.shape[1]
    owner = pool_owner.reshape(1, -1)
    local = pool_local.reshape(1, -1)
    parents = top_parent.reshape(1, 1, -1)
    senders = fine_sender.reshape(1, -1)
    receivers = fine_receiver.reshape(1, -1)
    side = math.isqrt(members)
    dma = pltpu.SemaphoreType.DMA
    gather_sems = [dma((30,)), dma((30,))]
    ints = jnp.int32
    rows16 = jax.ShapeDtypeStruct((members, 1, coarse_rows), F32)
    ints16 = jax.ShapeDtypeStruct((members, 1, coarse_rows), ints)
    doubled = shape(1, senders.shape[1], ints)
    pairs_shape = shape(2 * coarse_all, LANES, F32)

    coarse_row = coarse_receiver.reshape(1, -1)
    top_row = top_receiver.reshape(1, -1)
    (
        table, terms, near_nodes, weights, near_coarse, near_top, near_gains, near_receivers,
        near_coarse_row, near_top_row, all_counts, all_parents, twice_parents, twice_senders,
        twice_receivers, parent,
    ) = call(
        exchange_kernel,
        (
            shape(2 * (nodes + 4 * halo), LANES, F32), shape(2 * nodes + 8, LANES, F32),
            shape(nodes), *[jax.ShapeDtypeStruct(fine_weights.shape, BF16)] * 3,
            shape(3, width, F32), doubled, shape(1, coarse_row.shape[1], ints),
            shape(1, top_row.shape[1], ints), rows16, ints16, ints16,
            doubled, doubled, shape(1, nodes, ints),
        ),
        (),
        (
            lists, fine_nodes, fine_weights, coarse_weights, top_weights, gains, owner, local, parents,
            senders, receivers, coarse_row, top_row,
        ),
        [
            SMEM(lists.shape, ints), VMEM((1, nodes), ints), VMEM((1, nodes), ints), VMEM((1, 1, coarse_rows), ints),
            VMEM(senders.shape, ints), VMEM((nodes, 2, LANES), F32),
            VMEM((4, halo, 2, LANES), F32), VMEM((4, halo, width), BF16),
            VMEM((4, halo, width), BF16), VMEM((members, 1, coarse_rows), F32), dma((14,)),
        ]
        + [dma((4,))] * 2 + [dma((members - 1,))] * 4,
        "exchange", 0, pltpu.MemorySpace.HBM,
    )
    fine_one = call(
        fine_kernel, shape(nodes), (twice_senders, twice_receivers),
        (table, terms, near_nodes, weights, near_gains, near_receivers),
        [VMEM((2048, LANES), F32), VMEM((2, 1024, width), BF16), VMEM((nodes, width), F32)],
        "fine_layer",
    )
    half = coarse_rows // 2
    gathered = VMEM((side, side, coarse_rows, width), BF16)
    edges = coarse_sender.reshape(-1), coarse_receiver.reshape(-1)
    pairs, top_zero = call(
        coarse_kernel, (pairs_shape, shape(top_rows)), edges,
        (fine_one, parent, all_counts, all_parents, near_coarse, near_gains, near_coarse_row),
        [
            VMEM((coarse_rows, width), BF16), VMEM((top_rows, LANES), F32),
            VMEM((coarse_all, 2, LANES), F32), VMEM((coarse_rows, 2, LANES), F32),
            VMEM((2048, LANES), F32), VMEM((1024, width), BF16), VMEM((coarse_rows, width), F32),
            VMEM((top_rows, width), F32), gathered, gathered,
            VMEM((2, 3, side, half, width), BF16), VMEM((2, side, half, width), F32),
            VMEM((2, 3, side, half, width), BF16), VMEM((2, side, half, width), BF16),
            VMEM((2, 3, half, width), BF16),
            dma((12,)), dma((12,)), *gather_sems, *gather_sems,
        ],
        "coarse_levels", 1,
    )
    pairs = pltpu.with_memory_space_constraint(pairs, VMEM)
    edges = top_sender.reshape(-1), top_receiver.reshape(-1)
    place = lax.axis_index("gx").astype(ints).reshape(1)
    fine_state, coarse_state = call(
        top_kernel, (shape(nodes), shape(coarse_rows)),
        (*edges, twice_parents.reshape(-1), parent.reshape(-1), place),
        (pairs, top_zero, fine_one, near_top, near_gains, near_top_row),
        [
            VMEM((2 * top_rows, LANES), F32), VMEM((2 * top_rows, LANES), F32),
            VMEM((2048, LANES), F32), VMEM((2, 1024, width), BF16), VMEM((top_rows, width), F32),
        ],
        "top_layer",
    )
    return (fine_state, coarse_state[None])


def solution(mesh):
    placed = (
        P(("gx", "gy"), None), P(), P(), P(), P(),
        P("gx", "gy", None, None), P("gx", "gy", None), P("gx", "gy", None),
        P(("gx", "gy"), None), P(("gx", "gy")),
        P("gy", "gx"), P("gy", "gx"), P("gy", "gx"), P("gy", None), P("gy", None),
    )
    return jax.shard_map(
        body,
        mesh=mesh,
        in_specs=placed,
        out_specs=(P(("gx", "gy"), None), P("gy", "gx", None)),
        check_vma=False,
    )
```

```python
import math

import jax
import jax.numpy as jnp
from jax import lax
from jax.experimental import pallas as pl
from jax.experimental.pallas import tpu as pltpu
from jax.sharding import PartitionSpec as P

F32 = jnp.float32
BF16 = jnp.bfloat16
LANES = 128
VMEM = pltpu.VMEM
SMEM = pltpu.SMEM


def silu(v):
    half = 0.5 * v
    return half + half * jnp.tanh(half)


def dot(a, b):
    return jnp.dot(a, b, preferred_element_type=F32)


def put_rows(pairs, begin, rows, value):
    pairs[pl.ds(2 * begin, rows, stride=2), :] = value[:, :LANES]
    pairs[pl.ds(2 * begin + 1, rows, stride=2), :] = value[:, LANES:]


def get_rows(pairs, begin, rows):
    left = pairs[pl.ds(2 * begin, rows, stride=2), :]
    right = pairs[pl.ds(2 * begin + 1, rows, stride=2), :]
    return left, right


def project_rows(states, weight, pairs, at, rows, block):
    @pl.loop(0, rows // block)
    def _(t):
        begin = pl.multiple_of(t * block, block)
        term = dot(states[pl.ds(begin, block), :], weight).astype(BF16).astype(F32)
        put_rows(pairs, at + begin, block, term)


def spread_rows(table, pairs, at, rows, block):
    @pl.loop(0, rows // block)
    def _(t):
        begin = pl.multiple_of(t * block, block)
        put_rows(pairs, at + begin, block, table[pl.ds(begin, block), :].astype(F32))


def pick_some(at, edges, group, out, pick):
    for begin in range(0, edges, group):
        found = [pick(begin + u) for u in range(group)]
        for u in range(0, group, 4):
            to = pl.multiple_of(2 * (at + begin + u), 8)
            out[pl.ds(to, 8), :] = jnp.concatenate(found[u : u + 4], axis=0)


def pick_pairs(edges, unroll, out, pick):
    @pl.loop(0, edges // unroll)
    def _(t):
        begin = t * unroll
        pick_some(begin, unroll, 16, out, lambda u: pick(begin + u))


def pair(table, twice):
    return table[pl.ds(pl.multiple_of(twice, 2), 2), :]


def one_hot(targets, begin, rows):
    shape = (rows, targets.shape[1])
    return jnp.where(
        lax.broadcasted_iota(jnp.int32, shape, 0) + begin == targets, 1.0, 0.0
    ).astype(BF16)


def activate(sums, hidden, begin, rows):
    left, right = get_rows(sums, begin, rows)
    hidden[pl.ds(begin, rows), :LANES] = silu(left).astype(BF16)
    hidden[pl.ds(begin, rows), LANES:] = silu(right).astype(BF16)


def pass_edges(pick, target_row, sums, hidden, total, edges, chunk):
    count = total.shape[0]
    chunks = edges // chunk

    def ready(c, slot):
        pick_some(0, chunk, 16, sums, lambda u: pick(c * chunk + u))
        activate(sums, hidden.at[slot], 0, chunk)

    def summed(c, slot):
        targets = target_row[:, pl.ds(pl.multiple_of(c * chunk, chunk), chunk)]
        return dot(one_hot(targets, 0, count), hidden[slot])

    ready(0, 0)
    total[...] = jnp.zeros_like(total)

    if chunks > 1:
        @pl.loop(1, chunks)
        def _(c):
            slot = lax.rem(c, 2)
            total[...] += summed(c - 1, 1 - slot)
            ready(c, slot)

    total[...] += summed(chunks - 1, (chunks - 1) % 2)


def update(states, total, weights, gain, begin, rows):
    h = states[pl.ds(begin, rows), :]
    aggregate = dot(total[pl.ds(begin, rows), :].astype(BF16), weights[2]).astype(BF16)
    inner = silu(dot(h, weights[3]) + dot(aggregate, weights[4])).astype(BF16)
    output = dot(inner, weights[5])
    centred = output - jnp.mean(output, axis=1, keepdims=True)
    spread = jnp.mean(centred * centred, axis=1, keepdims=True)
    return (h.astype(F32) + gain * centred * lax.rsqrt(spread + 1e-05)).astype(BF16)


def fine_kernel(
    senders, receivers, table, terms, nodes, weights, gains, target_row,
    fine_one, sums, hidden, total,
):
    pass_edges(
        lambda e: pair(table, senders[0, e]) + pair(terms, receivers[0, e]),
        target_row, sums, hidden, total, target_row.shape[1], 1024,
    )
    fine_one[...] = update(nodes, total, weights, gains[0:1, :], 0, nodes.shape[0])


def top_kernel(
    senders, receivers, twice_parents, fine_parents, fine_tops, place, coarse, top_zero, fine_one,
    weights_far, gains, target_row,
    fine_state, coarse_state, weights, fetched, coarse_pairs, table, terms, sums, hidden, total,
):
    count = top_zero.shape[0]
    own = coarse_state.shape[0]
    fetch = pltpu.make_async_copy(weights_far, weights, fetched)
    fetch.start()
    spread_rows(coarse, coarse_pairs, 0, coarse.shape[0], 1024)
    fetch.wait()
    project_rows(top_zero, weights[0], table, 0, count, 512)
    project_rows(top_zero, weights[1], terms, 0, count, 512)
    pass_edges(
        lambda e: pair(table, senders[0, e]) + pair(terms, receivers[0, e]),
        target_row, sums, hidden, total, target_row.shape[1], 1024,
    )
    put_rows(table, 0, count, update(top_zero, total, weights, gains[2:3, :], 0, count).astype(F32))

    def lift(parent, above):
        return pair(coarse_pairs, 2 * parent) + pair(table, above)

    first = place[0] * own
    pick_pairs(own, 32, sums, lambda e: lift(first + e, twice_parents[first + e]))
    left, right = get_rows(sums, 0, own)
    coarse_state[:, :LANES] = left.astype(BF16)
    coarse_state[:, LANES:] = right.astype(BF16)
    chunk = sums.shape[0] // 2

    @pl.loop(0, fine_one.shape[0] // chunk)
    def _(c):
        pick_pairs(
            chunk, 64, sums,
            lambda e: lift(fine_parents[c * chunk + e], fine_tops[c * chunk + e]),
        )

        @pl.loop(0, chunk // 256)
        def _(t):
            begin = pl.multiple_of(t * 256, 256)
            to = pl.multiple_of(c * chunk + begin, 256)
            left, right = get_rows(sums, begin, 256)
            for value, at in ((left, 0), (right, LANES)):
                own_part = fine_one[pl.ds(to, 256), at : at + LANES].astype(F32)
                fine_state[pl.ds(to, 256), at : at + LANES] = (
                    own_part + value.astype(BF16).astype(F32)
                ).astype(BF16)


MESH = pl.DeviceIdType.MESH


def step(place, by, span):
    return lax.rem(place + by + span, span)


def remote(source, target, sems, which, device):
    return pltpu.make_async_remote_copy(
        src_ref=source, dst_ref=target, send_sem=sems[0].at[which], recv_sem=sems[1].at[which],
        device_id=device, device_id_type=MESH,
    )


WAYS = (1, -1, 2)


def greet_first(devices):
    barrier = pltpu.get_barrier_semaphore()
    for device in devices:
        pl.semaphore_signal(barrier, inc=1, device_id=device, device_id_type=MESH)


def greet_last(devices):
    pl.semaphore_wait(pltpu.get_barrier_semaphore(), len(devices))


class Torus:
    def __init__(self, side):
        self.side = side
        me = lax.axis_index("gx")
        self.at = me // side, lax.rem(me, side)

    def near(self, axis, by):
        x, y = self.at
        if axis == 0:
            return {"gx": step(x, by, self.side) * self.side + y}
        return {"gx": x * self.side + step(y, by, self.side)}

    def ring(self):
        return [self.near(axis, by) for axis in (0, 1) for by in WAYS]

    def there(self, axis, by):
        return step(self.at[axis], by, self.side)


def exchange_kernel(
    lists_far, nodes_far, weights_far, coarse_weights_far, gains_far, owners_far, locals_far,
    parents_far, senders_far, receivers_far, coarse_row_far, top_row_far,
    top_senders_far,
    table, terms, nodes, weights, coarse_weights, gains, receivers, coarse_row,
    top_row, all_counts, all_parents, twice_parents, twice_senders, twice_receivers, fine_parents,
    twice_top_senders, twice_top_receivers,
    lists, owners, locals_, parents, senders, top_senders, rows3, picked, sent, halo, counts, fetched,
    send_halo, recv_halo, send_count, recv_count, send_parent, recv_parent,
):
    members, across = lax.axis_size("gx"), lax.axis_size("gy")
    me, beside = lax.axis_index("gx"), lax.axis_index("gy")
    ahead = {"gx": step(me, 1, members)}, {"gx": step(me, -1, members)}
    aside = {"gy": step(beside, 1, across)}, {"gy": step(beside, -1, across)}
    peers = [{"gx": step(me, by, members)} for by in range(1, members)]
    greet_first(peers + list(aside))
    wanted = (
        (weights_far.at[0], weights.at[0]), (nodes_far, nodes), (parents_far, parents),
        (owners_far, owners), (locals_far, locals_), (senders_far, senders),
        (receivers_far, receivers), (weights_far.at[pl.ds(1, 5)], weights.at[pl.ds(1, 5)]),
        (coarse_weights_far, coarse_weights),
        (gains_far, gains), (coarse_row_far, coarse_row), (top_row_far, top_row),
        (top_senders_far, top_senders), (lists_far, lists),
    )
    fetches = [
        pltpu.make_async_copy(source, target, fetched.at[k])
        for k, (source, target) in enumerate(wanted)
    ]
    for fetch in fetches:
        fetch.start()
    for k in (0, 1, 13):
        fetches[k].wait()
    rows = nodes.shape[0]
    term = dot(nodes[...], weights[0]).astype(BF16).astype(F32)
    rows3[:, 0, :] = term[:, :LANES]
    rows3[:, 1, :] = term[:, LANES:]
    length = lists.shape[1]
    halos, copies = [], []
    for slot, device in enumerate(ahead + aside):

        @pl.loop(0, length // 32)
        def _(t):
            begin = t * 32
            found = [rows3[lists[slot, begin + u]] for u in range(32)]
            for u in range(32):
                picked[slot, begin + u] = found[u]

        sent[slot, :, :LANES] = picked[slot, :, 0, :].astype(BF16)
        sent[slot, :, LANES:] = picked[slot, :, 1, :].astype(BF16)
        if slot == 0:
            greet_last(peers + list(aside))
        copy = remote(sent.at[slot], halo.at[slot], (send_halo, recv_halo), slot, device)
        copy.start()
        halos.append(copy)
    fetches[2].wait()
    for by, device in enumerate(peers):
        sems = send_parent, recv_parent
        copies.append(remote(parents.at[0], all_parents.at[me], sems, by, device))
        copies[-1].start()
    fetches[3].wait()
    fetches[4].wait()
    by_owner = one_hot(owners[...], 0, members)
    by_local = one_hot(locals_[...], 0, counts.shape[2])
    found = lax.dot_general(
        by_owner, by_local, (((1,), (1,)), ((), ())), preferred_element_type=F32
    )
    for member in range(members):
        counts[member] = found[member : member + 1]
    for by, device in enumerate(peers):
        goal = step(me, by + 1, members)
        sems = send_count, recv_count
        copies.append(remote(counts.at[goal], all_counts.at[me], sems, by, device))
        copies[-1].start()
    all_counts[me] = counts[me]
    all_parents[me] = parents[0]
    fine_parents[...] = owners[...] * counts.shape[2] + locals_[...]
    for fetch in fetches[5:13]:
        fetch.wait()
    put_rows(table, 0, rows, dot(nodes[...], weights[0]).astype(BF16).astype(F32))
    project_rows(nodes, weights[1], terms, 0, rows, rows)
    terms[pl.ds(2 * rows, 8), :] = jnp.zeros((8, LANES), F32)
    twice_senders[...] = 2 * senders[...]
    twice_receivers[...] = 2 * receivers[...]
    twice_top_senders[...] = 2 * top_senders[...]
    twice_top_receivers[...] = 2 * top_row[...]
    for slot, copy in enumerate(halos):
        copy.wait()
        put_rows(table, rows + slot * length, length, halo[slot].astype(F32))
    for copy in copies:
        copy.wait()
    twice_parents[...] = 2 * all_parents[...]


class Gathering:
    def __init__(self, torus, whole, sems):
        self.torus, self.whole, self.sems = torus, whole, sems
        self.half = whole.shape[2] // 2
        self.opened, self.outer, self.inner = [], {}, {}

    def block(self, first, one, two):
        x, y = (one, two) if first == 0 else (two, one)
        return self.whole.at[x, y, pl.ds(first * self.half, self.half)]

    def send(self, first, axis, held, which, way):
        copy = remote(
            held, held, self.sems, (first * 5 + which) * 3 + way,
            self.torus.near(axis, WAYS[way]),
        )
        copy.start()
        self.opened.append(copy)
        return copy

    def widen(self, pairs, first, one, two):
        if pairs is None:
            return
        x, y = (one, two) if first == 0 else (two, one)
        side, rows = self.torus.side, self.whole.shape[2]
        begin = (x * side + y) * rows + first * self.half
        value = self.whole[x, y, pl.ds(first * self.half, self.half)].astype(F32)
        if len(pairs.shape) == 2:
            put_rows(pairs, begin, self.half, value)
        else:
            pairs[pl.ds(begin, self.half), 0, :] = value[:, :LANES]
            pairs[pl.ds(begin, self.half), 1, :] = value[:, LANES:]

    def begin(self, first):
        torus = self.torus
        held = self.block(first, torus.at[first], torus.at[1 - first])
        for way in range(3):
            self.outer[first, way] = self.send(first, first, held, 0, way)
        self.pass_on(first, 0)

    def place(self, first, column):
        torus = self.torus
        return torus.at[first] if column == 0 else torus.there(first, -WAYS[column - 1])

    def pass_on(self, first, column):
        held = self.block(first, self.place(first, column), self.torus.at[1 - first])
        for way in range(3):
            self.inner[first, column, way] = self.send(first, 1 - first, held, 1 + column, way)

    def finish(self, pairs, after=lambda column: None):
        torus = self.torus
        for way in range(3):
            for first in (0, 1):
                self.outer[first, way].wait_recv()
                self.pass_on(first, 1 + way)
        for column in range(4):
            for first in (0, 1):
                self.widen(pairs, first, self.place(first, column), torus.at[1 - first])
            for way in range(3):
                for first in (0, 1):
                    self.inner[first, column, way].wait_recv()
                    self.widen(
                        pairs, first, self.place(first, column),
                        torus.there(1 - first, -WAYS[way]),
                    )
            after(column)
        for copy in self.opened:
            copy.wait_send()


def coarse_kernel(
    senders, receivers, twice_parents, fine_parents, fine_one, parent_row, all_counts, all_parents, weights, gains, target_row,
    whole_one, top_zero, fine_tops,
    coarse_zero, top_count, table3, terms3, sums, hidden, total, top_total,
    gathered, pooled, kept, arrived, partial, arrived2, send_sum, recv_sum, send_all, recv_all,
    send_one, recv_one,
):
    torus = Torus(gathered.shape[0])
    side, rows = torus.side, gathered.shape[2]
    half = rows // 2
    greet_first(torus.ring())
    parents = parent_row[...]
    opened, first_hop, second_hop = [], {}, {}

    def share(part, goal):
        begins = [
            (k * side + goal if part == 0 else goal * side + k) * rows + part * half
            for k in range(side)
        ]
        chosen = jnp.concatenate([one_hot(parents, begin, half) for begin in begins], axis=0)
        return dot(chosen, fine_one[...]).reshape(side, half, 2 * LANES)

    for way in (2, 0, 1):
        for part in (0, 1):
            axis = 1 - part
            pooled[part, way] = share(part, torus.there(axis, WAYS[way])).astype(BF16)
            if (way, part) == (2, 0):
                greet_last(torus.ring())
            copy = remote(
                pooled.at[part, way], arrived.at[part, way], (send_sum, recv_sum),
                part * 3 + way, torus.near(axis, WAYS[way]),
            )
            copy.start()
            opened.append(copy)
            first_hop[part, way] = copy
    for part in (0, 1):
        kept[part] = share(part, torus.at[1 - part])
    ones = jnp.ones((side * rows, LANES), BF16)
    top_count[...] = jnp.zeros_like(top_count)

    @pl.loop(0, side)
    def _(k):
        above = jnp.concatenate([all_parents[k * side + q] for q in range(side)], axis=1)
        top_count[...] += dot(one_hot(above, 0, top_count.shape[0]), ones)

    for part in (0, 1):
        for way in range(3):
            first_hop[part, way].wait_recv()
        partial[part] = (
            kept[part]
            + arrived[part, 0].astype(F32)
            + arrived[part, 1].astype(F32)
            + arrived[part, 2].astype(F32)
        ).astype(BF16)
        for way in range(3):
            copy = remote(
                partial.at[part, torus.there(part, WAYS[way])], arrived2.at[part, way],
                (send_sum, recv_sum), 6 + part * 3 + way, torus.near(part, WAYS[way]),
            )
            copy.start()
            opened.append(copy)
            second_hop[part, way] = copy

    @pl.loop(0, fine_tops.shape[0] // 32)
    def _(t):
        begin = t * 32
        found = [twice_parents[fine_parents[begin + u]] for u in range(32)]
        for u in range(32):
            fine_tops[begin + u] = found[u]

    total_count = jnp.sum(all_counts[...], axis=(0, 1)).reshape(1, rows)
    square = (rows, rows)
    diagonal = lax.broadcasted_iota(jnp.int32, square, 0) == lax.broadcasted_iota(
        jnp.int32, square, 1
    )
    children = jnp.maximum(
        jnp.sum(jnp.where(diagonal, total_count, 0.0), axis=1, keepdims=True), 1.0
    )
    x, y = torus.at
    gathering = Gathering(torus, gathered, (send_all, recv_all))
    for part in (0, 1):
        for way in range(3):
            second_hop[part, way].wait_recv()
        whole = (
            partial[part, torus.at[part]].astype(F32)
            + arrived2[part, 0].astype(F32)
            + arrived2[part, 1].astype(F32)
            + arrived2[part, 2].astype(F32)
        )
        mean = (whole / children[part * half : (part + 1) * half]).astype(BF16)
        coarse_zero[pl.ds(part * half, half), :] = mean
        gathered[x, y, pl.ds(part * half, half)] = dot(mean, weights[0]).astype(BF16)
        gathering.begin(part)
    term = dot(coarse_zero[...], weights[1]).astype(BF16).astype(F32)
    terms3[:, 0, :] = term[:, :LANES]
    terms3[:, 1, :] = term[:, LANES:]
    gathering.finish(table3)
    for copy in opened:
        copy.wait_send()

    edges = target_row.shape[1]
    pick_pairs(edges, 32, sums, lambda e: table3[senders[e]] + terms3[receivers[e]])
    activate(sums, hidden, 0, edges)
    total[...] = dot(one_hot(target_row[...], 0, rows), hidden[...])
    whole_one[x, y] = update(coarse_zero, total, weights, gains[1:2, :], 0, rows)

    sharing = Gathering(torus, whole_one, (send_one, recv_one))
    sharing.begin(0)
    sharing.begin(1)
    top_total[...] = jnp.zeros_like(top_total)

    def after(column):
        at_x, at_y = sharing.place(0, column), sharing.place(1, column)
        low, high = slice(0, half), slice(half, 2 * half)
        above = [all_parents[at_x * side + k, :, low] for k in range(side)]
        above += [all_parents[k * side + at_y, :, high] for k in range(side)]
        states = [whole_one[at_x, k, low] for k in range(side)]
        states += [whole_one[k, at_y, high] for k in range(side)]
        chosen = one_hot(jnp.concatenate(above, axis=1), 0, top_total.shape[0])
        top_total[...] += dot(chosen, jnp.concatenate(states, axis=0))

    sharing.finish(None, after)
    above = jnp.maximum(top_count[...], 1.0)
    top_zero[:, :LANES] = (top_total[:, :LANES] / above).astype(BF16)
    top_zero[:, LANES:] = (top_total[:, LANES:] / above).astype(BF16)


def call(kernel, outs, scalars, arrays, scratch, name, collective=None, far=(), out_spaces=None):
    hbm = pltpu.MemorySpace.HBM
    arrays = [
        pltpu.with_memory_space_constraint(array, hbm) if k in far else array
        for k, array in enumerate(arrays)
    ]
    in_specs = [pl.BlockSpec(memory_space=SMEM)] * len(scalars)
    in_specs += [pl.BlockSpec(memory_space=hbm if k in far else VMEM) for k in range(len(arrays))]
    return pl.pallas_call(
        kernel,
        out_shape=outs,
        in_specs=in_specs,
        out_specs=(
            jax.tree.map(lambda _: pl.BlockSpec(memory_space=VMEM), outs)
            if out_spaces is None
            else tuple(pl.BlockSpec(memory_space=place) for place in out_spaces)
        ),
        scratch_shapes=scratch,
        compiler_params=pltpu.CompilerParams(
            vmem_limit_bytes=40 << 20, collective_id=collective,
            has_side_effects=collective is not None,
        ),
        cost_estimate=pl.CostEstimate(flops=10**9, bytes_accessed=1 << 20, transcendentals=0),
        name=name,
    )(*scalars, *arrays)


def shape(rows, width=256, dtype=BF16):
    return jax.ShapeDtypeStruct((rows, width), dtype)


def body(
    fine_nodes, fine_weights, coarse_weights, top_weights, gains, send_list, fine_sender,
    fine_receiver, pool_owner, pool_local, coarse_sender, coarse_receiver, top_parent, top_sender,
    top_receiver,
):
    nodes = fine_nodes.shape[0]
    width = fine_nodes.shape[1]
    members = lax.axis_size("gx")
    coarse_rows = nodes // 8
    coarse_all = coarse_rows * members
    top_rows = coarse_all // 8
    lists = send_list.reshape(4, -1)
    halo = lists.shape[1]
    owner = pool_owner.reshape(1, -1)
    local = pool_local.reshape(1, -1)
    parents = top_parent.reshape(1, 1, -1)
    senders = fine_sender.reshape(1, -1)
    receivers = fine_receiver.reshape(1, -1)
    side = math.isqrt(members)
    dma = pltpu.SemaphoreType.DMA
    gather_sems = [dma((30,)), dma((30,))]
    ints = jnp.int32
    rows16 = jax.ShapeDtypeStruct((members, 1, coarse_rows), F32)
    ints16 = jax.ShapeDtypeStruct((members, 1, coarse_rows), ints)
    doubled = shape(1, senders.shape[1], ints)

    coarse_row = coarse_receiver.reshape(1, -1)
    top_row = top_receiver.reshape(1, -1)
    (
        table, terms, near_nodes, weights, near_coarse, near_gains, near_receivers,
        near_coarse_row, near_top_row, all_counts, all_parents, twice_parents, twice_senders,
        twice_receivers, parent, twice_top_senders, twice_top_receivers,
    ) = call(
        exchange_kernel,
        (
            shape(2 * (nodes + 4 * halo), LANES, F32), shape(2 * nodes + 8, LANES, F32),
            shape(nodes), *[jax.ShapeDtypeStruct(fine_weights.shape, BF16)] * 2,
            shape(3, width, F32), doubled, shape(1, coarse_row.shape[1], ints),
            shape(1, top_row.shape[1], ints), rows16, ints16, ints16,
            doubled, doubled, shape(1, nodes, ints),
            *[shape(1, top_row.shape[1], ints)] * 2,
        ),
        (),
        (
            lists, fine_nodes, fine_weights, coarse_weights, gains, owner, local, parents,
            senders, receivers, coarse_row, top_row, top_sender.reshape(1, -1),
        ),
        [
            SMEM(lists.shape, ints), VMEM((1, nodes), ints), VMEM((1, nodes), ints), VMEM((1, 1, coarse_rows), ints),
            VMEM(senders.shape, ints), VMEM(top_row.shape, ints), VMEM((nodes, 2, LANES), F32),
            VMEM((4, halo, 2, LANES), F32), VMEM((4, halo, width), BF16),
            VMEM((4, halo, width), BF16), VMEM((members, 1, coarse_rows), F32), dma((14,)),
        ]
        + [dma((4,))] * 2 + [dma((members - 1,))] * 4,
        "exchange", 0, far=range(13),
    )
    fine_one = call(
        fine_kernel, shape(nodes), (twice_senders, twice_receivers),
        (table, terms, near_nodes, weights, near_gains, near_receivers),
        [VMEM((2048, LANES), F32), VMEM((2, 1024, width), BF16), VMEM((nodes, width), F32)],
        "fine_layer",
    )
    half = coarse_rows // 2
    gathered = VMEM((side, side, coarse_rows, width), BF16)
    edges = coarse_sender.reshape(-1), coarse_receiver.reshape(-1)
    gathered_one, top_zero, fine_tops = call(
        coarse_kernel,
        (
            jax.ShapeDtypeStruct((side, side, coarse_rows, width), BF16), shape(top_rows),
            jax.ShapeDtypeStruct((nodes,), ints),
        ),
        (*edges, twice_parents.reshape(-1), parent.reshape(-1)),
        (fine_one, parent, all_counts, all_parents, near_coarse, near_gains, near_coarse_row),
        [
            VMEM((coarse_rows, width), BF16), VMEM((top_rows, LANES), F32),
            VMEM((coarse_all, 2, LANES), F32), VMEM((coarse_rows, 2, LANES), F32),
            VMEM((2048, LANES), F32), VMEM((1024, width), BF16), VMEM((coarse_rows, width), F32),
            VMEM((top_rows, width), F32), gathered,
            VMEM((2, 3, side, half, width), BF16), VMEM((2, side, half, width), F32),
            VMEM((2, 3, side, half, width), BF16), VMEM((2, side, half, width), BF16),
            VMEM((2, 3, half, width), BF16),
            dma((12,)), dma((12,)), *gather_sems, *gather_sems,
        ],
        "coarse_levels", 1, out_spaces=(VMEM, VMEM, SMEM),
    )
    place = lax.axis_index("gx").astype(ints).reshape(1)
    fine_state, coarse_state = call(
        top_kernel, (shape(nodes), shape(coarse_rows)),
        (
            twice_top_senders, twice_top_receivers, twice_parents.reshape(-1), parent.reshape(-1),
            fine_tops, place,
        ),
        (gathered_one.reshape(coarse_all, width), top_zero, fine_one, top_weights, near_gains, near_top_row),
        [
            VMEM(top_weights.shape, BF16), dma(()),
            VMEM((2 * coarse_all, LANES), F32), VMEM((2 * top_rows, LANES), F32),
            VMEM((2 * top_rows, LANES), F32), VMEM((2048, LANES), F32), VMEM((2, 1024, width), BF16), VMEM((top_rows, width), F32),
        ],
        "top_layer", far=(3,),
    )
    return (fine_state, coarse_state[None])


def solution(mesh):
    placed = (
        P(("gx", "gy"), None), P(), P(), P(), P(),
        P("gx", "gy", None, None), P("gx", "gy", None), P("gx", "gy", None),
        P(("gx", "gy"), None), P(("gx", "gy")),
        P("gy", "gx"), P("gy", "gx"), P("gy", "gx"), P("gy", None), P("gy", None),
    )
    return jax.shard_map(
        body,
        mesh=mesh,
        in_specs=placed,
        out_specs=(P(("gx", "gy"), None), P("gy", "gx", None)),
        check_vma=False,
    )
```

```python
import math

import jax
import jax.numpy as jnp
from jax import lax
from jax.experimental import pallas as pl
from jax.experimental.pallas import tpu as pltpu
from jax.sharding import PartitionSpec as P

F32 = jnp.float32
BF16 = jnp.bfloat16
LANES = 128
VMEM = pltpu.VMEM
SMEM = pltpu.SMEM


def silu(v):
    half = 0.5 * v
    return half + half * jnp.tanh(half)


def dot(a, b):
    return jnp.dot(a, b, preferred_element_type=F32)


def put_rows(pairs, begin, rows, value):
    pairs[pl.ds(2 * begin, rows, stride=2), :] = value[:, :LANES]
    pairs[pl.ds(2 * begin + 1, rows, stride=2), :] = value[:, LANES:]


def get_rows(pairs, begin, rows):
    left = pairs[pl.ds(2 * begin, rows, stride=2), :]
    right = pairs[pl.ds(2 * begin + 1, rows, stride=2), :]
    return left, right


def project_rows(states, weight, pairs, at, rows, block):
    @pl.loop(0, rows // block)
    def _(t):
        begin = pl.multiple_of(t * block, block)
        term = dot(states[pl.ds(begin, block), :], weight).astype(BF16).astype(F32)
        put_rows(pairs, at + begin, block, term)


def spread_rows(table, pairs, at, rows, block):
    @pl.loop(0, rows // block)
    def _(t):
        begin = pl.multiple_of(t * block, block)
        put_rows(pairs, at + begin, block, table[pl.ds(begin, block), :].astype(F32))


def pick_some(at, edges, group, out, pick):
    for begin in range(0, edges, group):
        found = [pick(begin + u) for u in range(group)]
        for u in range(0, group, 4):
            to = pl.multiple_of(2 * (at + begin + u), 8)
            out[pl.ds(to, 8), :] = jnp.concatenate(found[u : u + 4], axis=0)


def pick_pairs(edges, unroll, out, pick):
    @pl.loop(0, edges // unroll)
    def _(t):
        begin = t * unroll
        pick_some(begin, unroll, 16, out, lambda u: pick(begin + u))


def pair(table, twice):
    return table[pl.ds(pl.multiple_of(twice, 2), 2), :]


def one_hot(targets, begin, rows):
    shape = (rows, targets.shape[1])
    return jnp.where(
        lax.broadcasted_iota(jnp.int32, shape, 0) + begin == targets, 1.0, 0.0
    ).astype(BF16)


def activate(sums, hidden, begin, rows):
    left, right = get_rows(sums, begin, rows)
    hidden[pl.ds(begin, rows), :LANES] = silu(left).astype(BF16)
    hidden[pl.ds(begin, rows), LANES:] = silu(right).astype(BF16)


def pass_edges(pick, target_row, sums, hidden, total, edges, chunk):
    count = total.shape[0]
    chunks = edges // chunk

    def ready(c, slot):
        pick_some(0, chunk, 16, sums, lambda u: pick(c * chunk + u))
        activate(sums, hidden.at[slot], 0, chunk)

    def summed(c, slot):
        targets = target_row[:, pl.ds(pl.multiple_of(c * chunk, chunk), chunk)]
        return dot(one_hot(targets, 0, count), hidden[slot])

    ready(0, 0)
    total[...] = jnp.zeros_like(total)

    if chunks > 1:
        @pl.loop(1, chunks)
        def _(c):
            slot = lax.rem(c, 2)
            total[...] += summed(c - 1, 1 - slot)
            ready(c, slot)

    total[...] += summed(chunks - 1, (chunks - 1) % 2)


def update(states, total, weights, gain, begin, rows):
    h = states[pl.ds(begin, rows), :]
    aggregate = dot(total[pl.ds(begin, rows), :].astype(BF16), weights[2]).astype(BF16)
    inner = silu(dot(h, weights[3]) + dot(aggregate, weights[4])).astype(BF16)
    output = dot(inner, weights[5])
    centred = output - jnp.mean(output, axis=1, keepdims=True)
    spread = jnp.mean(centred * centred, axis=1, keepdims=True)
    return (h.astype(F32) + gain * centred * lax.rsqrt(spread + 1e-05)).astype(BF16)


def fine_kernel(
    senders, receivers, table, terms, nodes, weights, gains, target_row,
    fine_one, sums, hidden, total,
):
    pass_edges(
        lambda e: pair(table, senders[0, e]) + pair(terms, receivers[0, e]),
        target_row, sums, hidden, total, target_row.shape[1], 1024,
    )
    fine_one[...] = update(nodes, total, weights, gains[0:1, :], 0, nodes.shape[0])


def top_kernel(
    senders, receivers, twice_parents, fine_parents, fine_tops, place, coarse, top_zero, fine_one,
    weights_far, gains, target_row,
    fine_state, coarse_state, weights, fetched, coarse_pairs, table, terms, sums, hidden, total,
):
    count = top_zero.shape[0]
    own = coarse_state.shape[0]
    fetch = pltpu.make_async_copy(weights_far, weights, fetched)
    fetch.start()
    spread_rows(coarse, coarse_pairs, 0, coarse.shape[0], 1024)
    fetch.wait()
    project_rows(top_zero, weights[0], table, 0, count, 512)
    project_rows(top_zero, weights[1], terms, 0, count, 512)
    pass_edges(
        lambda e: pair(table, senders[0, e]) + pair(terms, receivers[0, e]),
        target_row, sums, hidden, total, target_row.shape[1], 1024,
    )
    put_rows(table, 0, count, update(top_zero, total, weights, gains[2:3, :], 0, count).astype(F32))

    def lift(parent, above):
        return pair(coarse_pairs, 2 * parent) + pair(table, above)

    first = place[0] * own
    pick_pairs(own, 32, sums, lambda e: lift(first + e, twice_parents[first + e]))
    left, right = get_rows(sums, 0, own)
    coarse_state[:, :LANES] = left.astype(BF16)
    coarse_state[:, LANES:] = right.astype(BF16)
    chunk = sums.shape[0] // 2

    @pl.loop(0, fine_one.shape[0] // chunk)
    def _(c):
        pick_pairs(
            chunk, 64, sums,
            lambda e: lift(fine_parents[c * chunk + e], fine_tops[c * chunk + e]),
        )

        @pl.loop(0, chunk // 256)
        def _(t):
            begin = pl.multiple_of(t * 256, 256)
            to = pl.multiple_of(c * chunk + begin, 256)
            left, right = get_rows(sums, begin, 256)
            for value, at in ((left, 0), (right, LANES)):
                own_part = fine_one[pl.ds(to, 256), at : at + LANES].astype(F32)
                fine_state[pl.ds(to, 256), at : at + LANES] = (
                    own_part + value.astype(BF16).astype(F32)
                ).astype(BF16)


MESH = pl.DeviceIdType.MESH


def step(place, by, span):
    return lax.rem(place + by + span, span)


def remote(source, target, sems, which, device):
    return pltpu.make_async_remote_copy(
        src_ref=source, dst_ref=target, send_sem=sems[0].at[which], recv_sem=sems[1].at[which],
        device_id=device, device_id_type=MESH,
    )


WAYS = (1, -1, 2)


def greet_first(devices):
    barrier = pltpu.get_barrier_semaphore()
    for device in devices:
        pl.semaphore_signal(barrier, inc=1, device_id=device, device_id_type=MESH)


def greet_last(devices):
    pl.semaphore_wait(pltpu.get_barrier_semaphore(), len(devices))


class Torus:
    def __init__(self, side):
        self.side = side
        me = lax.axis_index("gx")
        self.at = me // side, lax.rem(me, side)

    def near(self, axis, by):
        x, y = self.at
        if axis == 0:
            return {"gx": step(x, by, self.side) * self.side + y}
        return {"gx": x * self.side + step(y, by, self.side)}

    def ring(self):
        return [self.near(axis, by) for axis in (0, 1) for by in WAYS]

    def there(self, axis, by):
        return step(self.at[axis], by, self.side)


def exchange_kernel(
    lists_far, nodes_far, weights_far, coarse_weights_far, gains_far, owners_far, locals_far,
    parents_far, senders_far, receivers_far, coarse_row_far, top_row_far,
    top_senders_far,
    table, terms, nodes, weights, coarse_weights, gains, receivers, coarse_row,
    top_row, all_counts, all_parents, twice_parents, twice_senders, twice_receivers, fine_parents,
    twice_top_senders, twice_top_receivers,
    lists, owners, locals_, parents, senders, top_senders, rows3, picked, sent, halo, counts, fetched,
    send_halo, recv_halo, send_count, recv_count, send_parent, recv_parent,
):
    members, across = lax.axis_size("gx"), lax.axis_size("gy")
    me, beside = lax.axis_index("gx"), lax.axis_index("gy")
    ahead = {"gx": step(me, 1, members)}, {"gx": step(me, -1, members)}
    aside = {"gy": step(beside, 1, across)}, {"gy": step(beside, -1, across)}
    peers = [{"gx": step(me, by, members)} for by in range(1, members)]
    greet_first(peers + list(aside))
    wanted = (
        (weights_far.at[0], weights.at[0]), (nodes_far, nodes), (parents_far, parents),
        (owners_far, owners), (locals_far, locals_), (senders_far, senders),
        (receivers_far, receivers), (weights_far.at[pl.ds(1, 5)], weights.at[pl.ds(1, 5)]),
        (coarse_weights_far, coarse_weights),
        (gains_far, gains), (coarse_row_far, coarse_row), (top_row_far, top_row),
        (top_senders_far, top_senders), (lists_far, lists),
    )
    fetches = [
        pltpu.make_async_copy(source, target, fetched.at[k])
        for k, (source, target) in enumerate(wanted)
    ]
    for fetch in fetches:
        fetch.start()
    for k in (0, 1, 13):
        fetches[k].wait()
    rows = nodes.shape[0]
    term = dot(nodes[...], weights[0]).astype(BF16).astype(F32)
    rows3[:, 0, :] = term[:, :LANES]
    rows3[:, 1, :] = term[:, LANES:]
    length = lists.shape[1]
    halos, copies = [], []
    for slot, device in enumerate(ahead + aside):

        @pl.loop(0, length // 32)
        def _(t):
            begin = t * 32
            found = [rows3[lists[slot, begin + u]] for u in range(32)]
            for u in range(32):
                picked[slot, begin + u] = found[u]

        sent[slot, :, :LANES] = picked[slot, :, 0, :].astype(BF16)
        sent[slot, :, LANES:] = picked[slot, :, 1, :].astype(BF16)
        if slot == 0:
            greet_last(peers + list(aside))
        copy = remote(sent.at[slot], halo.at[slot], (send_halo, recv_halo), slot, device)
        copy.start()
        halos.append(copy)
    fetches[2].wait()
    for by, device in enumerate(peers):
        sems = send_parent, recv_parent
        copies.append(remote(parents.at[0], all_parents.at[me], sems, by, device))
        copies[-1].start()
    fetches[3].wait()
    fetches[4].wait()
    by_owner = one_hot(owners[...], 0, members)
    by_local = one_hot(locals_[...], 0, counts.shape[2])
    found = lax.dot_general(
        by_owner, by_local, (((1,), (1,)), ((), ())), preferred_element_type=F32
    )
    for member in range(members):
        counts[member] = found[member : member + 1]
    for by, device in enumerate(peers):
        goal = step(me, by + 1, members)
        sems = send_count, recv_count
        copies.append(remote(counts.at[goal], all_counts.at[me], sems, by, device))
        copies[-1].start()
    all_counts[me] = counts[me]
    all_parents[me] = parents[0]
    fine_parents[...] = owners[...] * counts.shape[2] + locals_[...]
    for fetch in fetches[5:13]:
        fetch.wait()
    put_rows(table, 0, rows, dot(nodes[...], weights[0]).astype(BF16).astype(F32))
    project_rows(nodes, weights[1], terms, 0, rows, rows)
    terms[pl.ds(2 * rows, 8), :] = jnp.zeros((8, LANES), F32)
    twice_senders[...] = 2 * senders[...]
    twice_receivers[...] = 2 * receivers[...]
    twice_top_senders[...] = 2 * top_senders[...]
    twice_top_receivers[...] = 2 * top_row[...]
    for slot, copy in enumerate(halos):
        copy.wait()
        put_rows(table, rows + slot * length, length, halo[slot].astype(F32))
    for copy in copies:
        copy.wait()
    twice_parents[...] = 2 * all_parents[...]


class Gathering:
    def __init__(self, torus, whole, sems):
        self.torus, self.whole, self.sems = torus, whole, sems
        self.half = whole.shape[2] // 2
        self.opened, self.outer, self.inner = [], {}, {}

    def block(self, first, one, two):
        x, y = (one, two) if first == 0 else (two, one)
        return self.whole.at[x, y, pl.ds(first * self.half, self.half)]

    def send(self, first, axis, held, which, way):
        copy = remote(
            held, held, self.sems, (first * 5 + which) * 3 + way,
            self.torus.near(axis, WAYS[way]),
        )
        copy.start()
        self.opened.append(copy)
        return copy

    def widen(self, pairs, first, one, two):
        if pairs is None:
            return
        x, y = (one, two) if first == 0 else (two, one)
        side, rows = self.torus.side, self.whole.shape[2]
        begin = (x * side + y) * rows + first * self.half
        value = self.whole[x, y, pl.ds(first * self.half, self.half)].astype(F32)
        if len(pairs.shape) == 2:
            put_rows(pairs, begin, self.half, value)
        else:
            pairs[pl.ds(begin, self.half), 0, :] = value[:, :LANES]
            pairs[pl.ds(begin, self.half), 1, :] = value[:, LANES:]

    def begin(self, first):
        torus = self.torus
        held = self.block(first, torus.at[first], torus.at[1 - first])
        for way in range(3):
            self.outer[first, way] = self.send(first, first, held, 0, way)
        self.pass_on(first, 0)

    def place(self, first, column):
        torus = self.torus
        return torus.at[first] if column == 0 else torus.there(first, -WAYS[column - 1])

    def pass_on(self, first, column):
        held = self.block(first, self.place(first, column), self.torus.at[1 - first])
        for way in range(3):
            self.inner[first, column, way] = self.send(first, 1 - first, held, 1 + column, way)

    def finish(self, pairs, after=lambda column: None):
        torus = self.torus
        for way in range(3):
            for first in (0, 1):
                self.outer[first, way].wait_recv()
                self.pass_on(first, 1 + way)
        for column in range(4):
            for first in (0, 1):
                self.widen(pairs, first, self.place(first, column), torus.at[1 - first])
            for way in range(3):
                for first in (0, 1):
                    self.inner[first, column, way].wait_recv()
                    self.widen(
                        pairs, first, self.place(first, column),
                        torus.there(1 - first, -WAYS[way]),
                    )
            after(column)
        for copy in self.opened:
            copy.wait_send()


def coarse_kernel(
    senders, receivers, twice_parents, fine_parents, fine_one, parent_row, all_counts, all_parents, weights, gains, target_row,
    whole_one, top_zero, fine_tops,
    coarse_zero, top_count, table3, terms3, sums, hidden, total, top_total,
    gathered, pooled, kept, arrived, partial, arrived2, send_sum, recv_sum, send_all, recv_all,
    send_one, recv_one,
):
    torus = Torus(gathered.shape[0])
    side, rows = torus.side, gathered.shape[2]
    half = rows // 2
    greet_first(torus.ring())
    parents = parent_row[...]
    opened, first_hop, second_hop = [], {}, {}

    def share(part, goal):
        begins = [
            (k * side + goal if part == 0 else goal * side + k) * rows + part * half
            for k in range(side)
        ]
        chosen = jnp.concatenate([one_hot(parents, begin, half) for begin in begins], axis=0)
        return dot(chosen, fine_one[...]).reshape(side, half, 2 * LANES)

    for way in (2, 0, 1):
        for part in (0, 1):
            axis = 1 - part
            pooled[part, way] = share(part, torus.there(axis, WAYS[way])).astype(BF16)
            if (way, part) == (2, 0):
                greet_last(torus.ring())
            copy = remote(
                pooled.at[part, way], arrived.at[part, way], (send_sum, recv_sum),
                part * 3 + way, torus.near(axis, WAYS[way]),
            )
            copy.start()
            opened.append(copy)
            first_hop[part, way] = copy
    for part in (0, 1):
        kept[part] = share(part, torus.at[1 - part])
    for part in (0, 1):
        for way in range(3):
            first_hop[part, way].wait_recv()
        partial[part] = (
            kept[part]
            + arrived[part, 0].astype(F32)
            + arrived[part, 1].astype(F32)
            + arrived[part, 2].astype(F32)
        ).astype(BF16)
        for way in range(3):
            copy = remote(
                partial.at[part, torus.there(part, WAYS[way])], arrived2.at[part, way],
                (send_sum, recv_sum), 6 + part * 3 + way, torus.near(part, WAYS[way]),
            )
            copy.start()
            opened.append(copy)
            second_hop[part, way] = copy
    total_count = jnp.sum(all_counts[...], axis=(0, 1)).reshape(1, rows)
    square = (rows, rows)
    diagonal = lax.broadcasted_iota(jnp.int32, square, 0) == lax.broadcasted_iota(
        jnp.int32, square, 1
    )
    children = jnp.maximum(
        jnp.sum(jnp.where(diagonal, total_count, 0.0), axis=1, keepdims=True), 1.0
    )
    x, y = torus.at
    gathering = Gathering(torus, gathered, (send_all, recv_all))
    for part in (0, 1):
        for way in range(3):
            second_hop[part, way].wait_recv()
        whole = (
            partial[part, torus.at[part]].astype(F32)
            + arrived2[part, 0].astype(F32)
            + arrived2[part, 1].astype(F32)
            + arrived2[part, 2].astype(F32)
        )
        mean = (whole / children[part * half : (part + 1) * half]).astype(BF16)
        coarse_zero[pl.ds(part * half, half), :] = mean
        gathered[x, y, pl.ds(part * half, half)] = dot(mean, weights[0]).astype(BF16)
        gathering.begin(part)
    term = dot(coarse_zero[...], weights[1]).astype(BF16).astype(F32)
    terms3[:, 0, :] = term[:, :LANES]
    terms3[:, 1, :] = term[:, LANES:]
    ones = jnp.ones((side * rows, LANES), BF16)
    top_count[...] = jnp.zeros_like(top_count)

    @pl.loop(0, side)
    def _(k):
        above = jnp.concatenate([all_parents[k * side + q] for q in range(side)], axis=1)
        top_count[...] += dot(one_hot(above, 0, top_count.shape[0]), ones)

    gathering.finish(table3)
    for copy in opened:
        copy.wait_send()

    edges = target_row.shape[1]
    pick_pairs(edges, 32, sums, lambda e: table3[senders[e]] + terms3[receivers[e]])
    activate(sums, hidden, 0, edges)
    total[...] = dot(one_hot(target_row[...], 0, rows), hidden[...])
    whole_one[x, y] = update(coarse_zero, total, weights, gains[1:2, :], 0, rows)

    sharing = Gathering(torus, whole_one, (send_one, recv_one))
    sharing.begin(0)
    sharing.begin(1)

    @pl.loop(0, fine_tops.shape[0] // 32)
    def _(t):
        begin = t * 32
        found = [twice_parents[fine_parents[begin + u]] for u in range(32)]
        for u in range(32):
            fine_tops[begin + u] = found[u]

    top_total[...] = jnp.zeros_like(top_total)

    def after(column):
        at_x, at_y = sharing.place(0, column), sharing.place(1, column)
        low, high = slice(0, half), slice(half, 2 * half)
        above = [all_parents[at_x * side + k, :, low] for k in range(side)]
        above += [all_parents[k * side + at_y, :, high] for k in range(side)]
        states = [whole_one[at_x, k, low] for k in range(side)]
        states += [whole_one[k, at_y, high] for k in range(side)]
        chosen = one_hot(jnp.concatenate(above, axis=1), 0, top_total.shape[0])
        top_total[...] += dot(chosen, jnp.concatenate(states, axis=0))

    sharing.finish(None, after)
    above = jnp.maximum(top_count[...], 1.0)
    top_zero[:, :LANES] = (top_total[:, :LANES] / above).astype(BF16)
    top_zero[:, LANES:] = (top_total[:, LANES:] / above).astype(BF16)


def call(kernel, outs, scalars, arrays, scratch, name, collective=None, far=(), out_spaces=None):
    hbm = pltpu.MemorySpace.HBM
    arrays = [
        pltpu.with_memory_space_constraint(array, hbm) if k in far else array
        for k, array in enumerate(arrays)
    ]
    in_specs = [pl.BlockSpec(memory_space=SMEM)] * len(scalars)
    in_specs += [pl.BlockSpec(memory_space=hbm if k in far else VMEM) for k in range(len(arrays))]
    return pl.pallas_call(
        kernel,
        out_shape=outs,
        in_specs=in_specs,
        out_specs=(
            jax.tree.map(lambda _: pl.BlockSpec(memory_space=VMEM), outs)
            if out_spaces is None
            else tuple(pl.BlockSpec(memory_space=place) for place in out_spaces)
        ),
        scratch_shapes=scratch,
        compiler_params=pltpu.CompilerParams(
            vmem_limit_bytes=40 << 20, collective_id=collective,
            has_side_effects=collective is not None,
        ),
        cost_estimate=pl.CostEstimate(flops=10**9, bytes_accessed=1 << 20, transcendentals=0),
        name=name,
    )(*scalars, *arrays)


def shape(rows, width=256, dtype=BF16):
    return jax.ShapeDtypeStruct((rows, width), dtype)


def body(
    fine_nodes, fine_weights, coarse_weights, top_weights, gains, send_list, fine_sender,
    fine_receiver, pool_owner, pool_local, coarse_sender, coarse_receiver, top_parent, top_sender,
    top_receiver,
):
    nodes = fine_nodes.shape[0]
    width = fine_nodes.shape[1]
    members = lax.axis_size("gx")
    coarse_rows = nodes // 8
    coarse_all = coarse_rows * members
    top_rows = coarse_all // 8
    lists = send_list.reshape(4, -1)
    halo = lists.shape[1]
    owner = pool_owner.reshape(1, -1)
    local = pool_local.reshape(1, -1)
    parents = top_parent.reshape(1, 1, -1)
    senders = fine_sender.reshape(1, -1)
    receivers = fine_receiver.reshape(1, -1)
    side = math.isqrt(members)
    dma = pltpu.SemaphoreType.DMA
    gather_sems = [dma((30,)), dma((30,))]
    ints = jnp.int32
    rows16 = jax.ShapeDtypeStruct((members, 1, coarse_rows), F32)
    ints16 = jax.ShapeDtypeStruct((members, 1, coarse_rows), ints)
    doubled = shape(1, senders.shape[1], ints)

    coarse_row = coarse_receiver.reshape(1, -1)
    top_row = top_receiver.reshape(1, -1)
    (
        table, terms, near_nodes, weights, near_coarse, near_gains, near_receivers,
        near_coarse_row, near_top_row, all_counts, all_parents, twice_parents, twice_senders,
        twice_receivers, parent, twice_top_senders, twice_top_receivers,
    ) = call(
        exchange_kernel,
        (
            shape(2 * (nodes + 4 * halo), LANES, F32), shape(2 * nodes + 8, LANES, F32),
            shape(nodes), *[jax.ShapeDtypeStruct(fine_weights.shape, BF16)] * 2,
            shape(3, width, F32), doubled, shape(1, coarse_row.shape[1], ints),
            shape(1, top_row.shape[1], ints), rows16, ints16, ints16,
            doubled, doubled, shape(1, nodes, ints),
            *[shape(1, top_row.shape[1], ints)] * 2,
        ),
        (),
        (
            lists, fine_nodes, fine_weights, coarse_weights, gains, owner, local, parents,
            senders, receivers, coarse_row, top_row, top_sender.reshape(1, -1),
        ),
        [
            SMEM(lists.shape, ints), VMEM((1, nodes), ints), VMEM((1, nodes), ints), VMEM((1, 1, coarse_rows), ints),
            VMEM(senders.shape, ints), VMEM(top_row.shape, ints), VMEM((nodes, 2, LANES), F32),
            VMEM((4, halo, 2, LANES), F32), VMEM((4, halo, width), BF16),
            VMEM((4, halo, width), BF16), VMEM((members, 1, coarse_rows), F32), dma((14,)),
        ]
        + [dma((4,))] * 2 + [dma((members - 1,))] * 4,
        "exchange", 0, far=range(13),
    )
    fine_one = call(
        fine_kernel, shape(nodes), (twice_senders, twice_receivers),
        (table, terms, near_nodes, weights, near_gains, near_receivers),
        [VMEM((2048, LANES), F32), VMEM((2, 1024, width), BF16), VMEM((nodes, width), F32)],
        "fine_layer",
    )
    half = coarse_rows // 2
    gathered = VMEM((side, side, coarse_rows, width), BF16)
    edges = coarse_sender.reshape(-1), coarse_receiver.reshape(-1)
    gathered_one, top_zero, fine_tops = call(
        coarse_kernel,
        (
            jax.ShapeDtypeStruct((side, side, coarse_rows, width), BF16), shape(top_rows),
            jax.ShapeDtypeStruct((nodes,), ints),
        ),
        (*edges, twice_parents.reshape(-1), parent.reshape(-1)),
        (fine_one, parent, all_counts, all_parents, near_coarse, near_gains, near_coarse_row),
        [
            VMEM((coarse_rows, width), BF16), VMEM((top_rows, LANES), F32),
            VMEM((coarse_all, 2, LANES), F32), VMEM((coarse_rows, 2, LANES), F32),
            VMEM((2048, LANES), F32), VMEM((1024, width), BF16), VMEM((coarse_rows, width), F32),
            VMEM((top_rows, width), F32), gathered,
            VMEM((2, 3, side, half, width), BF16), VMEM((2, side, half, width), F32),
            VMEM((2, 3, side, half, width), BF16), VMEM((2, side, half, width), BF16),
            VMEM((2, 3, half, width), BF16),
            dma((12,)), dma((12,)), *gather_sems, *gather_sems,
        ],
        "coarse_levels", 1, out_spaces=(VMEM, VMEM, SMEM),
    )
    place = lax.axis_index("gx").astype(ints).reshape(1)
    fine_state, coarse_state = call(
        top_kernel, (shape(nodes), shape(coarse_rows)),
        (
            twice_top_senders, twice_top_receivers, twice_parents.reshape(-1), parent.reshape(-1),
            fine_tops, place,
        ),
        (gathered_one.reshape(coarse_all, width), top_zero, fine_one, top_weights, near_gains, near_top_row),
        [
            VMEM(top_weights.shape, BF16), dma(()),
            VMEM((2 * coarse_all, LANES), F32), VMEM((2 * top_rows, LANES), F32),
            VMEM((2 * top_rows, LANES), F32), VMEM((2048, LANES), F32), VMEM((2, 1024, width), BF16), VMEM((top_rows, width), F32),
        ],
        "top_layer", far=(3,),
    )
    return (fine_state, coarse_state[None])


def solution(mesh):
    placed = (
        P(("gx", "gy"), None), P(), P(), P(), P(),
        P("gx", "gy", None, None), P("gx", "gy", None), P("gx", "gy", None),
        P(("gx", "gy"), None), P(("gx", "gy")),
        P("gy", "gx"), P("gy", "gx"), P("gy", "gx"), P("gy", None), P("gy", None),
    )
    return jax.shard_map(
        body,
        mesh=mesh,
        in_specs=placed,
        out_specs=(P(("gx", "gy"), None), P("gy", "gx", None)),
        check_vma=False,
    )
```

```python
import math

import jax
import jax.numpy as jnp
from jax import lax
from jax.experimental import pallas as pl
from jax.experimental.pallas import tpu as pltpu
from jax.sharding import PartitionSpec as P

F32 = jnp.float32
BF16 = jnp.bfloat16
LANES = 128
VMEM = pltpu.VMEM
SMEM = pltpu.SMEM


def silu(v):
    half = 0.5 * v
    return half + half * jnp.tanh(half)


def dot(a, b):
    return jnp.dot(a, b, preferred_element_type=F32)


def put_rows(pairs, begin, rows, value):
    pairs[pl.ds(2 * begin, rows, stride=2), :] = value[:, :LANES]
    pairs[pl.ds(2 * begin + 1, rows, stride=2), :] = value[:, LANES:]


def get_rows(pairs, begin, rows):
    left = pairs[pl.ds(2 * begin, rows, stride=2), :]
    right = pairs[pl.ds(2 * begin + 1, rows, stride=2), :]
    return left, right


def project_rows(states, weight, pairs, at, rows, block):
    @pl.loop(0, rows // block)
    def _(t):
        begin = pl.multiple_of(t * block, block)
        term = dot(states[pl.ds(begin, block), :], weight).astype(BF16).astype(F32)
        put_rows(pairs, at + begin, block, term)


def spread_rows(table, pairs, at, rows, block):
    @pl.loop(0, rows // block)
    def _(t):
        begin = pl.multiple_of(t * block, block)
        put_rows(pairs, at + begin, block, table[pl.ds(begin, block), :].astype(F32))


def pick_some(at, edges, group, out, pick):
    for begin in range(0, edges, group):
        found = [pick(begin + u) for u in range(group)]
        for u in range(0, group, 4):
            to = pl.multiple_of(2 * (at + begin + u), 8)
            out[pl.ds(to, 8), :] = jnp.concatenate(found[u : u + 4], axis=0)


def pick_pairs(edges, unroll, out, pick):
    @pl.loop(0, edges // unroll)
    def _(t):
        begin = t * unroll
        pick_some(begin, unroll, 16, out, lambda u: pick(begin + u))


def pair(table, twice):
    return table[pl.ds(pl.multiple_of(twice, 2), 2), :]


def one_hot(targets, begin, rows):
    shape = (rows, targets.shape[1])
    return jnp.where(
        lax.broadcasted_iota(jnp.int32, shape, 0) + begin == targets, 1.0, 0.0
    ).astype(BF16)


def activate(sums, hidden, begin, rows):
    left, right = get_rows(sums, begin, rows)
    hidden[pl.ds(begin, rows), :LANES] = silu(left).astype(BF16)
    hidden[pl.ds(begin, rows), LANES:] = silu(right).astype(BF16)


def pass_edges(pick, target_row, sums, hidden, total, edges, chunk):
    count = total.shape[0]
    chunks = edges // chunk

    def ready(c, slot):
        pick_some(0, chunk, 16, sums, lambda u: pick(c * chunk + u))
        activate(sums, hidden.at[slot], 0, chunk)

    def summed(c, slot):
        targets = target_row[:, pl.ds(pl.multiple_of(c * chunk, chunk), chunk)]
        return dot(one_hot(targets, 0, count), hidden[slot])

    ready(0, 0)
    total[...] = jnp.zeros_like(total)

    if chunks > 1:
        @pl.loop(1, chunks)
        def _(c):
            slot = lax.rem(c, 2)
            total[...] += summed(c - 1, 1 - slot)
            ready(c, slot)

    total[...] += summed(chunks - 1, (chunks - 1) % 2)


def update(states, total, weights, gain, begin, rows):
    h = states[pl.ds(begin, rows), :]
    aggregate = dot(total[pl.ds(begin, rows), :].astype(BF16), weights[2]).astype(BF16)
    inner = silu(dot(h, weights[3]) + dot(aggregate, weights[4])).astype(BF16)
    output = dot(inner, weights[5])
    centred = output - jnp.mean(output, axis=1, keepdims=True)
    spread = jnp.mean(centred * centred, axis=1, keepdims=True)
    return (h.astype(F32) + gain * centred * lax.rsqrt(spread + 1e-05)).astype(BF16)


def fine_kernel(
    senders, receivers, table, terms, nodes, weights, gains, target_row,
    fine_one, sums, hidden, total,
):
    pass_edges(
        lambda e: pair(table, senders[0, e]) + pair(terms, receivers[0, e]),
        target_row, sums, hidden, total, target_row.shape[1], 1024,
    )
    fine_one[...] = update(nodes, total, weights, gains[0:1, :], 0, nodes.shape[0])


def top_kernel(
    senders, receivers, twice_parents, fine_parents, fine_tops, place, coarse, top_zero, fine_one,
    weights_far, gains, target_row,
    fine_state, coarse_state, weights, fetched, coarse_pairs, table, terms, sums, hidden, total,
):
    count = top_zero.shape[0]
    own = coarse_state.shape[0]
    fetch = pltpu.make_async_copy(weights_far, weights, fetched)
    fetch.start()
    spread_rows(coarse, coarse_pairs, 0, coarse.shape[0], 1024)
    fetch.wait()
    project_rows(top_zero, weights[0], table, 0, count, 512)
    project_rows(top_zero, weights[1], terms, 0, count, 512)
    pass_edges(
        lambda e: pair(table, senders[0, e]) + pair(terms, receivers[0, e]),
        target_row, sums, hidden, total, target_row.shape[1], 1024,
    )
    put_rows(table, 0, count, update(top_zero, total, weights, gains[2:3, :], 0, count).astype(F32))

    def lift(parent, above):
        return pair(coarse_pairs, 2 * parent) + pair(table, above)

    first = place[0] * own
    pick_pairs(own, 32, sums, lambda e: lift(first + e, twice_parents[first + e]))
    left, right = get_rows(sums, 0, own)
    coarse_state[:, :LANES] = left.astype(BF16)
    coarse_state[:, LANES:] = right.astype(BF16)
    chunk = sums.shape[0] // 2

    @pl.loop(0, fine_one.shape[0] // chunk)
    def _(c):
        pick_pairs(
            chunk, 64, sums,
            lambda e: lift(fine_parents[c * chunk + e], fine_tops[c * chunk + e]),
        )

        @pl.loop(0, chunk // 256)
        def _(t):
            begin = pl.multiple_of(t * 256, 256)
            to = pl.multiple_of(c * chunk + begin, 256)
            left, right = get_rows(sums, begin, 256)
            for value, at in ((left, 0), (right, LANES)):
                own_part = fine_one[pl.ds(to, 256), at : at + LANES].astype(F32)
                fine_state[pl.ds(to, 256), at : at + LANES] = (
                    own_part + value.astype(BF16).astype(F32)
                ).astype(BF16)


MESH = pl.DeviceIdType.MESH


def step(place, by, span):
    return lax.rem(place + by + span, span)


def remote(source, target, sems, which, device):
    return pltpu.make_async_remote_copy(
        src_ref=source, dst_ref=target, send_sem=sems[0].at[which], recv_sem=sems[1].at[which],
        device_id=device, device_id_type=MESH,
    )


WAYS = (1, -1, 2)


def greet_first(devices):
    barrier = pltpu.get_barrier_semaphore()
    for device in devices:
        pl.semaphore_signal(barrier, inc=1, device_id=device, device_id_type=MESH)


def greet_last(devices):
    pl.semaphore_wait(pltpu.get_barrier_semaphore(), len(devices))


class Torus:
    def __init__(self, side):
        self.side = side
        me = lax.axis_index("gx")
        self.at = me // side, lax.rem(me, side)

    def near(self, axis, by):
        x, y = self.at
        if axis == 0:
            return {"gx": step(x, by, self.side) * self.side + y}
        return {"gx": x * self.side + step(y, by, self.side)}

    def ring(self):
        return [self.near(axis, by) for axis in (0, 1) for by in WAYS]

    def there(self, axis, by):
        return step(self.at[axis], by, self.side)


def exchange_kernel(
    lists_far, nodes_far, weights_far, coarse_weights_far, gains_far, owners_far, locals_far,
    parents_far, senders_far, receivers_far, coarse_row_far, top_row_far,
    top_senders_far,
    table, terms, nodes, weights, coarse_weights, gains, receivers, coarse_row,
    top_row, all_counts, all_parents, twice_parents, twice_senders, twice_receivers, fine_parents,
    twice_top_senders, twice_top_receivers,
    lists, owners, locals_, parents, senders, top_senders, rows3, picked, sent, halo, counts, fetched,
    send_halo, recv_halo, send_count, recv_count, send_parent, recv_parent,
):
    members, across = lax.axis_size("gx"), lax.axis_size("gy")
    me, beside = lax.axis_index("gx"), lax.axis_index("gy")
    ahead = {"gx": step(me, 1, members)}, {"gx": step(me, -1, members)}
    aside = {"gy": step(beside, 1, across)}, {"gy": step(beside, -1, across)}
    peers = [{"gx": step(me, by, members)} for by in range(1, members)]
    greet_first(peers + list(aside))
    wanted = (
        (weights_far.at[0], weights.at[0]), (nodes_far, nodes), (parents_far, parents),
        (owners_far, owners), (locals_far, locals_), (senders_far, senders),
        (receivers_far, receivers), (weights_far.at[pl.ds(1, 5)], weights.at[pl.ds(1, 5)]),
        (coarse_weights_far, coarse_weights),
        (gains_far, gains), (coarse_row_far, coarse_row), (top_row_far, top_row),
        (top_senders_far, top_senders), (lists_far, lists),
    )
    fetches = [
        pltpu.make_async_copy(source, target, fetched.at[k])
        for k, (source, target) in enumerate(wanted)
    ]
    for fetch in fetches:
        fetch.start()
    for k in (0, 1, 13):
        fetches[k].wait()
    rows = nodes.shape[0]
    term = dot(nodes[...], weights[0]).astype(BF16).astype(F32)
    rows3[:, 0, :] = term[:, :LANES]
    rows3[:, 1, :] = term[:, LANES:]
    length = lists.shape[1]
    halos, copies = [], []
    for slot, device in enumerate(ahead + aside):

        @pl.loop(0, length // 32)
        def _(t):
            begin = t * 32
            found = [rows3[lists[slot, begin + u]] for u in range(32)]
            for u in range(32):
                picked[slot, begin + u] = found[u]

        sent[slot, :, :LANES] = picked[slot, :, 0, :].astype(BF16)
        sent[slot, :, LANES:] = picked[slot, :, 1, :].astype(BF16)
        if slot == 0:
            greet_last(peers + list(aside))
        copy = remote(sent.at[slot], halo.at[slot], (send_halo, recv_halo), slot, device)
        copy.start()
        halos.append(copy)
    fetches[2].wait()
    for by, device in enumerate(peers):
        sems = send_parent, recv_parent
        copies.append(remote(parents.at[0], all_parents.at[me], sems, by, device))
        copies[-1].start()
    fetches[3].wait()
    fetches[4].wait()
    by_owner = one_hot(owners[...], 0, members)
    by_local = one_hot(locals_[...], 0, counts.shape[2])
    found = lax.dot_general(
        by_owner, by_local, (((1,), (1,)), ((), ())), preferred_element_type=F32
    )
    for member in range(members):
        counts[member] = found[member : member + 1]
    for by, device in enumerate(peers):
        goal = step(me, by + 1, members)
        sems = send_count, recv_count
        copies.append(remote(counts.at[goal], all_counts.at[me], sems, by, device))
        copies[-1].start()
    all_counts[me] = counts[me]
    all_parents[me] = parents[0]
    fine_parents[...] = owners[...] * counts.shape[2] + locals_[...]
    for fetch in fetches[5:13]:
        fetch.wait()
    put_rows(table, 0, rows, dot(nodes[...], weights[0]).astype(BF16).astype(F32))
    project_rows(nodes, weights[1], terms, 0, rows, rows)
    terms[pl.ds(2 * rows, 8), :] = jnp.zeros((8, LANES), F32)
    twice_senders[...] = 2 * senders[...]
    twice_receivers[...] = 2 * receivers[...]
    twice_top_senders[...] = 2 * top_senders[...]
    twice_top_receivers[...] = 2 * top_row[...]
    for slot, copy in enumerate(halos):
        copy.wait()
        put_rows(table, rows + slot * length, length, halo[slot].astype(F32))
    for copy in copies:
        copy.wait()
    twice_parents[...] = 2 * all_parents[...]


class Gathering:
    def __init__(self, torus, whole, sems):
        self.torus, self.whole, self.sems = torus, whole, sems
        self.half = whole.shape[2] // 2
        self.opened, self.outer, self.inner = [], {}, {}

    def block(self, first, one, two):
        x, y = (one, two) if first == 0 else (two, one)
        return self.whole.at[x, y, pl.ds(first * self.half, self.half)]

    def send(self, first, axis, held, which, way):
        copy = remote(
            held, held, self.sems, (first * 5 + which) * 3 + way,
            self.torus.near(axis, WAYS[way]),
        )
        copy.start()
        self.opened.append(copy)
        return copy

    def widen(self, pairs, first, one, two):
        if pairs is None:
            return
        x, y = (one, two) if first == 0 else (two, one)
        side, rows = self.torus.side, self.whole.shape[2]
        begin = (x * side + y) * rows + first * self.half
        value = self.whole[x, y, pl.ds(first * self.half, self.half)].astype(F32)
        if len(pairs.shape) == 2:
            put_rows(pairs, begin, self.half, value)
        else:
            pairs[pl.ds(begin, self.half), 0, :] = value[:, :LANES]
            pairs[pl.ds(begin, self.half), 1, :] = value[:, LANES:]

    def begin(self, first):
        torus = self.torus
        held = self.block(first, torus.at[first], torus.at[1 - first])
        for way in range(3):
            self.outer[first, way] = self.send(first, first, held, 0, way)
        self.pass_on(first, 0)

    def place(self, first, column):
        torus = self.torus
        return torus.at[first] if column == 0 else torus.there(first, -WAYS[column - 1])

    def pass_on(self, first, column):
        held = self.block(first, self.place(first, column), self.torus.at[1 - first])
        for way in range(3):
            self.inner[first, column, way] = self.send(first, 1 - first, held, 1 + column, way)

    def finish(self, pairs, after=lambda column: None, during=lambda: None):
        torus = self.torus
        for way in range(3):
            for first in (0, 1):
                self.outer[first, way].wait_recv()
                self.pass_on(first, 1 + way)
        during()
        for column in range(4):
            for first in (0, 1):
                self.widen(pairs, first, self.place(first, column), torus.at[1 - first])
            for way in range(3):
                for first in (0, 1):
                    self.inner[first, column, way].wait_recv()
                    self.widen(
                        pairs, first, self.place(first, column),
                        torus.there(1 - first, -WAYS[way]),
                    )
            after(column)
        for copy in self.opened:
            copy.wait_send()


def coarse_kernel(
    senders, receivers, twice_parents, fine_parents, fine_one, parent_row, all_counts, all_parents, weights, gains, target_row,
    whole_one, top_zero, fine_tops,
    coarse_zero, top_count, table3, terms3, sums, ahead, hidden, total, top_total,
    gathered, pooled, kept, arrived, partial, arrived2, send_sum, recv_sum, send_all, recv_all,
    send_one, recv_one,
):
    torus = Torus(gathered.shape[0])
    side, rows = torus.side, gathered.shape[2]
    half = rows // 2
    greet_first(torus.ring())
    parents = parent_row[...]
    opened, first_hop, second_hop = [], {}, {}

    def share(part, goal):
        begins = [
            (k * side + goal if part == 0 else goal * side + k) * rows + part * half
            for k in range(side)
        ]
        chosen = jnp.concatenate([one_hot(parents, begin, half) for begin in begins], axis=0)
        return dot(chosen, fine_one[...]).reshape(side, half, 2 * LANES)

    for way in (2, 0, 1):
        for part in (0, 1):
            axis = 1 - part
            pooled[part, way] = share(part, torus.there(axis, WAYS[way])).astype(BF16)
            if (way, part) == (2, 0):
                greet_last(torus.ring())
            copy = remote(
                pooled.at[part, way], arrived.at[part, way], (send_sum, recv_sum),
                part * 3 + way, torus.near(axis, WAYS[way]),
            )
            copy.start()
            opened.append(copy)
            first_hop[part, way] = copy
    for part in (0, 1):
        kept[part] = share(part, torus.at[1 - part])
    for way in (2, 0):
        for part in (0, 1):
            first_hop[part, way].wait_recv()
            kept[part] += arrived[part, way].astype(F32)
    for part in (0, 1):
        first_hop[part, 1].wait_recv()
        partial[part] = (kept[part] + arrived[part, 1].astype(F32)).astype(BF16)
        for way in range(3):
            copy = remote(
                partial.at[part, torus.there(part, WAYS[way])], arrived2.at[part, way],
                (send_sum, recv_sum), 6 + part * 3 + way, torus.near(part, WAYS[way]),
            )
            copy.start()
            opened.append(copy)
            second_hop[part, way] = copy
    total_count = jnp.sum(all_counts[...], axis=(0, 1)).reshape(1, rows)
    square = (rows, rows)
    diagonal = lax.broadcasted_iota(jnp.int32, square, 0) == lax.broadcasted_iota(
        jnp.int32, square, 1
    )
    children = jnp.maximum(
        jnp.sum(jnp.where(diagonal, total_count, 0.0), axis=1, keepdims=True), 1.0
    )
    x, y = torus.at
    gathering = Gathering(torus, gathered, (send_all, recv_all))
    for part in (0, 1):
        for way in range(3):
            second_hop[part, way].wait_recv()
        whole = (
            partial[part, torus.at[part]].astype(F32)
            + arrived2[part, 0].astype(F32)
            + arrived2[part, 1].astype(F32)
            + arrived2[part, 2].astype(F32)
        )
        mean = (whole / children[part * half : (part + 1) * half]).astype(BF16)
        coarse_zero[pl.ds(part * half, half), :] = mean
        gathered[x, y, pl.ds(part * half, half)] = dot(mean, weights[0]).astype(BF16)
        gathering.begin(part)
    term = dot(coarse_zero[...], weights[1]).astype(BF16).astype(F32)
    terms3[:, 0, :] = term[:, :LANES]
    terms3[:, 1, :] = term[:, LANES:]
    ones = jnp.ones((side * rows, LANES), BF16)
    top_count[...] = jnp.zeros_like(top_count)

    @pl.loop(0, side)
    def _(k):
        above = jnp.concatenate([all_parents[k * side + q] for q in range(side)], axis=1)
        top_count[...] += dot(one_hot(above, 0, top_count.shape[0]), ones)

    edges = target_row.shape[1]

    def during():
        pick_pairs(edges, 32, ahead, lambda e: terms3[receivers[e]])

    gathering.finish(table3, during=during)
    for copy in opened:
        copy.wait_send()
    pick_pairs(edges, 32, sums, lambda e: table3[senders[e]] + pair(ahead, 2 * e))
    activate(sums, hidden, 0, edges)
    total[...] = dot(one_hot(target_row[...], 0, rows), hidden[...])
    whole_one[x, y] = update(coarse_zero, total, weights, gains[1:2, :], 0, rows)

    sharing = Gathering(torus, whole_one, (send_one, recv_one))
    sharing.begin(0)
    sharing.begin(1)

    @pl.loop(0, fine_tops.shape[0] // 32)
    def _(t):
        begin = t * 32
        found = [twice_parents[fine_parents[begin + u]] for u in range(32)]
        for u in range(32):
            fine_tops[begin + u] = found[u]

    top_total[...] = jnp.zeros_like(top_total)

    def after(column):
        at_x, at_y = sharing.place(0, column), sharing.place(1, column)
        low, high = slice(0, half), slice(half, 2 * half)
        above = [all_parents[at_x * side + k, :, low] for k in range(side)]
        above += [all_parents[k * side + at_y, :, high] for k in range(side)]
        states = [whole_one[at_x, k, low] for k in range(side)]
        states += [whole_one[k, at_y, high] for k in range(side)]
        chosen = one_hot(jnp.concatenate(above, axis=1), 0, top_total.shape[0])
        top_total[...] += dot(chosen, jnp.concatenate(states, axis=0))

    sharing.finish(None, after)
    above = jnp.maximum(top_count[...], 1.0)
    top_zero[:, :LANES] = (top_total[:, :LANES] / above).astype(BF16)
    top_zero[:, LANES:] = (top_total[:, LANES:] / above).astype(BF16)


def call(kernel, outs, scalars, arrays, scratch, name, collective=None, far=(), out_spaces=None):
    hbm = pltpu.MemorySpace.HBM
    arrays = [
        pltpu.with_memory_space_constraint(array, hbm) if k in far else array
        for k, array in enumerate(arrays)
    ]
    in_specs = [pl.BlockSpec(memory_space=SMEM)] * len(scalars)
    in_specs += [pl.BlockSpec(memory_space=hbm if k in far else VMEM) for k in range(len(arrays))]
    return pl.pallas_call(
        kernel,
        out_shape=outs,
        in_specs=in_specs,
        out_specs=(
            jax.tree.map(lambda _: pl.BlockSpec(memory_space=VMEM), outs)
            if out_spaces is None
            else tuple(pl.BlockSpec(memory_space=place) for place in out_spaces)
        ),
        scratch_shapes=scratch,
        compiler_params=pltpu.CompilerParams(
            vmem_limit_bytes=40 << 20, collective_id=collective,
            has_side_effects=collective is not None,
        ),
        cost_estimate=pl.CostEstimate(flops=10**9, bytes_accessed=1 << 20, transcendentals=0),
        name=name,
    )(*scalars, *arrays)


def shape(rows, width=256, dtype=BF16):
    return jax.ShapeDtypeStruct((rows, width), dtype)


def body(
    fine_nodes, fine_weights, coarse_weights, top_weights, gains, send_list, fine_sender,
    fine_receiver, pool_owner, pool_local, coarse_sender, coarse_receiver, top_parent, top_sender,
    top_receiver,
):
    nodes = fine_nodes.shape[0]
    width = fine_nodes.shape[1]
    members = lax.axis_size("gx")
    coarse_rows = nodes // 8
    coarse_all = coarse_rows * members
    top_rows = coarse_all // 8
    lists = send_list.reshape(4, -1)
    halo = lists.shape[1]
    owner = pool_owner.reshape(1, -1)
    local = pool_local.reshape(1, -1)
    parents = top_parent.reshape(1, 1, -1)
    senders = fine_sender.reshape(1, -1)
    receivers = fine_receiver.reshape(1, -1)
    side = math.isqrt(members)
    dma = pltpu.SemaphoreType.DMA
    gather_sems = [dma((30,)), dma((30,))]
    ints = jnp.int32
    rows16 = jax.ShapeDtypeStruct((members, 1, coarse_rows), F32)
    ints16 = jax.ShapeDtypeStruct((members, 1, coarse_rows), ints)
    doubled = shape(1, senders.shape[1], ints)

    coarse_row = coarse_receiver.reshape(1, -1)
    top_row = top_receiver.reshape(1, -1)
    (
        table, terms, near_nodes, weights, near_coarse, near_gains, near_receivers,
        near_coarse_row, near_top_row, all_counts, all_parents, twice_parents, twice_senders,
        twice_receivers, parent, twice_top_senders, twice_top_receivers,
    ) = call(
        exchange_kernel,
        (
            shape(2 * (nodes + 4 * halo), LANES, F32), shape(2 * nodes + 8, LANES, F32),
            shape(nodes), *[jax.ShapeDtypeStruct(fine_weights.shape, BF16)] * 2,
            shape(3, width, F32), doubled, shape(1, coarse_row.shape[1], ints),
            shape(1, top_row.shape[1], ints), rows16, ints16, ints16,
            doubled, doubled, shape(1, nodes, ints),
            *[shape(1, top_row.shape[1], ints)] * 2,
        ),
        (),
        (
            lists, fine_nodes, fine_weights, coarse_weights, gains, owner, local, parents,
            senders, receivers, coarse_row, top_row, top_sender.reshape(1, -1),
        ),
        [
            SMEM(lists.shape, ints), VMEM((1, nodes), ints), VMEM((1, nodes), ints), VMEM((1, 1, coarse_rows), ints),
            VMEM(senders.shape, ints), VMEM(top_row.shape, ints), VMEM((nodes, 2, LANES), F32),
            VMEM((4, halo, 2, LANES), F32), VMEM((4, halo, width), BF16),
            VMEM((4, halo, width), BF16), VMEM((members, 1, coarse_rows), F32), dma((14,)),
        ]
        + [dma((4,))] * 2 + [dma((members - 1,))] * 4,
        "exchange", 0, far=range(13),
    )
    fine_one = call(
        fine_kernel, shape(nodes), (twice_senders, twice_receivers),
        (table, terms, near_nodes, weights, near_gains, near_receivers),
        [VMEM((2048, LANES), F32), VMEM((2, 1024, width), BF16), VMEM((nodes, width), F32)],
        "fine_layer",
    )
    half = coarse_rows // 2
    gathered = VMEM((side, side, coarse_rows, width), BF16)
    edges = coarse_sender.reshape(-1), coarse_receiver.reshape(-1)
    gathered_one, top_zero, fine_tops = call(
        coarse_kernel,
        (
            jax.ShapeDtypeStruct((side, side, coarse_rows, width), BF16), shape(top_rows),
            jax.ShapeDtypeStruct((nodes,), ints),
        ),
        (*edges, twice_parents.reshape(-1), parent.reshape(-1)),
        (fine_one, parent, all_counts, all_parents, near_coarse, near_gains, near_coarse_row),
        [
            VMEM((coarse_rows, width), BF16), VMEM((top_rows, LANES), F32),
            VMEM((coarse_all, 2, LANES), F32), VMEM((coarse_rows, 2, LANES), F32),
            VMEM((2048, LANES), F32), VMEM((2048, LANES), F32),
            VMEM((1024, width), BF16), VMEM((coarse_rows, width), F32),
            VMEM((top_rows, width), F32), gathered,
            VMEM((2, 3, side, half, width), BF16), VMEM((2, side, half, width), F32),
            VMEM((2, 3, side, half, width), BF16), VMEM((2, side, half, width), BF16),
            VMEM((2, 3, half, width), BF16),
            dma((12,)), dma((12,)), *gather_sems, *gather_sems,
        ],
        "coarse_levels", 1, out_spaces=(VMEM, VMEM, SMEM),
    )
    place = lax.axis_index("gx").astype(ints).reshape(1)
    fine_state, coarse_state = call(
        top_kernel, (shape(nodes), shape(coarse_rows)),
        (
            twice_top_senders, twice_top_receivers, twice_parents.reshape(-1), parent.reshape(-1),
            fine_tops, place,
        ),
        (gathered_one.reshape(coarse_all, width), top_zero, fine_one, top_weights, near_gains, near_top_row),
        [
            VMEM(top_weights.shape, BF16), dma(()),
            VMEM((2 * coarse_all, LANES), F32), VMEM((2 * top_rows, LANES), F32),
            VMEM((2 * top_rows, LANES), F32), VMEM((2048, LANES), F32), VMEM((2, 1024, width), BF16), VMEM((top_rows, width), F32),
        ],
        "top_layer", far=(3,),
    )
    return (fine_state, coarse_state[None])


def solution(mesh):
    placed = (
        P(("gx", "gy"), None), P(), P(), P(), P(),
        P("gx", "gy", None, None), P("gx", "gy", None), P("gx", "gy", None),
        P(("gx", "gy"), None), P(("gx", "gy")),
        P("gy", "gx"), P("gy", "gx"), P("gy", "gx"), P("gy", None), P("gy", None),
    )
    return jax.shard_map(
        body,
        mesh=mesh,
        in_specs=placed,
        out_specs=(P(("gx", "gy"), None), P("gy", "gx", None)),
        check_vma=False,
    )
```

```python
import math

import jax
import jax.numpy as jnp
from jax import lax
from jax.experimental import pallas as pl
from jax.experimental.pallas import tpu as pltpu
from jax.sharding import PartitionSpec as P

F32 = jnp.float32
BF16 = jnp.bfloat16
LANES = 128
VMEM = pltpu.VMEM
SMEM = pltpu.SMEM


def silu(v):
    half = 0.5 * v
    return half + half * jnp.tanh(half)


def dot(a, b):
    return jnp.dot(a, b, preferred_element_type=F32)


def put_rows(pairs, begin, rows, value):
    pairs[pl.ds(2 * begin, rows, stride=2), :] = value[:, :LANES]
    pairs[pl.ds(2 * begin + 1, rows, stride=2), :] = value[:, LANES:]


def get_rows(pairs, begin, rows):
    left = pairs[pl.ds(2 * begin, rows, stride=2), :]
    right = pairs[pl.ds(2 * begin + 1, rows, stride=2), :]
    return left, right


def project_rows(states, weight, pairs, at, rows, block):
    @pl.loop(0, rows // block)
    def _(t):
        begin = pl.multiple_of(t * block, block)
        term = dot(states[pl.ds(begin, block), :], weight).astype(BF16).astype(F32)
        put_rows(pairs, at + begin, block, term)


def spread_rows(table, pairs, at, rows, block):
    @pl.loop(0, rows // block)
    def _(t):
        begin = pl.multiple_of(t * block, block)
        put_rows(pairs, at + begin, block, table[pl.ds(begin, block), :].astype(F32))


def pick_some(at, edges, group, out, pick):
    for begin in range(0, edges, group):
        found = [pick(begin + u) for u in range(group)]
        for u in range(0, group, 4):
            to = pl.multiple_of(2 * (at + begin + u), 8)
            out[pl.ds(to, 8), :] = jnp.concatenate(found[u : u + 4], axis=0)


def pick_pairs(edges, unroll, out, pick):
    @pl.loop(0, edges // unroll)
    def _(t):
        begin = t * unroll
        pick_some(begin, unroll, 16, out, lambda u: pick(begin + u))


def pair(table, twice):
    return table[pl.ds(pl.multiple_of(twice, 2), 2), :]


def one_hot(targets, begin, rows):
    shape = (rows, targets.shape[1])
    return jnp.where(
        lax.broadcasted_iota(jnp.int32, shape, 0) + begin == targets, 1.0, 0.0
    ).astype(BF16)


def activate(sums, hidden, begin, rows):
    left, right = get_rows(sums, begin, rows)
    hidden[pl.ds(begin, rows), :LANES] = silu(left).astype(BF16)
    hidden[pl.ds(begin, rows), LANES:] = silu(right).astype(BF16)


def pass_edges(pick, target_row, sums, hidden, total, edges, chunk):
    count = total.shape[0]
    chunks = edges // chunk

    def ready(c, slot):
        pick_some(0, chunk, 16, sums, lambda u: pick(c * chunk + u))
        activate(sums, hidden.at[slot], 0, chunk)

    def summed(c, slot):
        targets = target_row[:, pl.ds(pl.multiple_of(c * chunk, chunk), chunk)]
        return dot(one_hot(targets, 0, count), hidden[slot])

    ready(0, 0)
    total[...] = jnp.zeros_like(total)

    if chunks > 1:
        @pl.loop(1, chunks)
        def _(c):
            slot = lax.rem(c, 2)
            total[...] += summed(c - 1, 1 - slot)
            ready(c, slot)

    total[...] += summed(chunks - 1, (chunks - 1) % 2)


def update(states, total, weights, gain, begin, rows):
    h = states[pl.ds(begin, rows), :]
    aggregate = dot(total[pl.ds(begin, rows), :].astype(BF16), weights[2]).astype(BF16)
    inner = silu(dot(h, weights[3]) + dot(aggregate, weights[4])).astype(BF16)
    output = dot(inner, weights[5])
    centred = output - jnp.mean(output, axis=1, keepdims=True)
    spread = jnp.mean(centred * centred, axis=1, keepdims=True)
    return (h.astype(F32) + gain * centred * lax.rsqrt(spread + 1e-05)).astype(BF16)


def fine_kernel(
    senders, receivers, table, terms, nodes, weights, gains, target_row,
    fine_one, sums, hidden, total,
):
    pass_edges(
        lambda e: pair(table, senders[0, e]) + pair(terms, receivers[0, e]),
        target_row, sums, hidden, total, target_row.shape[1], 1024,
    )
    fine_one[...] = update(nodes, total, weights, gains[0:1, :], 0, nodes.shape[0])


def top_kernel(
    senders, receivers, twice_parents, fine_parents, fine_tops, place, coarse, top_zero, fine_one,
    weights_far, gains, target_row,
    fine_state, coarse_state, weights, fetched, coarse_pairs, table, terms, sums, hidden, total,
):
    count = top_zero.shape[0]
    own = coarse_state.shape[0]
    fetch = pltpu.make_async_copy(weights_far, weights, fetched)
    fetch.start()
    spread_rows(coarse, coarse_pairs, 0, coarse.shape[0], 1024)
    fetch.wait()
    project_rows(top_zero, weights[0], table, 0, count, 512)
    project_rows(top_zero, weights[1], terms, 0, count, 512)
    pass_edges(
        lambda e: pair(table, senders[0, e]) + pair(terms, receivers[0, e]),
        target_row, sums, hidden, total, target_row.shape[1], 1024,
    )
    put_rows(table, 0, count, update(top_zero, total, weights, gains[2:3, :], 0, count).astype(F32))

    def lift(parent, above):
        return pair(coarse_pairs, 2 * parent) + pair(table, above)

    first = place[0] * own
    pick_pairs(own, 32, sums, lambda e: lift(first + e, twice_parents[first + e]))
    left, right = get_rows(sums, 0, own)
    coarse_state[:, :LANES] = left.astype(BF16)
    coarse_state[:, LANES:] = right.astype(BF16)
    chunk = sums.shape[0] // 2

    @pl.loop(0, fine_one.shape[0] // chunk)
    def _(c):
        pick_pairs(
            chunk, 64, sums,
            lambda e: lift(fine_parents[c * chunk + e], fine_tops[c * chunk + e]),
        )

        @pl.loop(0, chunk // 256)
        def _(t):
            begin = pl.multiple_of(t * 256, 256)
            to = pl.multiple_of(c * chunk + begin, 256)
            left, right = get_rows(sums, begin, 256)
            for value, at in ((left, 0), (right, LANES)):
                own_part = fine_one[pl.ds(to, 256), at : at + LANES].astype(F32)
                fine_state[pl.ds(to, 256), at : at + LANES] = (
                    own_part + value.astype(BF16).astype(F32)
                ).astype(BF16)


MESH = pl.DeviceIdType.MESH


def step(place, by, span):
    return lax.rem(place + by + span, span)


def remote(source, target, sems, which, device):
    return pltpu.make_async_remote_copy(
        src_ref=source, dst_ref=target, send_sem=sems[0].at[which], recv_sem=sems[1].at[which],
        device_id=device, device_id_type=MESH,
    )


WAYS = (2, 1, -1)


def greet_first(devices):
    barrier = pltpu.get_barrier_semaphore()
    for device in devices:
        pl.semaphore_signal(barrier, inc=1, device_id=device, device_id_type=MESH)


def greet_last(devices):
    pl.semaphore_wait(pltpu.get_barrier_semaphore(), len(devices))


class Torus:
    def __init__(self, side):
        self.side = side
        me = lax.axis_index("gx")
        self.at = me // side, lax.rem(me, side)

    def near(self, axis, by):
        x, y = self.at
        if axis == 0:
            return {"gx": step(x, by, self.side) * self.side + y}
        return {"gx": x * self.side + step(y, by, self.side)}

    def ring(self):
        return [self.near(axis, by) for axis in (0, 1) for by in WAYS]

    def there(self, axis, by):
        return step(self.at[axis], by, self.side)


def exchange_kernel(
    lists_far, nodes_far, weights_far, coarse_weights_far, gains_far, owners_far, locals_far,
    parents_far, senders_far, receivers_far, coarse_row_far, top_row_far,
    top_senders_far,
    table, terms, nodes, weights, coarse_weights, gains, receivers, coarse_row,
    top_row, all_counts, all_parents, twice_parents, twice_senders, twice_receivers, fine_parents,
    twice_top_senders, twice_top_receivers,
    lists, owners, locals_, parents, senders, top_senders, rows3, picked, sent, halo, counts, fetched,
    send_halo, recv_halo, send_count, recv_count, send_parent, recv_parent,
):
    members, across = lax.axis_size("gx"), lax.axis_size("gy")
    me, beside = lax.axis_index("gx"), lax.axis_index("gy")
    ahead = {"gx": step(me, 1, members)}, {"gx": step(me, -1, members)}
    aside = {"gy": step(beside, 1, across)}, {"gy": step(beside, -1, across)}
    peers = [{"gx": step(me, by, members)} for by in range(1, members)]
    greet_first(peers + list(aside))
    wanted = (
        (weights_far.at[0], weights.at[0]), (nodes_far, nodes), (parents_far, parents),
        (owners_far, owners), (locals_far, locals_), (senders_far, senders),
        (receivers_far, receivers), (weights_far.at[pl.ds(1, 5)], weights.at[pl.ds(1, 5)]),
        (coarse_weights_far, coarse_weights),
        (gains_far, gains), (coarse_row_far, coarse_row), (top_row_far, top_row),
        (top_senders_far, top_senders), (lists_far, lists),
    )
    fetches = [
        pltpu.make_async_copy(source, target, fetched.at[k])
        for k, (source, target) in enumerate(wanted)
    ]
    for fetch in fetches:
        fetch.start()
    for k in (0, 1, 13):
        fetches[k].wait()
    rows = nodes.shape[0]
    term = dot(nodes[...], weights[0]).astype(BF16).astype(F32)
    rows3[:, 0, :] = term[:, :LANES]
    rows3[:, 1, :] = term[:, LANES:]
    length = lists.shape[1]
    halos, copies = [], []
    for slot, device in enumerate(ahead + aside):

        @pl.loop(0, length // 32)
        def _(t):
            begin = t * 32
            found = [rows3[lists[slot, begin + u]] for u in range(32)]
            for u in range(32):
                picked[slot, begin + u] = found[u]

        sent[slot, :, :LANES] = picked[slot, :, 0, :].astype(BF16)
        sent[slot, :, LANES:] = picked[slot, :, 1, :].astype(BF16)
        if slot == 0:
            greet_last(peers + list(aside))
        copy = remote(sent.at[slot], halo.at[slot], (send_halo, recv_halo), slot, device)
        copy.start()
        halos.append(copy)
    fetches[2].wait()
    for by, device in enumerate(peers):
        sems = send_parent, recv_parent
        copies.append(remote(parents.at[0], all_parents.at[me], sems, by, device))
        copies[-1].start()
    fetches[3].wait()
    fetches[4].wait()
    by_owner = one_hot(owners[...], 0, members)
    by_local = one_hot(locals_[...], 0, counts.shape[2])
    found = lax.dot_general(
        by_owner, by_local, (((1,), (1,)), ((), ())), preferred_element_type=F32
    )
    for member in range(members):
        counts[member] = found[member : member + 1]
    for by, device in enumerate(peers):
        goal = step(me, by + 1, members)
        sems = send_count, recv_count
        copies.append(remote(counts.at[goal], all_counts.at[me], sems, by, device))
        copies[-1].start()
    all_counts[me] = counts[me]
    all_parents[me] = parents[0]
    fine_parents[...] = owners[...] * counts.shape[2] + locals_[...]
    for fetch in fetches[5:13]:
        fetch.wait()
    put_rows(table, 0, rows, dot(nodes[...], weights[0]).astype(BF16).astype(F32))
    project_rows(nodes, weights[1], terms, 0, rows, rows)
    terms[pl.ds(2 * rows, 8), :] = jnp.zeros((8, LANES), F32)
    twice_senders[...] = 2 * senders[...]
    twice_receivers[...] = 2 * receivers[...]
    twice_top_senders[...] = 2 * top_senders[...]
    twice_top_receivers[...] = 2 * top_row[...]
    for slot, copy in enumerate(halos):
        copy.wait()
        put_rows(table, rows + slot * length, length, halo[slot].astype(F32))
    for copy in copies:
        copy.wait()
    twice_parents[...] = 2 * all_parents[...]


class Gathering:
    def __init__(self, torus, whole, sems):
        self.torus, self.whole, self.sems = torus, whole, sems
        self.half = whole.shape[2] // 2
        self.opened, self.outer, self.inner = [], {}, {}

    def block(self, first, one, two):
        x, y = (one, two) if first == 0 else (two, one)
        return self.whole.at[x, y, pl.ds(first * self.half, self.half)]

    def send(self, first, axis, held, which, way):
        copy = remote(
            held, held, self.sems, (first * 5 + which) * 3 + way,
            self.torus.near(axis, WAYS[way]),
        )
        copy.start()
        self.opened.append(copy)
        return copy

    def widen(self, pairs, first, one, two):
        if pairs is None:
            return
        x, y = (one, two) if first == 0 else (two, one)
        side, rows = self.torus.side, self.whole.shape[2]
        begin = (x * side + y) * rows + first * self.half
        value = self.whole[x, y, pl.ds(first * self.half, self.half)].astype(F32)
        if len(pairs.shape) == 2:
            put_rows(pairs, begin, self.half, value)
        else:
            pairs[pl.ds(begin, self.half), 0, :] = value[:, :LANES]
            pairs[pl.ds(begin, self.half), 1, :] = value[:, LANES:]

    def begin(self, first):
        torus = self.torus
        held = self.block(first, torus.at[first], torus.at[1 - first])
        for way in range(3):
            self.outer[first, way] = self.send(first, first, held, 0, way)
        self.pass_on(first, 0)

    def place(self, first, column):
        torus = self.torus
        return torus.at[first] if column == 0 else torus.there(first, -WAYS[column - 1])

    def pass_on(self, first, column):
        held = self.block(first, self.place(first, column), self.torus.at[1 - first])
        for way in range(3):
            self.inner[first, column, way] = self.send(first, 1 - first, held, 1 + column, way)

    def finish(self, pairs, after=lambda column: None):
        torus = self.torus
        for way in (1, 2, 0):
            for first in (0, 1):
                self.outer[first, way].wait_recv()
                self.pass_on(first, 1 + way)
        for column in (0, 2, 3, 1):
            for first in (0, 1):
                self.widen(pairs, first, self.place(first, column), torus.at[1 - first])
            for way in (1, 2, 0):
                for first in (0, 1):
                    self.inner[first, column, way].wait_recv()
                    self.widen(
                        pairs, first, self.place(first, column),
                        torus.there(1 - first, -WAYS[way]),
                    )
            after(column)
        for copy in self.opened:
            copy.wait_send()


def coarse_kernel(
    senders, receivers, twice_parents, fine_parents, fine_one, parent_row, all_counts, all_parents, weights, gains, target_row,
    whole_one, top_zero, fine_tops,
    coarse_zero, top_count, table3, terms3, sums, hidden, total, top_total,
    gathered, pooled, kept, arrived, partial, arrived2, send_sum, recv_sum, send_all, recv_all,
    send_one, recv_one,
):
    torus = Torus(gathered.shape[0])
    side, rows = torus.side, gathered.shape[2]
    half = rows // 2
    greet_first(torus.ring())
    parents = parent_row[...]
    opened, first_hop, second_hop = [], {}, {}

    def share(part, goal):
        begins = [
            (k * side + goal if part == 0 else goal * side + k) * rows + part * half
            for k in range(side)
        ]
        chosen = jnp.concatenate([one_hot(parents, begin, half) for begin in begins], axis=0)
        return dot(chosen, fine_one[...]).reshape(side, half, 2 * LANES)

    for way in range(3):
        for part in (0, 1):
            axis = 1 - part
            pooled[part, way] = share(part, torus.there(axis, WAYS[way])).astype(BF16)
            if (way, part) == (0, 0):
                greet_last(torus.ring())
            copy = remote(
                pooled.at[part, way], arrived.at[part, way], (send_sum, recv_sum),
                part * 3 + way, torus.near(axis, WAYS[way]),
            )
            copy.start()
            opened.append(copy)
            first_hop[part, way] = copy
    for part in (0, 1):
        kept[part] = share(part, torus.at[1 - part])
    for part in (0, 1):
        for way in range(3):
            first_hop[part, way].wait_recv()
        partial[part] = (
            kept[part]
            + arrived[part, 0].astype(F32)
            + arrived[part, 1].astype(F32)
            + arrived[part, 2].astype(F32)
        ).astype(BF16)
        for way in range(3):
            copy = remote(
                partial.at[part, torus.there(part, WAYS[way])], arrived2.at[part, way],
                (send_sum, recv_sum), 6 + part * 3 + way, torus.near(part, WAYS[way]),
            )
            copy.start()
            opened.append(copy)
            second_hop[part, way] = copy
    total_count = jnp.sum(all_counts[...], axis=(0, 1)).reshape(1, rows)
    square = (rows, rows)
    diagonal = lax.broadcasted_iota(jnp.int32, square, 0) == lax.broadcasted_iota(
        jnp.int32, square, 1
    )
    children = jnp.maximum(
        jnp.sum(jnp.where(diagonal, total_count, 0.0), axis=1, keepdims=True), 1.0
    )
    x, y = torus.at
    gathering = Gathering(torus, gathered, (send_all, recv_all))
    for part in (0, 1):
        for way in range(3):
            second_hop[part, way].wait_recv()
        whole = (
            partial[part, torus.at[part]].astype(F32)
            + arrived2[part, 0].astype(F32)
            + arrived2[part, 1].astype(F32)
            + arrived2[part, 2].astype(F32)
        )
        mean = (whole / children[part * half : (part + 1) * half]).astype(BF16)
        coarse_zero[pl.ds(part * half, half), :] = mean
        gathered[x, y, pl.ds(part * half, half)] = dot(mean, weights[0]).astype(BF16)
        gathering.begin(part)
    term = dot(coarse_zero[...], weights[1]).astype(BF16).astype(F32)
    terms3[:, 0, :] = term[:, :LANES]
    terms3[:, 1, :] = term[:, LANES:]
    ones = jnp.ones((side * rows, LANES), BF16)
    top_count[...] = jnp.zeros_like(top_count)

    @pl.loop(0, side)
    def _(k):
        above = jnp.concatenate([all_parents[k * side + q] for q in range(side)], axis=1)
        top_count[...] += dot(one_hot(above, 0, top_count.shape[0]), ones)

    gathering.finish(table3)
    for copy in opened:
        copy.wait_send()

    edges = target_row.shape[1]
    pick_pairs(edges, 32, sums, lambda e: table3[senders[e]] + terms3[receivers[e]])
    activate(sums, hidden, 0, edges)
    total[...] = dot(one_hot(target_row[...], 0, rows), hidden[...])
    whole_one[x, y] = update(coarse_zero, total, weights, gains[1:2, :], 0, rows)

    sharing = Gathering(torus, whole_one, (send_one, recv_one))
    sharing.begin(0)
    sharing.begin(1)

    @pl.loop(0, fine_tops.shape[0] // 32)
    def _(t):
        begin = t * 32
        found = [twice_parents[fine_parents[begin + u]] for u in range(32)]
        for u in range(32):
            fine_tops[begin + u] = found[u]

    top_total[...] = jnp.zeros_like(top_total)

    def after(column):
        at_x, at_y = sharing.place(0, column), sharing.place(1, column)
        low, high = slice(0, half), slice(half, 2 * half)
        above = [all_parents[at_x * side + k, :, low] for k in range(side)]
        above += [all_parents[k * side + at_y, :, high] for k in range(side)]
        states = [whole_one[at_x, k, low] for k in range(side)]
        states += [whole_one[k, at_y, high] for k in range(side)]
        chosen = one_hot(jnp.concatenate(above, axis=1), 0, top_total.shape[0])
        top_total[...] += dot(chosen, jnp.concatenate(states, axis=0))

    sharing.finish(None, after)
    above = jnp.maximum(top_count[...], 1.0)
    top_zero[:, :LANES] = (top_total[:, :LANES] / above).astype(BF16)
    top_zero[:, LANES:] = (top_total[:, LANES:] / above).astype(BF16)


def call(kernel, outs, scalars, arrays, scratch, name, collective=None, far=(), out_spaces=None):
    hbm = pltpu.MemorySpace.HBM
    arrays = [
        pltpu.with_memory_space_constraint(array, hbm) if k in far else array
        for k, array in enumerate(arrays)
    ]
    in_specs = [pl.BlockSpec(memory_space=SMEM)] * len(scalars)
    in_specs += [pl.BlockSpec(memory_space=hbm if k in far else VMEM) for k in range(len(arrays))]
    return pl.pallas_call(
        kernel,
        out_shape=outs,
        in_specs=in_specs,
        out_specs=(
            jax.tree.map(lambda _: pl.BlockSpec(memory_space=VMEM), outs)
            if out_spaces is None
            else tuple(pl.BlockSpec(memory_space=place) for place in out_spaces)
        ),
        scratch_shapes=scratch,
        compiler_params=pltpu.CompilerParams(
            vmem_limit_bytes=40 << 20, collective_id=collective,
            has_side_effects=collective is not None,
        ),
        cost_estimate=pl.CostEstimate(flops=10**9, bytes_accessed=1 << 20, transcendentals=0),
        name=name,
    )(*scalars, *arrays)


def shape(rows, width=256, dtype=BF16):
    return jax.ShapeDtypeStruct((rows, width), dtype)


def body(
    fine_nodes, fine_weights, coarse_weights, top_weights, gains, send_list, fine_sender,
    fine_receiver, pool_owner, pool_local, coarse_sender, coarse_receiver, top_parent, top_sender,
    top_receiver,
):
    nodes = fine_nodes.shape[0]
    width = fine_nodes.shape[1]
    members = lax.axis_size("gx")
    coarse_rows = nodes // 8
    coarse_all = coarse_rows * members
    top_rows = coarse_all // 8
    lists = send_list.reshape(4, -1)
    halo = lists.shape[1]
    owner = pool_owner.reshape(1, -1)
    local = pool_local.reshape(1, -1)
    parents = top_parent.reshape(1, 1, -1)
    senders = fine_sender.reshape(1, -1)
    receivers = fine_receiver.reshape(1, -1)
    side = math.isqrt(members)
    dma = pltpu.SemaphoreType.DMA
    gather_sems = [dma((30,)), dma((30,))]
    ints = jnp.int32
    rows16 = jax.ShapeDtypeStruct((members, 1, coarse_rows), F32)
    ints16 = jax.ShapeDtypeStruct((members, 1, coarse_rows), ints)
    doubled = shape(1, senders.shape[1], ints)

    coarse_row = coarse_receiver.reshape(1, -1)
    top_row = top_receiver.reshape(1, -1)
    (
        table, terms, near_nodes, weights, near_coarse, near_gains, near_receivers,
        near_coarse_row, near_top_row, all_counts, all_parents, twice_parents, twice_senders,
        twice_receivers, parent, twice_top_senders, twice_top_receivers,
    ) = call(
        exchange_kernel,
        (
            shape(2 * (nodes + 4 * halo), LANES, F32), shape(2 * nodes + 8, LANES, F32),
            shape(nodes), *[jax.ShapeDtypeStruct(fine_weights.shape, BF16)] * 2,
            shape(3, width, F32), doubled, shape(1, coarse_row.shape[1], ints),
            shape(1, top_row.shape[1], ints), rows16, ints16, ints16,
            doubled, doubled, shape(1, nodes, ints),
            *[shape(1, top_row.shape[1], ints)] * 2,
        ),
        (),
        (
            lists, fine_nodes, fine_weights, coarse_weights, gains, owner, local, parents,
            senders, receivers, coarse_row, top_row, top_sender.reshape(1, -1),
        ),
        [
            SMEM(lists.shape, ints), VMEM((1, nodes), ints), VMEM((1, nodes), ints), VMEM((1, 1, coarse_rows), ints),
            VMEM(senders.shape, ints), VMEM(top_row.shape, ints), VMEM((nodes, 2, LANES), F32),
            VMEM((4, halo, 2, LANES), F32), VMEM((4, halo, width), BF16),
            VMEM((4, halo, width), BF16), VMEM((members, 1, coarse_rows), F32), dma((14,)),
        ]
        + [dma((4,))] * 2 + [dma((members - 1,))] * 4,
        "exchange", 0, far=range(13),
    )
    fine_one = call(
        fine_kernel, shape(nodes), (twice_senders, twice_receivers),
        (table, terms, near_nodes, weights, near_gains, near_receivers),
        [VMEM((2048, LANES), F32), VMEM((2, 1024, width), BF16), VMEM((nodes, width), F32)],
        "fine_layer",
    )
    half = coarse_rows // 2
    gathered = VMEM((side, side, coarse_rows, width), BF16)
    edges = coarse_sender.reshape(-1), coarse_receiver.reshape(-1)
    gathered_one, top_zero, fine_tops = call(
        coarse_kernel,
        (
            jax.ShapeDtypeStruct((side, side, coarse_rows, width), BF16), shape(top_rows),
            jax.ShapeDtypeStruct((nodes,), ints),
        ),
        (*edges, twice_parents.reshape(-1), parent.reshape(-1)),
        (fine_one, parent, all_counts, all_parents, near_coarse, near_gains, near_coarse_row),
        [
            VMEM((coarse_rows, width), BF16), VMEM((top_rows, LANES), F32),
            VMEM((coarse_all, 2, LANES), F32), VMEM((coarse_rows, 2, LANES), F32),
            VMEM((2048, LANES), F32), VMEM((1024, width), BF16), VMEM((coarse_rows, width), F32),
            VMEM((top_rows, width), F32), gathered,
            VMEM((2, 3, side, half, width), BF16), VMEM((2, side, half, width), F32),
            VMEM((2, 3, side, half, width), BF16), VMEM((2, side, half, width), BF16),
            VMEM((2, 3, half, width), BF16),
            dma((12,)), dma((12,)), *gather_sems, *gather_sems,
        ],
        "coarse_levels", 1, out_spaces=(VMEM, VMEM, SMEM),
    )
    place = lax.axis_index("gx").astype(ints).reshape(1)
    fine_state, coarse_state = call(
        top_kernel, (shape(nodes), shape(coarse_rows)),
        (
            twice_top_senders, twice_top_receivers, twice_parents.reshape(-1), parent.reshape(-1),
            fine_tops, place,
        ),
        (gathered_one.reshape(coarse_all, width), top_zero, fine_one, top_weights, near_gains, near_top_row),
        [
            VMEM(top_weights.shape, BF16), dma(()),
            VMEM((2 * coarse_all, LANES), F32), VMEM((2 * top_rows, LANES), F32),
            VMEM((2 * top_rows, LANES), F32), VMEM((2048, LANES), F32), VMEM((2, 1024, width), BF16), VMEM((top_rows, width), F32),
        ],
        "top_layer", far=(3,),
    )
    return (fine_state, coarse_state[None])


def solution(mesh):
    placed = (
        P(("gx", "gy"), None), P(), P(), P(), P(),
        P("gx", "gy", None, None), P("gx", "gy", None), P("gx", "gy", None),
        P(("gx", "gy"), None), P(("gx", "gy")),
        P("gy", "gx"), P("gy", "gx"), P("gy", "gx"), P("gy", None), P("gy", None),
    )
    return jax.shard_map(
        body,
        mesh=mesh,
        in_specs=placed,
        out_specs=(P(("gx", "gy"), None), P("gy", "gx", None)),
        check_vma=False,
    )
```
